32 devices in a mesh: dp: 4 (over z), row: 4 (over x, core), col: 2 (over y).
Axes of the slice: x: 2, y: 2, z: 4, core: 2. Of those that a mesh axis runs over, the one named last changes fastest.
Arguments:
- hidden_in: bfloat16 [768, 32768], P('row', ('dp', 'col')), may hold values from -6 to 6
- teacher: bfloat16 [768, 32768], P('row', ('dp', 'col')), may hold values from -6 to 6
- lengths: int32 [16], replicated, may hold values from 128 to 2048
- pos_embed: bfloat16 [16, 768], P(None, 'row'), may hold values from -3 to 3
- seg_qkv: bfloat16 [768, 2304], P('row', 'col'), may hold values from -0.21875 to 0.21875
- seg_proj: bfloat16 [768, 768], P('row', 'col'), may hold values from -0.625 to 0.625
- seg_gain1: bfloat16 [768], P('row'), may hold values from 0.5 to 1.5
- seg_bias1: bfloat16 [768], P('row'), may hold values from -1.5 to 1.5
- seg_up: bfloat16 [768, 3072], P('row', 'col'), may hold values from -0.21875 to 0.21875
- seg_down: bfloat16 [768, 3072], P('row', 'col'), may hold values from -0.21875 to 0.21875
- seg_gain2: bfloat16 [768], P('row'), may hold values from 0.5 to 1.5
- seg_bias2: bfloat16 [768], P('row'), may hold values from -1.5 to 1.5
- cross_qkv: bfloat16 [768, 2304], P('row', 'col'), may hold values from -0.21875 to 0.21875
- cross_proj: bfloat16 [768, 768], P('row', 'col'), may hold values from -0.4375 to 0.4375
- cross_gain1: bfloat16 [768], P('row'), may hold values from 0.5 to 1.5
- cross_bias1: bfloat16 [768], P('row'), may hold values from -1.5 to 1.5
- cross_up: bfloat16 [768, 3072], P('row', 'col'), may hold values from -0.21875 to 0.21875
- cross_down: bfloat16 [768, 3072], P('row', 'col'), may hold values from -0.21875 to 0.21875
- cross_gain2: bfloat16 [768], P('row'), may hold values from 0.5 to 1.5
- cross_bias2: bfloat16 [768], P('row'), may hold values from -1.5 to 1.5
Outputs:
- output: bfloat16 [768, 32768], P('row', ('dp', 'col'))
- mean_loss: float32 [], replicated
- input_grad: bfloat16 [768, 32768], P('row', ('dp', 'col'))
- pos_grad: float32 [16, 768], P(None, 'row')
- grad_seg_qkv: float32 [768, 2304], P('row', 'col')
- grad_seg_proj: float32 [768, 768], P('row', 'col')
- grad_seg_gain1: float32 [768], P('row')
- grad_seg_bias1: float32 [768], P('row')
- grad_seg_up: float32 [768, 3072], P('row', 'col')
- grad_seg_down: float32 [768, 3072], P('row', 'col')
- grad_seg_gain2: float32 [768], P('row')
- grad_seg_bias2: float32 [768], P('row')
- grad_cross_qkv: float32 [768, 2304], P('row', 'col')
- grad_cross_proj: float32 [768, 768], P('row', 'col')
- grad_cross_gain1: float32 [768], P('row')
- grad_cross_bias1: float32 [768], P('row')
- grad_cross_up: float32 [768, 3072], P('row', 'col')
- grad_cross_down: float32 [768, 3072], P('row', 'col')
- grad_cross_gain2: float32 [768], P('row')
- grad_cross_bias2: float32 [768], P('row')
The draws below stay inside these ranges and needn't reach their ends.
All inputs are finite; a program needn't handle non-finite values.
Results may differ from the reference program's by a relative error of at most 0.017.
Values may be sent and summed in bfloat16 or wider, within the bound.
No kernel may reach another device: no remote copies, remote signals or barrier semaphores. Data moves between devices by JAX's collectives and lax.ppermute only.
A program may use at most 256 MiB of HBM per device.

```python
import jax
import jax.numpy as jnp
from jax import lax

D = 768
HEAD_DIM = 64
FF = 3072
SEG = 128
SEGS = 16
SEQ_LEN = 2048
SEQS = 16
TOKENS = 32768


def set_ends(array, stream_key, least, high):
    dims = array.shape
    index_at = [jax.random.randint(jax.random.fold_in(stream_key, axis), (), 0, dims[axis]) for axis in range(len(dims))]
    array = array.at[tuple(index_at)].set(least)
    longest = dims.index(max(dims))
    index_at[longest] = (index_at[longest] + 1) % dims[longest]
    return array.at[tuple(index_at)].set(high)


def level_of(key, shape, split, least, largest):
    level = 1.0
    for position, shards_of in split:
        draws = jax.random.uniform(jax.random.fold_in(jax.random.fold_in(key, 6), position), (shards_of,), jnp.float32, least / len(split), largest / len(split))
        level = level * jnp.repeat(jnp.exp(draws), shape[position] // shards_of).reshape((-1,) + (1,) * (len(shape) - 1 - position))
    return level


def normal_values(stream_key, extent, deviation, most, shards=(), dtype=jnp.bfloat16):
    factor_of = level_of(stream_key, extent, shards, -0.22, 0.18) if shards else 1.0
    values = jax.random.normal(stream_key, extent, jnp.float32) * deviation * factor_of
    return jnp.minimum(jnp.maximum(values, -most), most).astype(dtype)


def setup_inputs(seed: int = 0) -> dict:
    streams_of = jax.random.split(jax.random.key(seed), 21)
    return {
        "hidden_in": normal_values(streams_of[0], (D, TOKENS), 1.0, 6.0, ((0, 4), (1, 8))),
        "teacher": normal_values(streams_of[1], (D, TOKENS), 1.0, 6.0, ((0, 4), (1, 8))),
        "lengths": set_ends(jax.random.randint(streams_of[2], (SEQS,), SEG, SEQ_LEN + 1), jax.random.fold_in(streams_of[2], 1), SEG, SEQ_LEN).astype(jnp.int32),
        "pos_embed": normal_values(streams_of[3], (SEGS, D), 0.5, 3.0, ((1, 4),)),
        "seg_qkv": normal_values(streams_of[4], (D, 3 * D), D ** -0.5, 0.21875, ((0, 4), (1, 2))),
        "seg_proj": normal_values(streams_of[5], (D, D), (D // 8) ** -0.5, 0.625, ((0, 4), (1, 2))),
        "seg_gain1": jnp.clip(1.0 + 0.1 * jax.random.normal(streams_of[6], (D,), jnp.float32), 0.5, 1.5).astype(jnp.bfloat16),
        "seg_bias1": normal_values(streams_of[7], (D,), 0.3, 1.5, ((0, 4),)),
        "seg_up": normal_values(streams_of[8], (D, FF), D ** -0.5, 0.21875, ((0, 4), (1, 2))),
        "seg_down": normal_values(streams_of[9], (D, FF), (FF // 4) ** -0.5, 0.21875, ((0, 4), (1, 2))),
        "seg_gain2": jnp.clip(1.0 + 0.1 * jax.random.normal(streams_of[10], (D,), jnp.float32), 0.5, 1.5).astype(jnp.bfloat16),
        "seg_bias2": normal_values(streams_of[11], (D,), 0.3, 1.5, ((0, 4),)),
        "cross_qkv": normal_values(streams_of[12], (D, 3 * D), D ** -0.5, 0.21875, ((0, 4), (1, 2))),
        "cross_proj": normal_values(streams_of[13], (D, D), (D // 4) ** -0.5, 0.4375, ((0, 4), (1, 2))),
        "cross_gain1": jnp.clip(1.0 + 0.1 * jax.random.normal(streams_of[14], (D,), jnp.float32), 0.5, 1.5).astype(jnp.bfloat16),
        "cross_bias1": normal_values(streams_of[15], (D,), 0.3, 1.5, ((0, 4),)),
        "cross_up": normal_values(streams_of[16], (D, FF), D ** -0.5, 0.21875, ((0, 4), (1, 2))),
        "cross_down": normal_values(streams_of[17], (D, FF), (FF // 4) ** -0.5, 0.21875, ((0, 4), (1, 2))),
        "cross_gain2": jnp.clip(1.0 + 0.1 * jax.random.normal(streams_of[18], (D,), jnp.float32), 0.5, 1.5).astype(jnp.bfloat16),
        "cross_bias2": normal_values(streams_of[19], (D,), 0.3, 1.5, ((0, 4),)),
    }


@jax.custom_vjp
def low(v):
    return lax.optimization_barrier(v.astype(jnp.bfloat16)).astype(jnp.float32)

@jax.custom_vjp
def low_back(v):
    return v

def low_keep(v):
    return (low(v), None)

def low_pass(kept, grad):
    return (grad,)

def back_keep(v):
    return (v, None)

def back_low(kept, grad):
    return (low(grad),)
low.defvjp(low_keep, low_pass)
low_back.defvjp(back_keep, back_low)
EPS = 1e-05
NEG = -1e+30
HIGH = lax.Precision.HIGHEST
ROOT_HALF = 0.7071067811865476

def matmul(left_side, right_side):
    return jnp.dot(left_side, right_side, precision=HIGH)

def matmul_trans(left_side, right_side):
    return lax.dot_general(left_side, right_side, (((1,), (1,)), ((), ())), precision=HIGH)

def gelu_value(hidden):
    return 0.5 * hidden * (1.0 + lax.erf(hidden * ROOT_HALF))

def layer_norm(residual, gain_vec, offset):
    center = lax.optimization_barrier(jnp.mean(residual, axis=-1, keepdims=True))
    spread = lax.optimization_barrier(jnp.mean(residual * residual, axis=-1, keepdims=True)) - center * center
    return (residual - center) * lax.rsqrt(spread + EPS) * gain_vec + offset

def attention(projected, key_ok, span_len):
    blocks = projected.shape[0] // span_len
    head_count = projected.shape[1] // (3 * HEAD_DIM)
    pieces = projected.reshape(blocks, span_len, head_count, 3, HEAD_DIM)
    scores = jnp.einsum('bqhe,bkhe->bhqk', pieces[:, :, :, 0], pieces[:, :, :, 1], precision=HIGH)
    scores = low_back(scores * HEAD_DIM ** (-0.5))
    scores = jnp.where(key_ok[:, None, None, :], scores, NEG)
    peak_score = lax.optimization_barrier(jnp.max(scores, axis=-1, keepdims=True))
    powers = jnp.exp(scores - peak_score)
    probability = low(powers / lax.optimization_barrier(jnp.sum(powers, axis=-1, keepdims=True)))
    mixture = jnp.einsum('bhqk,bkhe->bqhe', probability, pieces[:, :, :, 2], precision=HIGH)
    return mixture.reshape(projected.shape[0], head_count * HEAD_DIM)

def block(block_in, weights, key_ok, span_len):
    qkv_weight, proj_weight, gain_one, bias_one, up_weight, down_weight, gain_two, bias_two = weights
    projected = low_back(low(matmul(low(block_in), qkv_weight)))
    mixture = low_back(low(attention(projected, key_ok, span_len)))
    branch = low_back(matmul_trans(mixture, proj_weight))
    first_out = layer_norm(block_in + branch, gain_one, bias_one)
    hidden = low_back(matmul(low(first_out), up_weight))
    second = low_back(matmul_trans(low(gelu_value(hidden)), down_weight))
    return layer_norm(first_out + second, gain_two, bias_two)

def sequence_pair(seg_weights, cross_weights, pos_table, pair_in, pair_teacher, pair_lengths):
    positions = jnp.arange(SEQ_LEN)
    count_here = pair_in.shape[0]
    key_ok = (positions[None, :] < pair_lengths[:, None]) | (positions % SEG == 0)[None, :]
    seg_out = low_back(block(pair_in.reshape(-1, D), seg_weights, key_ok.reshape(-1, SEG), SEG))
    seg_view = seg_out.reshape(count_here, SEGS, SEG, D)
    cls_in = seg_view[:, :, 0, :] + pos_table[None]
    seg_valid = (jnp.arange(SEGS) * SEG)[None, :] < pair_lengths[:, None]
    cls_out = block(cls_in.reshape(-1, D), cross_weights, seg_valid, SEGS)
    full_out = seg_view.at[:, :, 0, :].set(cls_out.reshape(count_here, SEGS, D)).reshape(count_here, SEQ_LEN, D)
    live_rows = positions[None, :] < pair_lengths[:, None]
    differ = jnp.where(live_rows[:, :, None], full_out - pair_teacher, 0.0)
    return (full_out, jnp.sum(differ * differ))

def reference(hidden_in, teacher, lengths, pos_embed, seg_qkv, seg_proj, seg_gain1, seg_bias1, seg_up, seg_down, seg_gain2, seg_bias2, cross_qkv, cross_proj, cross_gain1, cross_bias1, cross_up, cross_down, cross_gain2, cross_bias2):
    seg_weights = tuple((weight.astype(jnp.float32) for weight in (seg_qkv, seg_proj, seg_gain1, seg_bias1, seg_up, seg_down, seg_gain2, seg_bias2)))
    cross_weights = tuple((weight.astype(jnp.float32) for weight in (cross_qkv, cross_proj, cross_gain1, cross_bias1, cross_up, cross_down, cross_gain2, cross_bias2)))
    valid_count = jnp.sum(lengths).astype(jnp.float32)
    pair_count = lengths.shape[0] // 2
    inputs_all = hidden_in.astype(jnp.float32).T.reshape(pair_count, 2, SEQ_LEN, D)
    teacher_all = teacher.astype(jnp.float32).T.reshape(pair_count, 2, SEQ_LEN, D)
    length_pairs = lengths.reshape(pair_count, 2)

    def objective(inputs_now, pos_table, seg_now, cross_now):
        step_fn = jax.checkpoint(sequence_pair)

        def scan_step(running, scan_item):
            pair_in, pair_teacher, pair_lengths = scan_item
            full_out, square_sum = step_fn(seg_now, cross_now, pos_table, pair_in, pair_teacher, pair_lengths)
            return (running + square_sum, full_out)
        running, outputs = lax.scan(scan_step, jnp.zeros((), jnp.float32), (inputs_now, teacher_all, length_pairs))
        loss_value = running / (2.0 * valid_count)
        return (TOKENS * loss_value, (outputs, loss_value))
    scaled, pull_back, aux_out = jax.vjp(objective, inputs_all, pos_embed.astype(jnp.float32), seg_weights, cross_weights, has_aux=True)
    grad_in, grad_pos, seg_grads, cross_grads = pull_back(jnp.ones((), jnp.float32))
    outputs, loss_value = aux_out
    return (outputs.reshape(-1, D).T.astype(jnp.bfloat16), loss_value, grad_in.reshape(-1, D).T.astype(jnp.bfloat16), grad_pos, seg_grads[0], seg_grads[1], seg_grads[2], seg_grads[3], seg_grads[4], seg_grads[5], seg_grads[6], seg_grads[7], cross_grads[0], cross_grads[1], cross_grads[2], cross_grads[3], cross_grads[4], cross_grads[5], cross_grads[6], cross_grads[7])
```

```python
import jax
import jax.numpy as jnp
from jax import lax
from jax.sharding import PartitionSpec as P

D = 768
HEAD_DIM = 64
SEG = 128
SEGS = 16
SEQ_LEN = 2048
SLICE = 192

EPS = 1e-05
NEG = -1e30
ROOT_HALF = 0.7071067811865476
INV_ROOT_TAU = 0.3989422804014327
bf16 = jnp.bfloat16
f32 = jnp.float32


def gelu_value(hidden):
    return 0.5 * hidden * (1.0 + lax.erf(hidden * ROOT_HALF))


def gelu_slope(hidden):
    return (
        0.5 * (1.0 + lax.erf(hidden * ROOT_HALF))
        + hidden * jnp.exp(-0.5 * hidden * hidden) * INV_ROOT_TAU
    )


def row_swap(k):
    def move(a):
        return lax.ppermute(a, "row", [(i, i ^ k) for i in range(4)])

    return move


to_core = row_swap(1)
to_x = row_swap(2)
to_xc = row_swap(3)


def to_y(a):
    return lax.ppermute(a, "col", [(0, 1), (1, 0)])


def to_z(a, k):
    n = lax.axis_size("dp")
    return lax.ppermute(a, "dp", [(i, i ^ k) for i in range(n)])


def ein(spec, a, b):
    return jnp.einsum(spec, a, b, preferred_element_type=f32)


def gather_weight(w):
    half = SLICE // 2
    p00 = w
    p20 = to_x(w)
    p01 = to_y(w)
    p10 = to_core(w)
    p21 = jnp.concatenate([to_y(p20[:half]), to_x(p01[half:])], axis=0)
    p30 = to_core(p20)
    p11 = to_core(p01)
    p31 = to_core(p21)
    return (
        jnp.concatenate([p00, p10, p20, p30], axis=0),
        jnp.concatenate([p01, p11, p21, p31], axis=0),
    )


def tokens_in(a, r):
    t = a.shape[1] // 4
    part = lambda k: lax.dynamic_slice_in_dim(a, (r ^ k) * t, t, 1)
    return jnp.concatenate(
        [part(0), to_core(part(1)), to_x(part(2)), to_xc(part(3))], axis=0
    )


def tokens_out(a, r):
    t = a.shape[1]
    out = jnp.zeros((SLICE, 4 * t), a.dtype)
    parts = [a[k * SLICE : (k + 1) * SLICE] for k in range(4)]
    moved = [parts[0], to_core(parts[1]), to_x(parts[2]), to_xc(parts[3])]
    for k in range(4):
        out = lax.dynamic_update_slice_in_dim(out, moved[k], (r ^ k) * t, 1)
    return out


def gather_rows(a):
    b = to_core(a)
    c = to_x(a)
    d = to_xc(a)
    return [a, b, c, d]


def norm_cols(resid):
    center = jnp.sum(resid, axis=0, keepdims=True) / D
    spread = jnp.sum(resid * resid, axis=0, keepdims=True) / D - center * center
    inv = lax.rsqrt(spread + EPS)
    return (resid - center) * inv, inv


def norm_cols_back(y, hat, inv, g):
    t = y * g
    m1 = jnp.sum(t, axis=0, keepdims=True) / D
    m2 = jnp.sum(t * hat, axis=0, keepdims=True) / D
    return inv * (t - m1 - hat * m2), jnp.sum(y * hat, axis=1), jnp.sum(y, axis=1)


def norm_rows(resid):
    center = jnp.sum(resid, axis=1, keepdims=True) / D
    spread = jnp.sum(resid * resid, axis=1, keepdims=True) / D - center * center
    inv = lax.rsqrt(spread + EPS)
    return (resid - center) * inv, inv


def norm_rows_back(y, hat, inv, g):
    t = y * g
    m1 = jnp.sum(t, axis=1, keepdims=True) / D
    m2 = jnp.sum(t * hat, axis=1, keepdims=True) / D
    return inv * (t - m1 - hat * m2), jnp.sum(y * hat, axis=0), jnp.sum(y, axis=0)


def seg_attend(proj, key_ok):
    t = proj.shape[1]
    p = proj.reshape(-1, 3, HEAD_DIM, t // SEG, SEG)
    s = ein("heBq,heBk->Bhqk", p[:, 0], p[:, 1]) * HEAD_DIM**-0.5
    s = jnp.where(key_ok.reshape(-1, 1, 1, SEG), s, NEG)
    s = s - jnp.max(s, axis=-1, keepdims=True)
    e = jnp.exp(s)
    prob = e / jnp.sum(e, axis=-1, keepdims=True)
    mix = ein("Bhqk,heBk->heBq", prob.astype(bf16), p[:, 2])
    return prob, mix.reshape(-1, t)


def seg_attend_back(proj, key_ok, dmix):
    t = proj.shape[1]
    prob, _ = seg_attend(proj, key_ok)
    p = proj.reshape(-1, 3, HEAD_DIM, t // SEG, SEG)
    dm = dmix.reshape(-1, HEAD_DIM, t // SEG, SEG)
    dv = ein("Bhqk,heBq->heBk", prob.astype(bf16), dm)
    dp = ein("heBq,heBk->Bhqk", dm, p[:, 2])
    ds = (prob * (dp - jnp.sum(prob * dp, axis=-1, keepdims=True))).astype(bf16)
    dq = ein("Bhqk,heBk->heBq", ds, p[:, 1]) * HEAD_DIM**-0.5
    dk = ein("Bhqk,heBq->heBk", ds, p[:, 0]) * HEAD_DIM**-0.5
    return jnp.stack([dq, dk, dv], axis=1).reshape(proj.shape)


def cross_scores(proj, ok):
    n = proj.shape[0]
    p = proj.reshape(n // SEGS, SEGS, -1, 3, HEAD_DIM)
    s = ein("bqhe,bkhe->bhqk", p[:, :, :, 0], p[:, :, :, 1]) * HEAD_DIM**-0.5
    s = jnp.where(ok[:, None, None, :], s, NEG)
    s = s - jnp.max(s, axis=-1, keepdims=True)
    e = jnp.exp(s)
    return e / jnp.sum(e, axis=-1, keepdims=True), p


def cross_attend(proj, ok):
    prob, p = cross_scores(proj, ok)
    mix = ein("bhqk,bkhe->bqhe", prob.astype(bf16), p[:, :, :, 2])
    return mix.reshape(proj.shape[0], -1)


def cross_attend_back(proj, ok, dmix):
    prob, p = cross_scores(proj, ok)
    dm = dmix.reshape(p[:, :, :, 2].shape)
    dv = ein("bhqk,bqhe->bkhe", prob.astype(bf16), dm)
    dp = ein("bqhe,bkhe->bhqk", dm, p[:, :, :, 2])
    ds = (prob * (dp - jnp.sum(prob * dp, axis=-1, keepdims=True))).astype(bf16)
    dq = ein("bhqk,bkhe->bqhe", ds, p[:, :, :, 1]) * HEAD_DIM**-0.5
    dk = ein("bhqk,bqhe->bkhe", ds, p[:, :, :, 0]) * HEAD_DIM**-0.5
    return jnp.stack([dq, dk, dv], axis=3).reshape(proj.shape)


def by_index(i, mine, other, axis):
    return jnp.where(
        i == 0,
        jnp.concatenate([mine, other], axis=axis),
        jnp.concatenate([other, mine], axis=axis),
    )


def group_sum(a):
    a = a + to_core(a)
    return a + to_y(a)


def dp_gather(a):
    n = lax.axis_size("dp")
    if n != 4:
        return lax.all_gather(a, "dp", axis=0, tiled=True)
    a = jnp.concatenate([a, to_z(a, 1)], axis=0)
    return jnp.concatenate([a, to_z(a, 2)], axis=0)


def dp_sum(a):
    n = lax.axis_size("dp")
    if n != 4:
        return lax.psum(a, "dp")
    a = a + to_z(a, 1)
    return a + to_z(a, 2)


def add_low(a, b):
    return (a.astype(f32) + b.astype(f32)).astype(bf16)


def reduce_grad(g, n):
    half = SLICE // 2
    pc = lambda k, j: g[k * SLICE : (k + 1) * SLICE, j * n : (j + 1) * n]
    got = to_core(jnp.concatenate([jnp.concatenate([pc(k, j) for j in range(2)], 1) for k in (1, 3)], 0))
    mine = jnp.concatenate([jnp.concatenate([pc(k, j) for j in range(2)], 1) for k in (0, 2)], 0)
    s = add_low(mine, got)
    q = lambda k, j, h: s[k * SLICE + h * half : k * SLICE + (h + 1) * half, j * n : (j + 1) * n]
    a0, a2 = q(0, 0, 0), q(1, 0, 0)
    ga = to_y(jnp.concatenate([q(0, 1, 0), q(1, 1, 0)], 0))
    a0, a2 = add_low(a0, ga[:half]), add_low(a2, ga[half:])
    a0 = add_low(a0, to_x(a2))
    b0, b1 = q(0, 0, 1), q(0, 1, 1)
    gb = to_x(jnp.concatenate([q(1, 0, 1), q(1, 1, 1)], 0))
    b0, b1 = add_low(b0, gb[:half]), add_low(b1, gb[half:])
    b0 = add_low(b0, to_y(b1))
    own = jnp.concatenate([a0, b0], 0)
    nd = lax.axis_size("dp")
    if nd != 4:
        return lax.psum(own, "dp").astype(f32)
    z = lax.axis_index("dp")
    i1, i2 = z & 1, z >> 1
    h1, h2 = SLICE // 2, SLICE // 4
    keep = lax.dynamic_slice_in_dim(own, i1 * h1, h1, 0)
    give = lax.dynamic_slice_in_dim(own, (1 - i1) * h1, h1, 0)
    keep = add_low(keep, to_z(give, 1))
    mine = lax.dynamic_slice_in_dim(keep, i2 * h2, h2, 0)
    give = lax.dynamic_slice_in_dim(keep, (1 - i2) * h2, h2, 0)
    mine = add_low(mine, to_z(give, 2))
    part = by_index(i2, mine, to_z(mine, 2), 0)
    return by_index(i1, part, to_z(part, 1), 0).astype(f32)


def body(
    hidden_in, teacher, lengths, pos_embed,
    seg_qkv, seg_proj, seg_gain1, seg_bias1, seg_up, seg_down, seg_gain2, seg_bias2,
    cross_qkv, cross_proj, cross_gain1, cross_bias1, cross_up, cross_down, cross_gain2, cross_bias2,
):
    r = lax.axis_index("row")
    y = lax.axis_index("col")
    z = lax.axis_index("dp")
    c = r & 1
    xi = r >> 1
    tok = hidden_in.shape[1] // 4
    per_chip = SEQ_LEN // tok
    seq_here = hidden_in.shape[1] // SEQ_LEN
    valid = jnp.sum(lengths).astype(f32)
    token_total = lengths.shape[0] * SEQ_LEN
    seq_id = lambda yy: (z * 2 + yy) * seq_here + xi
    my_len = lengths[seq_id(y)]
    pos = c * tok + jnp.arange(tok)
    live = pos < my_len
    key_ok = live | (pos % SEG == 0)

    small = jnp.concatenate(
        [
            jnp.stack([seg_gain1, seg_bias1, seg_gain2, seg_bias2, cross_gain1, cross_bias1, cross_gain2, cross_bias2]),
            pos_embed,
        ],
        axis=0,
    )
    sm = gather_rows(small)
    rel = jnp.concatenate(sm, axis=1).astype(f32)
    swap = lambda v: jnp.concatenate(
        [v[:, SLICE : 2 * SLICE], v[:, :SLICE], v[:, 3 * SLICE :], v[:, 2 * SLICE : 3 * SLICE]], axis=1
    )
    cabs = lambda v: jnp.where(c == 0, v, swap(v))
    sg1, sb1, sg2, sb2 = [rel[i][:, None] for i in range(4)]
    relc = cabs(rel)
    cg1, cb1, cg2, cb2 = [relc[4 + i][None, :] for i in range(4)]
    pos_tab = relc[8:]

    x = tokens_in(hidden_in, r)
    n_q, n_o, n_u = seg_qkv.shape[1], seg_proj.shape[1], seg_up.shape[1]
    wa0, wa1 = gather_weight(jnp.concatenate([seg_qkv, seg_proj], axis=1))
    wqkv = jnp.concatenate([wa0[:, :n_q], wa1[:, :n_q]], axis=1)
    wo = jnp.concatenate([wa0[:, n_q:], wa1[:, n_q:]], axis=1)
    wup = jnp.concatenate(gather_weight(seg_up), axis=1)
    wdown = jnp.concatenate(gather_weight(seg_down), axis=1)
    teach = tokens_in(teacher, r)

    def cross_weight(w):
        q = w.shape[1] // 2
        mine = lax.dynamic_slice_in_dim(w, c * q, q, 1)
        give = lax.dynamic_slice_in_dim(w, (1 - c) * q, q, 1)
        half = by_index(c, mine, to_core(give), 0)
        return jnp.concatenate([half, to_x(half)], axis=0)

    xqkv, xproj, xup, xdown = [cross_weight(w) for w in (cross_qkv, cross_proj, cross_up, cross_down)]

    proj = ein("dn,dt->nt", wqkv, x).astype(bf16)
    _, mix = seg_attend(proj, key_ok)
    mix = mix.astype(bf16)
    hat1, inv1 = norm_cols(x.astype(f32) + ein("om,mt->ot", wo, mix))
    first = hat1 * sg1 + sb1
    first_low = first.astype(bf16)
    hidden = ein("dn,dt->nt", wup, first_low)
    act = gelu_value(hidden).astype(bf16)
    slope = gelu_slope(hidden)
    hat2, inv2 = norm_cols(first + ein("on,nt->ot", wdown, act))
    seg_out = hat2 * sg2 + sb2

    pick = lambda a: cabs(a.reshape(D, -1, SEG)[:, :, 0].T)
    nloc = tok // SEG
    cls_mine = pick(seg_out) + lax.dynamic_slice_in_dim(pos_tab, c * nloc, nloc, 0)
    both = jnp.stack([cls_mine, pick(teach.astype(f32))])
    both = by_index(c, both, to_core(both), 1)
    both = by_index(y, both, to_y(both), 1)
    v, teach_cls = both[0], both[1]
    lens2 = jnp.stack([lengths[seq_id(0)], lengths[seq_id(1)]])
    ok = (jnp.arange(SEGS) * SEG)[None, :] < lens2[:, None]
    v_low = v.astype(bf16)
    cproj = ein("td,dn->tn", v_low, xqkv).astype(bf16)
    cmix = cross_attend(cproj, ok).astype(bf16)
    chat1, cinv1 = norm_rows(v + group_sum(ein("tm,om->to", cmix, xproj)))
    cfirst = chat1 * cg1 + cb1
    cfirst_low = cfirst.astype(bf16)
    chid = ein("td,dn->tn", cfirst_low, xup)
    cact = gelu_value(chid).astype(bf16)
    chat2, cinv2 = norm_rows(cfirst + group_sum(ein("tn,on->to", cact, xdown)))
    cls_out = chat2 * cg2 + cb2

    full = seg_out.reshape(D, nloc, SEG)
    own = lambda a: lax.dynamic_slice_in_dim(a, y * SEGS + c * nloc, nloc, 0)
    put = lambda a, rows: a.at[:, :, 0].set(cabs(rows).T)
    full_out = put(full, own(cls_out)).reshape(D, tok)
    masked = jnp.where(live[None, :], full_out - teach.astype(f32), 0.0)
    square = jnp.sum(masked * masked)
    scale = token_total / valid
    grad_full = masked * scale
    ycls = jnp.where(ok.reshape(-1, 1), cls_out - teach_cls, 0.0) * scale

    cd2, cdg2, cdb2 = norm_rows_back(ycls, chat2, cinv2, cg2)
    cd2_low = cd2.astype(bf16)
    cdhid = (ein("to,on->tn", cd2_low, xdown) * gelu_slope(chid)).astype(bf16)
    cd1, cdg1, cdb1 = norm_rows_back(cd2 + group_sum(ein("tn,dn->td", cdhid, xup)), chat1, cinv1, cg1)
    cd1_low = cd1.astype(bf16)
    cdmix = ein("to,om->tm", cd1_low, xproj).astype(bf16)
    cdproj = cross_attend_back(cproj, ok, cdmix).astype(bf16)
    dcls = cd1 + group_sum(ein("tn,dn->td", cdproj, xqkv))
    pos_part = jnp.sum(dcls.reshape(-1, SEGS, D), axis=0)

    wide = jnp.concatenate([v_low, cd1_low, cfirst_low, cd2_low], axis=1).reshape(-1, 4, 2, 2, SLICE)
    wide_at = lambda i: lax.dynamic_index_in_dim(wide[:, :, i], c, 2, keepdims=False).reshape(wide.shape[0], -1)
    narrow = jnp.concatenate([cdproj, cmix, cdhid, cact], axis=1)
    pack = lambda i: jnp.concatenate([wide_at(i), narrow], axis=1)
    acts = jnp.concatenate([pack(0), to_x(pack(1))], axis=0)
    acts = dp_gather(acts)
    wide_all = acts[:, : 4 * SLICE]
    nq = acts[:, 4 * SLICE :]
    other = to_core(nq)
    cuts = (cdproj.shape[1], cmix.shape[1], cdhid.shape[1], cact.shape[1])
    halves, at = [], 0
    for w in cuts:
        halves.append(by_index(c, nq[:, at : at + w], other[:, at : at + w], 1))
        at += w
    w4 = [wide_all[:, i * SLICE : (i + 1) * SLICE] for i in range(4)]
    g_cqkv = ein("td,tn->dn", w4[0], halves[0])
    g_cproj = ein("td,tn->dn", w4[1], halves[1])
    g_cup = ein("td,tn->dn", w4[2], halves[2])
    g_cdown = ein("td,tn->dn", w4[3], halves[3])

    yb = put(grad_full.reshape(D, nloc, SEG), own(dcls)).reshape(D, tok).astype(bf16).astype(f32)
    d2, dg2, db2 = norm_cols_back(yb, hat2, inv2, sg2)
    d2_low = d2.astype(bf16)
    dhid = (ein("on,ot->nt", wdown, d2_low) * slope).astype(bf16)
    d1, dg1, db1 = norm_cols_back(d2 + ein("dn,nt->dt", wup, dhid), hat1, inv1, sg1)
    d1_low = d1.astype(bf16)
    dmix = ein("om,ot->mt", wo, d1_low).astype(bf16)
    dproj = seg_attend_back(proj, key_ok, dmix).astype(bf16)
    dx = d1 + ein("dn,nt->dt", wqkv, dproj)
    w_down = ein("ot,nt->on", d2_low, act).astype(bf16)
    w_up = ein("dt,nt->dn", first_low, dhid).astype(bf16)
    w_proj = ein("ot,mt->om", d1_low, mix).astype(bf16)
    w_qkv = ein("dt,nt->dn", x, dproj).astype(bf16)
    g_down = reduce_grad(w_down, n_u)
    g_up = reduce_grad(w_up, n_u)
    g_proj = reduce_grad(w_proj, n_o)
    g_qkv = reduce_grad(w_qkv, n_q)

    sp = jnp.stack([dg1, db1, dg2, db2, jnp.full((D,), square, f32)]).reshape(5, 4, SLICE)
    sp = sp[:, 0::2] + to_core(sp[:, 1::2])
    cp = jnp.concatenate([cdg1, cdb1, cdg2, cdb2, pos_part.reshape(-1)]).reshape(4 + SEGS, 2, 2, SLICE)
    cp = lax.dynamic_index_in_dim(cp, c, 2, keepdims=False)
    sp = sp + to_y(sp)
    al = jnp.concatenate([sp, cp], axis=0)
    al = al[:, 0] + to_x(al[:, 1])
    al = dp_sum(al)
    loss = al[4, 0] / (2.0 * valid)
    return (
        tokens_out(full_out.astype(bf16), r),
        loss,
        tokens_out(dx.astype(bf16), r),
        al[9:],
        g_qkv, g_proj, al[0], al[1], g_up, g_down, al[2], al[3],
        g_cqkv, g_cproj, al[5], al[6], g_cup, g_cdown, al[7], al[8],
    )


def solution(mesh):
    wide, cut, one = P("row", ("dp", "col")), P("row", "col"), P("row")
    block = (cut, cut, one, one, cut, cut, one, one)
    in_specs = (wide, wide, P(), P(None, "row")) + block + block
    out_specs = (wide, P(), wide, P(None, "row")) + block + block
    return jax.shard_map(body, mesh=mesh, in_specs=in_specs, out_specs=out_specs, check_vma=False)
```

```python
import functools
import jax
import jax.numpy as jnp
from jax import lax
from jax.experimental import pallas as pl
from jax.experimental.pallas import tpu as pltpu
from jax.sharding import PartitionSpec as P

D = 768
HEAD_DIM = 64
SEG = 128
SEGS = 16
SEQ_LEN = 2048
SLICE = 192
HALF = 96
EPS = 1e-05
NEG = -1e30
ROOT_HALF = 0.7071067811865476
INV_ROOT_TAU = 0.3989422804014327
bf16 = jnp.bfloat16
f32 = jnp.float32
GROUP = 12
GROUP_BACK = 6
COST = 0.005
VMEM_LIMIT = 60 * 1024 * 1024

NN = (((1,), (0,)), ((), ()))
NT = (((1,), (1,)), ((), ()))
TN = (((0,), (0,)), ((), ()))


def scalars(lengths, tok):
    r, y, z = lax.axis_index("row"), lax.axis_index("col"), lax.axis_index("dp")
    return z & 1, lengths[(z * lax.axis_size("col") + y) * 2 + (r >> 1)], (r & 1) * tok


def scale_of(lengths):
    n = lengths.shape[0]
    total = sum(lengths[i] for i in range(n)) if n <= 16 else lax.fori_loop(0, n, lambda i, a: a + lengths[i], 0)
    return (n * SEQ_LEN) / jnp.full((1, 1), total, jnp.int32).astype(f32)


def rel_rows(ref):
    r = lax.axis_index("row")
    return [ref[pl.ds(pl.multiple_of((r ^ k) * SLICE, 16), SLICE), :] for k in range(4)]


def put_rel_rows(ref, a):
    r = lax.axis_index("row")
    for k in range(4):
        ref[pl.ds(pl.multiple_of((r ^ k) * SLICE, 16), SLICE), :] = a[k * SLICE : (k + 1) * SLICE, :]


def dot(a, b, dims):
    return lax.dot_general(a, b, dims, preferred_element_type=f32)


def params(n=1):
    if n == 0:
        return pltpu.CompilerParams(vmem_limit_bytes=VMEM_LIMIT)
    return pltpu.CompilerParams(dimension_semantics=("arbitrary",) * n, vmem_limit_bytes=VMEM_LIMIT)


ANY = pl.BlockSpec(memory_space=pl.ANY)
SMEM = pl.BlockSpec(memory_space=pltpu.SMEM)


def whole(shape):
    return pl.BlockSpec(shape, lambda *_: (0,) * len(shape))


def piece_plan(refs, p):
    own, y1, x1, z1, y2, z2, c1, c2 = refs
    hi = p * HALF
    ho = (1 - p) * HALF
    x, xc = 2 * SLICE, 3 * SLICE
    return [
        (own, 0, SLICE, 0, 0), (c1, 0, SLICE, SLICE, 0),
        (x1, 0, HALF, x + hi, 0), (z1, 0, HALF, x + ho, 0),
        (c1, 2 * SLICE, HALF, xc + hi, 0), (c2, 0, HALF, xc + ho, 0),
        (y1, 0, SLICE, 0, 1), (c1, SLICE, SLICE, SLICE, 1),
        (y2, 0, HALF, x + hi, 1), (z2, 0, HALF, x + ho, 1),
        (c2, HALF, HALF, xc + hi, 1), (c2, 2 * HALF, HALF, xc + ho, 1),
    ]


def piece_copies(refs, dst, sem, p, src_cols, dst_col, base=0):
    lo, n = src_cols
    return [
        pltpu.make_async_copy(
            src.at[pl.ds(at, rows), pl.ds(lo, n)],
            dst.at[pl.ds(pl.multiple_of(row, 16), rows), pl.ds(dst_col(j), n)],
            sem.at[base + i],
        )
        for i, (src, at, rows, row, j) in enumerate(piece_plan(refs, p))
    ]


def gathered_copies(ref, dst, sem):
    r = lax.axis_index("row")
    n = ref.shape[2]
    return [
        pltpu.make_async_copy(
            ref.at[(r ^ k) * 2 + j], dst.at[pl.ds(k * SLICE, SLICE), pl.ds(j * n, n)], sem.at[k * 2 + j]
        )
        for k in range(4)
        for j in range(2)
    ]


def norm_cols(resid):
    center = jnp.sum(resid, axis=0, keepdims=True) * (1.0 / D)
    spread = jnp.sum(resid * resid, axis=0, keepdims=True) * (1.0 / D) - center * center
    inv = lax.rsqrt(spread + EPS)
    return (resid - center) * inv, inv


def norm_back_cols(y, hat, inv, g):
    t = y * g
    m1 = jnp.sum(t, axis=0, keepdims=True) * (1.0 / D)
    m2 = jnp.sum(t * hat, axis=0, keepdims=True) * (1.0 / D)
    return inv * (t - m1 - hat * m2)


def probs_group(qs, ks, ok):
    ss = [dot(k, q, TN) for q, k in zip(qs, ks)]
    ss = [jnp.where(ok, s * HEAD_DIM**-0.5, NEG) for s in ss]
    ms = [jnp.max(s, axis=0, keepdims=True) for s in ss]
    es = [jnp.exp(s - m) for s, m in zip(ss, ms)]
    ts = [1.0 / jnp.sum(e, axis=0, keepdims=True) for e in es]
    return [e * t for e, t in zip(es, ts)]


def key_ok_of(scal, b, tile):
    pos = lax.broadcasted_iota(jnp.int32, (SEG, SEG), 0)
    at = scal[2] + pl.program_id(0) * tile + b * SEG
    return (pos + at < scal[1]) | (pos == 0)


def put_cls(tile, hat, inv, hatc_o, invc_o):
    n = tile // SEG
    for b in range(n):
        at = pl.ds(pl.program_id(0) * n + b, 1)
        hatc_o[at, :] = hat[:, b * SEG : (b + 1) * SEG].T[0:1, :]
        invc_o[at, :] = jnp.broadcast_to(inv[:, b * SEG : b * SEG + 1], (1, SEG))


def attn_fwd_kernel(tile, lengths, xs, g1, b1, *rest):
    scal = scalars(lengths, tile * pl.num_programs(0))
    refs = rest[:8]
    proj_o, mix_o, hat_o, inv_o, low_o, hatc_o, invc_o, w, wo, sem = rest[8:]
    n_q = w.shape[1] // 2
    n_o = wo.shape[1] // 2

    @pl.when(pl.program_id(0) == 0)
    def _():
        cps = piece_copies(refs, w, sem, scal[0], (0, n_q), lambda j: j * n_q)
        cps += piece_copies(refs, wo, sem, scal[0], (n_q, n_o), lambda j: j * n_o, 12)
        for c in cps:
            c.start()
        for c in cps:
            c.wait()

    x = jnp.concatenate(rel_rows(xs), axis=0)
    proj_o[...] = dot(w[...], x, TN).astype(bf16)
    for b in range(tile // SEG):
        ok = key_ok_of(scal, b, tile)
        cols = slice(b * SEG, (b + 1) * SEG)
        for h0 in range(0, D // HEAD_DIM, GROUP):
            qkv = [
                [
                    proj_o[(h * 3 + j) * HEAD_DIM : (h * 3 + j + 1) * HEAD_DIM, cols]
                    for j in range(3)
                ]
                for h in range(h0, h0 + GROUP)
            ]
            pts = probs_group([a[0] for a in qkv], [a[1] for a in qkv], ok)
            mixed = [dot(a[2], p.astype(bf16), NN).astype(bf16) for a, p in zip(qkv, pts)]
            mix_o[h0 * HEAD_DIM : (h0 + GROUP) * HEAD_DIM, cols] = jnp.concatenate(mixed, axis=0)
    hat, inv = norm_cols(x.astype(f32) + dot(wo[...], mix_o[...], NN))
    hat_o[...] = hat
    inv_o[...] = inv
    low_o[...] = (hat * g1[...] + b1[...]).astype(bf16)
    put_cls(tile, hat, inv, hatc_o, invc_o)


def attn_fwd(lengths, xs, g1, b1, pieces, tile=256):
    t = xs.shape[1]
    n = pieces[0].shape[1]
    n_q = n * 3 // 4
    n_o = n - n_q
    colb = lambda rows: pl.BlockSpec((rows, tile), lambda i: (0, i))
    return pl.pallas_call(
        functools.partial(attn_fwd_kernel, tile),
        grid=(t // tile,),
        in_specs=[SMEM, colb(D)] + [whole((D, 1))] * 2 + [ANY] * 8,
        out_specs=[colb(2 * n_q), colb(D), colb(D), colb(1), colb(D), whole((t // SEG, D)), whole((t // SEG, SEG))],
        out_shape=[
            jax.ShapeDtypeStruct((2 * n_q, t), bf16),
            jax.ShapeDtypeStruct((D, t), bf16),
            jax.ShapeDtypeStruct((D, t), f32),
            jax.ShapeDtypeStruct((1, t), f32),
            jax.ShapeDtypeStruct((D, t), bf16),
            jax.ShapeDtypeStruct((t // SEG, D), f32),
            jax.ShapeDtypeStruct((t // SEG, SEG), f32),
        ],
        scratch_shapes=[
            pltpu.VMEM((D, 2 * n_q), bf16),
            pltpu.VMEM((D, 2 * n_o), bf16),
            pltpu.SemaphoreType.DMA((24,)),
        ],
        compiler_params=params(),
        name="seg_attend",
        cost_estimate=cost(2 * t * D * D * 4 + 4 * t * SEG * D, 20 * 1024 * t, t * SEG * 12),
    )(lengths, xs, g1, b1, *pieces)


def ffn_up_kernel(low, wg, act_o, slope_o, w, lt, sem):
    i = pl.program_id(0)

    @pl.when(i == 0)
    def _():
        cps = gathered_copies(wg, w, sem)
        for c in cps:
            c.start()
        lt[...] = low[...].T
        for c in cps:
            c.wait()

    wid = act_o.shape[1]
    at = pl.multiple_of(i * wid, 128)
    hidden = dot(lt[...], w[:, pl.ds(at, wid)], NN)
    phi = 0.5 * (1.0 + lax.erf(hidden * ROOT_HALF))
    act_o[...] = (hidden * phi).astype(bf16)
    slope = phi + hidden * jnp.exp(-0.5 * hidden * hidden) * INV_ROOT_TAU
    slope_o[...] = slope.astype(bf16)


def ffn_up(low, wg, wid=512):
    t = low.shape[1]
    n = wg.shape[2] * 2
    colb = pl.BlockSpec((t, wid), lambda i: (0, i))
    return pl.pallas_call(
        ffn_up_kernel,
        grid=(n // wid,),
        in_specs=[whole((D, t)), ANY],
        out_specs=[colb, colb],
        out_shape=[jax.ShapeDtypeStruct((t, n), bf16)] * 2,
        scratch_shapes=[pltpu.VMEM((D, n), bf16), pltpu.VMEM((t, D), bf16), pltpu.SemaphoreType.DMA((12,))],
        compiler_params=params(),
        name="seg_up",
        cost_estimate=cost(2 * t * D * n, 4 * t * n, 2 * t * n),
    )(low, wg)


def ffn_down_kernel(tile, act, hat1, g1, b1, g2, b2, wg, hat_o, inv_o, hatc_o, invc_o, w, sem):
    i = pl.program_id(0)

    @pl.when(i == 0)
    def _():
        cps = gathered_copies(wg, w, sem)
        for c in cps:
            c.start()
        for c in cps:
            c.wait()

    first = hat1[...] * g1[...] + b1[...]
    hat, inv = norm_cols(first + dot(w[...], act[...], NT))
    hat_o[...] = hat
    inv_o[...] = inv
    put_cls(tile, hat, inv, hatc_o, invc_o)


def ffn_down(act, hat1, g1, b1, g2, b2, wg, tile=256):
    t, n = act.shape
    colb = lambda rows: pl.BlockSpec((rows, tile), lambda i: (0, i))
    return pl.pallas_call(
        functools.partial(ffn_down_kernel, tile),
        grid=(t // tile,),
        in_specs=[pl.BlockSpec((tile, n), lambda i: (i, 0)), colb(D)] + [whole((D, 1))] * 4 + [ANY],
        out_specs=[colb(D), colb(1), whole((t // SEG, D)), whole((t // SEG, SEG))],
        out_shape=[
            jax.ShapeDtypeStruct((D, t), f32),
            jax.ShapeDtypeStruct((1, t), f32),
            jax.ShapeDtypeStruct((t // SEG, D), f32),
            jax.ShapeDtypeStruct((t // SEG, SEG), f32),
        ],
        scratch_shapes=[pltpu.VMEM((D, n), bf16), pltpu.SemaphoreType.DMA((12,))],
        compiler_params=params(),
        name="seg_down",
        cost_estimate=cost(2 * t * D * n, 2 * t * n + 8 * t * D, 0),
    )(act, hat1, g1, b1, g2, b2, wg)


def start_all(cps):
    for c in cps:
        c.start()


def wait_all(cps):
    for c in cps:
        c.wait()


def ffn_back_kernel(tile, lengths, hat2, inv2, xs, slope, g2, b2, wg, d2_o, d2low_o, dhid_o, sums_o, sq_o, wd, acc, sem):
    scal = scalars(lengths, tile * pl.num_programs(0))
    i = pl.program_id(0)
    cd = gathered_copies(wg, wd, sem)

    @pl.when(i == 0)
    def _():
        start_all(cd)
        acc[...] = jnp.zeros_like(acc)
        sq_o[...] = jnp.zeros_like(sq_o)

    lane = lax.broadcasted_iota(jnp.int32, (1, tile), 1) + i * tile
    keep = (lane + scal[2] < scal[1]) & (lane % SEG != 0)
    h2 = hat2[...]
    teach = jnp.concatenate(rel_rows(xs), axis=0).astype(f32)
    diff = jnp.where(keep, h2 * g2[...] + b2[...] - teach, 0.0)
    sq_o[...] += jnp.sum(diff * diff, axis=0, keepdims=True)
    y = (diff * scale_of(lengths)).astype(bf16).astype(f32)
    acc[0] += fold_lanes(y * h2)
    acc[1] += fold_lanes(y)
    d2 = norm_back_cols(y, h2, inv2[...], g2[...])
    d2_o[...] = d2
    d2_low = d2.astype(bf16)
    d2low_o[...] = d2_low

    @pl.when(i == 0)
    def _():
        wait_all(cd)

    dhid_o[...] = (dot(d2_low, wd[...], TN) * slope[...].astype(f32)).astype(bf16)
    lane_sums(acc, sums_o)


def fold_lanes(v):
    return sum(v[:, k * SEG : (k + 1) * SEG] for k in range(v.shape[1] // SEG))


def lane_sums(acc, sums_o):
    @pl.when(pl.program_id(0) == pl.num_programs(0) - 1)
    def _():
        for k in range(2):
            sums_o[k : k + 1, :] = jnp.sum(acc[k].T, axis=0, keepdims=True)


def ffn_back(lengths, hat2, inv2, teach, slope, g2, b2, wg, tile=256):
    t, n = slope.shape
    colb = lambda rows: pl.BlockSpec((rows, tile), lambda i: (0, i))
    rowb = pl.BlockSpec((tile, n), lambda i: (i, 0))
    return pl.pallas_call(
        functools.partial(ffn_back_kernel, tile),
        grid=(t // tile,),
        in_specs=[SMEM, colb(D), colb(1), colb(D), rowb] + [whole((D, 1))] * 2 + [ANY],
        out_specs=[colb(D), colb(D), rowb, whole((2, D)), whole((1, tile))],
        out_shape=[
            jax.ShapeDtypeStruct((D, t), f32),
            jax.ShapeDtypeStruct((D, t), bf16),
            jax.ShapeDtypeStruct((t, n), bf16),
            jax.ShapeDtypeStruct((2, D), f32),
            jax.ShapeDtypeStruct((1, tile), f32),
        ],
        scratch_shapes=[
            pltpu.VMEM((D, n), bf16),
            pltpu.VMEM((2, D, SEG), f32),
            pltpu.SemaphoreType.DMA((12,)),
        ],
        compiler_params=params(),
        name="seg_down_back",
        cost_estimate=cost(2 * t * D * n, 6 * t * n),
    )(lengths, hat2, inv2, teach, slope, g2, b2, wg)


def up_back_kernel(tile, d2, dhid, hat1, inv1, g1, wg, d1_o, sums_o, wu, acc, sem):
    i = pl.program_id(0)

    @pl.when(i == 0)
    def _():
        cu = gathered_copies(wg, wu, sem)
        start_all(cu)
        acc[...] = jnp.zeros_like(acc)
        wait_all(cu)

    s = d2[...] + dot(wu[...], dhid[...], NT)
    h1 = hat1[...]
    acc[0] += fold_lanes(s * h1)
    acc[1] += fold_lanes(s)
    d1_o[...] = norm_back_cols(s, h1, inv1[...], g1[...])
    lane_sums(acc, sums_o)


def up_back(d2, dhid, hat1, inv1, g1, wg, tile=256):
    t, n = dhid.shape
    colb = lambda rows: pl.BlockSpec((rows, tile), lambda i: (0, i))
    return pl.pallas_call(
        functools.partial(up_back_kernel, tile),
        grid=(t // tile,),
        in_specs=[colb(D), pl.BlockSpec((tile, n), lambda i: (i, 0)), colb(D), colb(1), whole((D, 1)), ANY],
        out_specs=[colb(D), whole((2, D))],
        out_shape=[jax.ShapeDtypeStruct((D, t), f32), jax.ShapeDtypeStruct((2, D), f32)],
        scratch_shapes=[
            pltpu.VMEM((D, n), bf16),
            pltpu.VMEM((2, D, SEG), f32),
            pltpu.SemaphoreType.DMA((12,)),
        ],
        compiler_params=params(),
        name="seg_up_back",
        cost_estimate=cost(2 * t * D * n, 4 * t * n),
    )(d2, dhid, hat1, inv1, g1, wg)


def norm_back_rows(y, hat, inv, g):
    t = y * g
    m1 = jnp.sum(t, axis=1, keepdims=True) * (1.0 / D)
    m2 = jnp.sum(t * hat, axis=1, keepdims=True) * (1.0 / D)
    return inv * (t - m1 - hat * m2)


def col_of(rows, k):
    n = rows.shape[0]
    pick = lax.broadcasted_iota(jnp.int32, (n, 1), 0) == k
    row = jnp.sum(jnp.where(pick, rows, 0.0), axis=0, keepdims=True)
    return jnp.broadcast_to(row, (SEG, rows.shape[1])).T


def put_rows(a, cls, tile):
    n = tile // SEG
    lane0 = lax.broadcasted_iota(jnp.int32, (1, SEG), 1) == 0
    return jnp.concatenate(
        [
            jnp.where(lane0, col_of(cls[...], pl.program_id(0) * n + b), a[:, b * SEG : (b + 1) * SEG])
            for b in range(n)
        ],
        axis=1,
    )


def half_copies(refs, dst, sem, p, j, src_cols, base=0):
    lo, n = src_cols
    return [
        pltpu.make_async_copy(
            src.at[pl.ds(at, rows), pl.ds(lo, n)], dst.at[pl.ds(pl.multiple_of(row, 16), rows), :], sem.at[base + i]
        )
        for i, (src, at, rows, row, _) in enumerate([a for a in piece_plan(refs, p) if a[4] == j])
    ]


def attn_back_kernel(tile, j, lengths, proj, d1, cls, *rest):
    scal = scalars(lengths, tile * pl.num_programs(0))
    refs = rest[:8]
    outs, (w, wo, sem) = rest[8:-3], rest[-3:]
    dproj_o = outs[0]
    i = pl.program_id(0)
    n_q, n_o = w.shape[1], wo.shape[1]
    cq = half_copies(refs, w, sem, scal[0], j, (0, n_q))

    @pl.when(i == 0)
    def _():
        co = half_copies(refs, wo, sem, scal[0], j, (n_q, n_o), 6)
        start_all(co)
        start_all(cq)
        wait_all(co)

    d1_all = put_rows(d1[...], cls, tile) if j == 1 else d1[...]
    d1_low = cls[...] if j == 0 else d1_all.astype(bf16)
    dmix = dot(wo[...], d1_low, TN).astype(bf16)
    for b in range(tile // SEG):
        ok = key_ok_of(scal, b, tile)
        cols = slice(b * SEG, (b + 1) * SEG)
        for h0 in range(0, n_o // HEAD_DIM, GROUP_BACK):
            hs = range(h0, h0 + GROUP_BACK)
            part = lambda k: [proj[(h * 3 + k) * HEAD_DIM : (h * 3 + k + 1) * HEAD_DIM, cols] for h in hs]
            qs, ks, vs = part(0), part(1), part(2)
            dms = [dmix[h * HEAD_DIM : (h + 1) * HEAD_DIM, cols] for h in hs]
            ps = probs_group(qs, ks, ok)
            dps = [dot(v, dm, TN) for v, dm in zip(vs, dms)]
            dvs = [dot(dm, p.astype(bf16), NT) for dm, p in zip(dms, ps)]
            inner = [jnp.sum(p * dp, axis=0, keepdims=True) for p, dp in zip(ps, dps)]
            dss = [(p * (dp - a)).astype(bf16) for p, dp, a in zip(ps, dps, inner)]
            dqs = [dot(k, ds, NN) * HEAD_DIM**-0.5 for k, ds in zip(ks, dss)]
            dks = [dot(q, ds, NT) * HEAD_DIM**-0.5 for q, ds in zip(qs, dss)]
            out = [a.astype(bf16) for trio in zip(dqs, dks, dvs) for a in trio]
            dproj_o[h0 * 3 * HEAD_DIM : (h0 + GROUP_BACK) * 3 * HEAD_DIM, cols] = jnp.concatenate(out, axis=0)

    @pl.when(i == 0)
    def _():
        wait_all(cq)

    dx = d1_all + dot(w[...], dproj_o[...], NN)
    if j == 1:
        outs[1][...] = d1_low
        outs[2][...] = dx
    else:
        put_rel_rows(outs[1], dx.astype(bf16))


def attn_back(j, lengths, proj, d1, cls, pieces, tile=256):
    t = proj.shape[1]
    n = pieces[0].shape[1]
    n_q = n * 3 // 4
    n_o = n - n_q
    colb = lambda rows, k=0: pl.BlockSpec((rows, tile), lambda i: (k, i))
    wide = [((D, t), bf16, D), ((D, t), f32, D)] if j == 1 else [((D, t), bf16, D)]
    return pl.pallas_call(
        functools.partial(attn_back_kernel, tile, j),
        grid=(t // tile,),
        in_specs=[SMEM, colb(n_q, j), colb(D), whole(cls.shape) if j == 1 else colb(D)] + [ANY] * 8,
        out_specs=[colb(n_q)] + [colb(a[2]) for a in wide],
        out_shape=[jax.ShapeDtypeStruct((n_q, t), bf16)] + [jax.ShapeDtypeStruct(a[0], a[1]) for a in wide],
        scratch_shapes=[
            pltpu.VMEM((D, n_q), bf16),
            pltpu.VMEM((D, n_o), bf16),
            pltpu.SemaphoreType.DMA((12,)),
        ],
        compiler_params=params(),
        name="seg_attend_back",
        cost_estimate=cost(t * D * D * 4 + 6 * t * SEG * D, 10 * 1024 * t, t * SEG * 6),
    )(lengths, proj, d1, cls, *pieces)


def split_rows(g, keep_o, send_o):
    keep_o[:SLICE, :] = g[:SLICE]
    send_o[:SLICE, :] = g[SLICE : 2 * SLICE]
    keep_o[SLICE:, :] = g[2 * SLICE : 3 * SLICE]
    send_o[SLICE:, :] = g[3 * SLICE :]


def grad_kernel(a, b, o):
    r = lax.axis_index("row")
    g = dot(a[...], b[...], NN).astype(bf16)
    for k in range(4):
        o[r ^ k, 0] = g[k * SLICE : (k + 1) * SLICE]


def weight_grad(a, b, wid=512):
    t, n = b.shape
    q = n // 2 // wid
    return pl.pallas_call(
        grad_kernel,
        grid=(n // wid,),
        in_specs=[whole((D, t)), pl.BlockSpec((t, wid), lambda i: (0, i))],
        out_specs=pl.BlockSpec((4, 1, SLICE, wid), lambda i: (0, i // q, 0, i % q)),
        out_shape=jax.ShapeDtypeStruct((4, 2, SLICE, n // 2), bf16),
        compiler_params=params(),
        name="weight_grad",
        cost_estimate=cost(2 * t * D * n, 2 * (t + D) * n, 0),
    )(a, b)


def attn_grad_kernel(steps_q, xs, low, dproj, mix, keep_o, send_o):
    i = pl.program_id(0)

    @pl.when(i < steps_q)
    def _():
        x = jnp.concatenate(rel_rows(xs), axis=0)
        split_rows(dot(x, dproj[...], NT).astype(bf16), keep_o, send_o)

    @pl.when(i == steps_q)
    def _():
        split_rows(dot(low[...], mix[...], NT).astype(bf16), keep_o, send_o)


def attn_grad(j, xs, low, dproj, mix):
    t = low.shape[1]
    n_q, n_o = dproj.shape[0], mix.shape[0] // 2
    wid = n_o
    q = n_q // wid
    out = pl.BlockSpec((2 * SLICE, wid), lambda i: (0, i))
    return pl.pallas_call(
        functools.partial(attn_grad_kernel, q),
        grid=(q + 1,),
        in_specs=[whole((D, t)), whole((D, t)), pl.BlockSpec((wid, t), lambda i: (jnp.minimum(i, q - 1), 0)),
                  pl.BlockSpec((wid, t), lambda i: (j, 0))],
        out_specs=[out, out],
        out_shape=[jax.ShapeDtypeStruct((2 * SLICE, n_q + n_o), bf16)] * 2,
        compiler_params=params(),
        name="attend_weight_grad",
        cost_estimate=cost(t * D * 4 * D, (t + D) * 4 * D, 0),
    )(xs, low, dproj, mix)


def add4(refs):
    return sum(a[...].astype(f32) for a in refs)


def chip_kernel(k0, g0, k1, g1, o):
    here = (lax.axis_index("row") >> 1) * 2 + lax.axis_index("col")
    for jj, (k, g) in enumerate(((k0, g0), (k1, g1))):
        a = add4((k, g)).astype(bf16)
        for xx in range(2):
            at = pl.multiple_of((here ^ (xx * 2 + jj)) * SLICE, 16)
            o[pl.ds(at, SLICE), :] = a[xx * SLICE : (xx + 1) * SLICE]


def chip_sum(keep, got, wid=768):
    n = keep.shape[1] // 2
    k = n // wid
    lo = pl.BlockSpec((2 * SLICE, wid), lambda i: (0, i))
    hi = pl.BlockSpec((2 * SLICE, wid), lambda i: (0, i + k))
    return pl.pallas_call(
        chip_kernel,
        grid=(k,),
        in_specs=[lo, lo, hi, hi],
        out_specs=pl.BlockSpec((4 * SLICE, wid), lambda i: (0, i)),
        out_shape=jax.ShapeDtypeStruct((4 * SLICE, n), bf16),
        compiler_params=params(),
        name="chip_sum",
        cost_estimate=cost(0, 12 * SLICE * n),
    )(keep, got, keep, got)


def chip_half_kernel(k0, g0, a_o, b_o):
    a = add4((k0, g0)).astype(bf16)
    a_o[...] = a[:SLICE]
    b_o[...] = a[SLICE:]


def chip_half(keep, got, wid=768):
    n = keep.shape[1]
    lo = pl.BlockSpec((2 * SLICE, wid), lambda i: (0, i))
    return pl.pallas_call(
        chip_half_kernel,
        grid=(n // wid,),
        in_specs=[lo, lo],
        out_specs=[pl.BlockSpec((SLICE, wid), lambda i: (0, i))] * 2,
        out_shape=[jax.ShapeDtypeStruct((SLICE, n), bf16)] * 2,
        compiler_params=params(),
        name="chip_sum",
        cost_estimate=cost(0, 6 * SLICE * n),
    )(keep, got)


def add_stacked(refs):
    out = []
    for a in refs:
        for i in range(0, a.shape[0], SLICE):
            out.append(a[i : i + SLICE, :].astype(f32))
    return sum(out)


def plane_kernel(*refs):
    parts, outs, total_s = refs[:-5], refs[-5:-1], refs[-1]
    z = lax.axis_index("dp")
    h = outs[0].shape[0]
    total_s[...] = add_stacked(parts).astype(bf16)
    for k, o in enumerate(outs):
        o[...] = total_s[pl.ds(pl.multiple_of((z ^ k) * h, 16), h), :]


def plane_sum(*parts):
    n = parts[0].shape[1]
    vm = pl.BlockSpec(memory_space=pltpu.VMEM)
    return pl.pallas_call(
        plane_kernel,
        in_specs=[vm] * len(parts),
        out_specs=[vm] * 4,
        out_shape=[jax.ShapeDtypeStruct((SLICE // 4, n), bf16)] * 4,
        scratch_shapes=[pltpu.VMEM((SLICE, n), bf16)],
        compiler_params=params(0),
        name="plane_sum",
        cost_estimate=cost(0, 10 * SLICE * n),
    )(*parts)


def quarter_kernel(*refs):
    refs[-1][...] = add4(refs[:-1]).astype(bf16)


def quarter_sum(*parts):
    vm = pl.BlockSpec(memory_space=pltpu.VMEM)
    return pl.pallas_call(
        quarter_kernel,
        in_specs=[vm] * len(parts),
        out_specs=vm,
        out_shape=jax.ShapeDtypeStruct(parts[0].shape, bf16),
        compiler_params=params(0),
        name="quarter_sum",
        cost_estimate=cost(0, 1e6),
    )(*parts)


def place_kernel(cut, p0, p1, p2, p3, *outs):
    z = lax.axis_index("dp")
    h = p0.shape[0]
    for k, p in enumerate((p0, p1, p2, p3)):
        rows = pl.ds(pl.multiple_of((z ^ k) * h, 8), h)
        outs[0][rows, :] = p[:, :cut].astype(f32)
        if len(outs) > 1:
            outs[1][rows, :] = p[:, cut:].astype(f32)


def place_quarters(parts, cut):
    vm = pl.BlockSpec(memory_space=pltpu.VMEM)
    h, n = parts[0].shape
    shapes = [(4 * h, cut)] + ([(4 * h, n - cut)] if cut < n else [])
    return pl.pallas_call(
        functools.partial(place_kernel, cut),
        in_specs=[vm] * 4,
        out_specs=[vm] * len(shapes),
        out_shape=[jax.ShapeDtypeStruct(a, f32) for a in shapes],
        compiler_params=params(0),
        name="place_quarters",
        cost_estimate=cost(0, 2e6),
    )(*parts)


def output_kernel(tile, hat2, g2, b2, cls, o):
    put_rel_rows(o, put_rows(hat2[...] * g2[...] + b2[...], cls, tile).astype(bf16))


def emit_output(hat2, g2, b2, cls, tile=256):
    t = hat2.shape[1]
    colb = lambda rows: pl.BlockSpec((rows, tile), lambda i: (0, i))
    return pl.pallas_call(
        functools.partial(output_kernel, tile),
        grid=(t // tile,),
        in_specs=[colb(D)] + [whole((D, 1))] * 2 + [whole(cls.shape)],
        out_specs=colb(D),
        out_shape=jax.ShapeDtypeStruct((D, t), bf16),
        compiler_params=params(),
        name="emit_output",
        cost_estimate=cost(0, 6 * t * D),
    )(hat2, g2, b2, cls)
def cost(flops, nbytes, trans=0):
    return pl.CostEstimate(flops=int(flops * COST), bytes_accessed=int(nbytes * COST), transcendentals=int(trans * COST))


def vmcall(kernel, name, smem, vmem, anys, outs, scratch, c):
    vm = pl.BlockSpec(memory_space=pltpu.VMEM)
    return pl.pallas_call(
        kernel,
        in_specs=[SMEM] * len(smem) + [vm] * len(vmem) + [ANY] * len(anys),
        out_specs=[vm] * len(outs),
        out_shape=[jax.ShapeDtypeStruct(s, d) for s, d in outs],
        scratch_shapes=scratch,
        compiler_params=params(0),
        name=name,
        cost_estimate=c,
    )(*smem, *vmem, *anys)


def axes():
    r = lax.axis_index("row")
    return r, lax.axis_index("col"), lax.axis_index("dp")


def prep_kernel(qkv, proj, a_o, xa_o):
    p = lax.axis_index("dp") & 1
    n_q = qkv.shape[1]
    half = pl.ds(pl.multiple_of(p * HALF, 16), HALF)
    xa_o[:, :n_q] = qkv[half, :]
    xa_o[:, n_q:] = proj[half, :]
    a_o[:, :n_q] = qkv[...]
    a_o[:, n_q:] = proj[...]


def prep(qkv, proj):
    n = qkv.shape[1] + proj.shape[1]
    return vmcall(
        prep_kernel, "prep_weights", [], [qkv, proj], [], [((SLICE, n), bf16), ((HALF, n), bf16)], [], cost(0, 2e6),
    )


VEC = 32


def stack_kernel(x, *rest):
    vecs, o = rest[:-1], rest[-1]
    t = o.shape[1]
    rows = o.shape[0] // 4
    for q in range(4):
        o[q * rows : q * rows + SLICE, :] = x[:, q * t : (q + 1) * t]
    if vecs:
        v = jnp.concatenate([a[...].reshape(1, SLICE).astype(f32) for a in vecs[:-1]] + [vecs[-1][...].astype(f32)], axis=0)
        v = jnp.concatenate([v, jnp.zeros((VEC - v.shape[0], SLICE), f32)], axis=0).astype(bf16)
        for q in range(4):
            o[q * rows + SLICE : (q + 1) * rows, :SLICE] = v
            o[q * rows + SLICE : (q + 1) * rows, SLICE:] = jnp.zeros((VEC, t - SLICE), bf16)


def token_stack(x, *vecs):
    rows = SLICE + (VEC if vecs else 0)
    return vmcall(
        stack_kernel, "token_stack", [], [x, *vecs], [], [((4 * rows, x.shape[1] // 4), bf16)], [], cost(0, 3e6)
    )[0]


def join_kernel(p, o):
    t = p.shape[1]
    for q in range(4):
        o[:, q * t : (q + 1) * t] = p[q * SLICE : (q + 1) * SLICE, :]


def token_join(p):
    return vmcall(join_kernel, "token_join", [], [p], [], [((SLICE, 4 * p.shape[1]), bf16)], [], cost(0, 3e6))[0]


def cross_prep_kernel(qkv, proj, up, down, mine_o, give_o):
    c = lax.axis_index("row") & 1
    at = 0
    for w in (qkv, proj, up, down):
        q = w.shape[1] // 2
        a, b = w[:, :q].astype(f32), w[:, q:].astype(f32)
        mine_o[:, at : at + q] = jnp.where(c == 0, a, b).astype(bf16)
        give_o[:, at : at + q] = jnp.where(c == 0, b, a).astype(bf16)
        at += q


def cross_prep(qkv, proj, up, down):
    vm = pl.BlockSpec(memory_space=pltpu.VMEM)
    n = (qkv.shape[1] + proj.shape[1] + up.shape[1] + down.shape[1]) // 2
    return pl.pallas_call(
        cross_prep_kernel,
        in_specs=[vm] * 4,
        out_specs=[vm] * 2,
        out_shape=[jax.ShapeDtypeStruct((SLICE, n), bf16)] * 2,
        compiler_params=params(0),
        name="cross_prep",
        cost_estimate=cost(0, 4e6),
    )(qkv, proj, up, down)


def pick_kernel(mine, got, o):
    c, p = lax.axis_index("row") & 1, lax.axis_index("dp") & 1

    @pl.when(c == p)
    def _():
        o[...] = mine[...]

    @pl.when(c != p)
    def _():
        o[...] = got[...]


def cross_pick(mine, got):
    vm = pl.BlockSpec(memory_space=pltpu.VMEM)
    return pl.pallas_call(
        pick_kernel,
        in_specs=[vm] * 2,
        out_specs=vm,
        out_shape=jax.ShapeDtypeStruct(mine.shape, bf16),
        compiler_params=params(0),
        name="cross_pick",
        cost_estimate=cost(0, 3e6),
    )(mine, got)


def swap_cores(v):
    s = SLICE
    return jnp.concatenate([v[:, s : 2 * s], v[:, :s], v[:, 3 * s :], v[:, 2 * s : 3 * s]], axis=1)


def core_order(v):
    c = lax.axis_index("row") & 1
    return jnp.where(c == 0, v, swap_cores(v))


def vec_kernel(h, x_o, rel_o, abs_o, c0, c1, c2, c3):
    rows = h.shape[0] // 4
    for q in range(4):
        x_o[q * SLICE : (q + 1) * SLICE, :] = h[q * rows : q * rows + SLICE, :]
    r = lax.axis_index("row")
    part = [
        h[pl.ds(pl.multiple_of((r ^ k) * rows + SLICE, 16), VEC), :][:, : 2 * SEG].astype(f32)[:24, :SLICE] for k in range(4)
    ]
    rel = jnp.concatenate(part, axis=1)
    rel_o[...] = rel
    abs_o[...] = core_order(rel)
    cols = rel[:8].T
    for i, o in enumerate((c0, c1, c2, c3)):
        o[...] = cols[:, i : i + 1]


def unstack(h):
    n = 8 + SEGS
    return vmcall(
        vec_kernel, "unstack", [], [h], [],
        [((D, h.shape[1]), bf16)] + [((n, D), f32)] * 2 + [((D, 1), f32)] * 4, [], cost(0, 3e6),
    )


H2, H1, TE, IV = slice(0, D), slice(D, 2 * D), slice(2 * D, 3 * D), slice(3 * D, 3 * D + SEG)
MSG = 3 * D + SEG


def msg_kernel(hat2, inv2, hat1, teach, o):
    n = hat2.shape[0]
    o[:, H2] = core_order(hat2[...])
    o[:, H1] = core_order(hat1[...])
    o[:, IV] = inv2[...]
    rows = []
    parts = rel_rows(teach)
    for b in range(n):
        at = slice(b * SEG, (b + 1) * SEG)
        rows.append(jnp.concatenate([t[:, at].astype(f32).T[0:1, :] for t in parts], axis=1))
    o[:, TE] = core_order(jnp.concatenate(rows, axis=0))


def cls_message(hat2, inv2, hat1, teach):
    vm = pl.BlockSpec(memory_space=pltpu.VMEM)
    return pl.pallas_call(
        msg_kernel,
        in_specs=[vm] * 4,
        out_specs=vm,
        out_shape=jax.ShapeDtypeStruct((hat2.shape[0], MSG), f32),
        compiler_params=params(0),
        name="cls_message",
        cost_estimate=cost(0, 2e6),
    )(hat2, inv2, hat1, teach)


def pair_kernel(a, b, o):
    n = a.shape[0]
    c = lax.axis_index("row") & 1
    o[pl.ds(pl.multiple_of(c * n, 8), n), :] = a[...]
    o[pl.ds(pl.multiple_of((1 - c) * n, 8), n), :] = b[...]


def pair_rows(a, b):
    return vmcall(pair_kernel, "core_pair", [], [a, b], [], [((2 * a.shape[0], a.shape[1]), a.dtype)], [], cost(0, 1e6))[0]


def fold_kernel(a, b, o):
    o[...] = add4((a, b)).astype(o.dtype)


def fold(a, b):
    return vmcall(fold_kernel, "core_fold", [], [a, b], [], [(a.shape, a.dtype)], [], cost(0, 1e5))[0]


def cross_copies(refs, dst, sem, lo, n, base=0):
    c, p = lax.axis_index("row") & 1, lax.axis_index("dp") & 1
    at = [c * SLICE, (1 - c) * SLICE, 2 * SLICE + p * SLICE, 2 * SLICE + (1 - p) * SLICE]
    return [
        pltpu.make_async_copy(
            src.at[:, pl.ds(lo, n)], dst.at[pl.ds(pl.multiple_of(row, 16), SLICE), :], sem.at[base + i]
        )
        for i, (src, row) in enumerate(zip(refs, at))
    ]


def norm_rows(resid):
    center = jnp.sum(resid, axis=1, keepdims=True) * (1.0 / D)
    spread = jnp.sum(resid * resid, axis=1, keepdims=True) * (1.0 / D) - center * center
    inv = lax.rsqrt(spread + EPS)
    return (resid - center) * inv, inv


def total(parts):
    return sum(p[...].astype(f32) for p in parts)


def cls_rows(vec, m):
    pos = vec[8 : 8 + SEGS, :]
    return m[:, H2] * vec[2:3, :] + vec[3:4, :] + jnp.concatenate([pos] * (m.shape[0] // SEGS), axis=0)


def cross_probs(cproj, lens):
    n = cproj.shape[0]
    qi = lax.broadcasted_iota(jnp.int32, (n, n), 0)
    ki = lax.broadcasted_iota(jnp.int32, (n, n), 1)
    limit = jnp.where(ki < SEGS, lens[0], lens[1])
    ok = (qi // SEGS == ki // SEGS) & ((ki % SEGS) * SEG < limit)
    out = []
    for h in range(cproj.shape[1] // (3 * HEAD_DIM)):
        q, k, v = [cproj[:, (3 * h + j) * HEAD_DIM : (3 * h + j + 1) * HEAD_DIM] for j in range(3)]
        s = jnp.where(ok, dot(q, k, NT) * HEAD_DIM**-0.5, NEG)
        e = jnp.exp(s - jnp.max(s, axis=1, keepdims=True))
        out.append((q, k, v, e / jnp.sum(e, axis=1, keepdims=True)))
    return out


def group_lens(lengths, rows):
    r, _, z = axes()
    here = lax.axis_size("col")
    return [lengths[(z * here + j) * 2 + (r >> 1)] for j in range(2)]


def cross1_kernel(lengths, vec, m0, m1, *rest):
    refs = rest[:4]
    m_o, cproj_o, cmix_o, part_o, vlow_o, w, sem = rest[4:]
    _, y, _ = axes()
    n_q = cproj_o.shape[1]
    cps = cross_copies(refs, w, sem, 0, w.shape[1])
    start_all(cps)
    n = m0.shape[0]
    for m, yy in ((m0, y), (m1, 1 - y)):
        m_o[pl.ds(pl.multiple_of(yy * n, 8), n), :] = m[...]
    v_low = cls_rows(vec[...], m_o[...]).astype(bf16)
    vlow_o[...] = v_low
    wait_all(cps)
    cproj = dot(v_low, w[:, :n_q], NN).astype(bf16)
    cproj_o[...] = cproj
    mix = [dot(p.astype(bf16), v, NN) for _, _, v, p in cross_probs(cproj, group_lens(lengths, None))]
    mix = jnp.concatenate(mix, axis=1).astype(bf16)
    cmix_o[...] = mix
    part_o[...] = dot(mix, w[:, n_q:], NT).astype(bf16)


def cross1(lengths, vec, msgs, refs, n_q, n_o):
    n = 2 * msgs[0].shape[0]
    return vmcall(
        cross1_kernel, "cross_attend", [lengths], [vec, *msgs], refs,
        [((n, MSG), f32), ((n, n_q), bf16), ((n, n_o), bf16), ((n, D), bf16), ((n, D), bf16)],
        [pltpu.VMEM((D, n_q + n_o), bf16), pltpu.SemaphoreType.DMA((4,))],
        cost(2e7, 2e6),
    )


def cross2_kernel(vec, m, p0, p1, *rest):
    refs = rest[:4]
    hat_o, inv_o, low_o, act_o, slope_o, part_o, wu, wd, sem = rest[4:]
    n = wu.shape[1]
    lo = refs[0].shape[1] - 2 * n
    cps = cross_copies(refs, wu, sem, lo, n) + cross_copies(refs, wd, sem, lo + n, n, 4)
    start_all(cps)
    hat, inv = norm_rows(cls_rows(vec[...], m[...]) + total((p0, p1)))
    hat_o[...] = hat
    inv_o[...] = jnp.broadcast_to(inv, inv_o.shape)
    low = (hat * vec[4:5, :] + vec[5:6, :]).astype(bf16)
    low_o[...] = low
    wait_all(cps)
    hidden = dot(low, wu[...], NN)
    phi = 0.5 * (1.0 + lax.erf(hidden * ROOT_HALF))
    act = (hidden * phi).astype(bf16)
    act_o[...] = act
    slope_o[...] = phi + hidden * jnp.exp(-0.5 * hidden * hidden) * INV_ROOT_TAU
    part_o[...] = dot(act, wd[...], NT).astype(bf16)


def cross2(vec, m, parts, refs, n_u):
    n = m.shape[0]
    return vmcall(
        cross2_kernel, "cross_ffn", [], [vec, m, *parts], refs,
        [((n, D), f32), ((n, SEG), f32), ((n, D), bf16), ((n, n_u), bf16), ((n, n_u), f32), ((n, D), bf16)],
        [pltpu.VMEM((D, n_u), bf16)] * 2 + [pltpu.SemaphoreType.DMA((8,))],
        cost(2e7, 3e6),
    )


def own_rows(ref, n):
    r, y, _ = axes()
    return ref[pl.ds(pl.multiple_of((y * 2 + (r & 1)) * n, 8), n), :]


def cross3_kernel(lengths, vec, m, hat1, slope, p0, p1, *rest):
    refs = rest[:4]
    cls_o, sq_o, sums_o, d2_o, d2low_o, dhid_o, part_o, wu, wd, keep, sem = rest[4:]
    n = wu.shape[1]
    lo = refs[0].shape[1] - 2 * n
    cps = cross_copies(refs, wu, sem, lo, n) + cross_copies(refs, wd, sem, lo + n, n, 4)
    start_all(cps)
    first = hat1[...] * vec[4:5, :] + vec[5:6, :]
    hat2, inv2 = norm_rows(first + total((p0, p1)))
    out = hat2 * vec[6:7, :] + vec[7:8, :]
    rows = out.shape[0]
    ti = lax.broadcasted_iota(jnp.int32, (rows, 1), 0)
    lens = group_lens(lengths, rows)
    live = (ti % SEGS) * SEG < jnp.where(ti < SEGS, lens[0], lens[1])
    diff = jnp.where(live, out - m[:, TE], 0.0)
    k = cls_o.shape[0]
    keep[...] = out
    cls_o[...] = core_order(own_rows(keep, k))
    keep[...] = diff
    mine = own_rows(keep, k)
    sq_o[...] = jnp.sum(mine * mine, axis=0, keepdims=True)
    yv = diff * scale_of(lengths)
    sums_o[0:1, :] = jnp.sum(yv * hat2, axis=0, keepdims=True)
    sums_o[1:2, :] = jnp.sum(yv, axis=0, keepdims=True)
    d2 = norm_back_rows(yv, hat2, inv2, vec[6:7, :])
    d2_o[...] = d2
    d2_low = d2.astype(bf16)
    d2low_o[...] = d2_low
    wait_all(cps)
    dhid = (dot(d2_low, wd[...], NN) * slope[...]).astype(bf16)
    dhid_o[...] = dhid
    part_o[...] = dot(dhid, wu[...], NT).astype(bf16)


def cross3(lengths, vec, m, hat1, slope, parts, refs):
    n, n_u = slope.shape
    return vmcall(
        cross3_kernel, "cross_ffn_back", [lengths], [vec, m, hat1, slope, *parts], refs,
        [((n // 4, D), f32), ((1, D), f32), ((2, D), f32), ((n, D), f32), ((n, D), bf16), ((n, n_u), bf16), ((n, D), bf16)],
        [pltpu.VMEM((D, n_u), bf16)] * 2 + [pltpu.VMEM((n, D), f32), pltpu.SemaphoreType.DMA((8,))],
        cost(2e7, 3e6),
    )


def cross4_kernel(lengths, vec, d2, hat1, inv1, cproj, p0, p1, *rest):
    refs = rest[:4]
    d1_o, d1low_o, sums_o, dproj_o, part_o, w, sem = rest[4:]
    n_q = dproj_o.shape[1]
    cps = cross_copies(refs, w, sem, 0, w.shape[1])
    start_all(cps)
    s = d2[...] + total((p0, p1))
    h1 = hat1[...]
    sums_o[0:1, :] = jnp.sum(s * h1, axis=0, keepdims=True)
    sums_o[1:2, :] = jnp.sum(s, axis=0, keepdims=True)
    d1 = norm_back_rows(s, h1, inv1[:, 0:1], vec[4:5, :])
    d1_o[...] = d1
    d1_low = d1.astype(bf16)
    d1low_o[...] = d1_low
    wait_all(cps)
    dmix = dot(d1_low, w[:, n_q:], NN).astype(bf16)
    outs = []
    for h, (q, k, v, p) in enumerate(cross_probs(cproj[...], group_lens(lengths, None))):
        dm = dmix[:, h * HEAD_DIM : (h + 1) * HEAD_DIM]
        dv = dot(p.astype(bf16), dm, TN)
        dp = dot(dm, v, NT)
        ds = (p * (dp - jnp.sum(p * dp, axis=1, keepdims=True))).astype(bf16)
        outs += [dot(ds, k, NN) * HEAD_DIM**-0.5, dot(ds, q, TN) * HEAD_DIM**-0.5, dv]
    dproj = jnp.concatenate(outs, axis=1).astype(bf16)
    dproj_o[...] = dproj
    part_o[...] = dot(dproj, w[:, :n_q], NT).astype(bf16)


def cross4(lengths, vec, d2, hat1, inv1, cproj, parts, refs, n_o):
    n, n_q = cproj.shape
    return vmcall(
        cross4_kernel, "cross_attend_back", [lengths], [vec, d2, hat1, inv1, cproj, *parts], refs,
        [((n, D), f32), ((n, D), bf16), ((2, D), f32), ((n, n_q), bf16), ((n, D), bf16)],
        [pltpu.VMEM((D, n_q + n_o), bf16), pltpu.SemaphoreType.DMA((4,))],
        cost(2e7, 2e6),
    )


def quarter_copies(ref, dst, sem, base=0):
    r, y, _ = axes()
    n = dst.shape[1]
    cols = pl.ds(pl.multiple_of((r & 1) * n, 128), n)
    return [
        pltpu.make_async_copy(
            ref.at[(((r >> 1) ^ (s >> 1)) * 2 + (s & 1)) * 2 + y, :, cols],
            dst.at[pl.ds(s * SLICE, SLICE), :],
            sem.at[base + s],
        )
        for s in range(4)
    ]


def cross5_kernel(vec, m, d1, p0, p1, *rest):
    ups, downs, pos_o, sums_o, d2_o, d2low_o, low_o, act_o, dhid_o, part_o, wu, wd, sem = rest
    cps = quarter_copies(ups, wu, sem) + quarter_copies(downs, wd, sem, 4)
    start_all(cps)
    dcls = d1[...] + total((p0, p1))
    pos_o[...] = sum(dcls[i : i + SEGS] for i in range(0, dcls.shape[0], SEGS))
    yv = dcls.astype(bf16).astype(f32)
    h2 = m[:, H2]
    sums_o[0:1, :] = jnp.sum(yv * h2, axis=0, keepdims=True)
    sums_o[1:2, :] = jnp.sum(yv, axis=0, keepdims=True)
    d2 = norm_back_rows(yv, h2, m[:, 3 * D : 3 * D + 1], vec[2:3, :])
    d2_o[...] = d2
    d2_low = d2.astype(bf16)
    d2low_o[...] = d2_low
    low = (m[:, H1] * vec[0:1, :] + vec[1:2, :]).astype(bf16)
    low_o[...] = low
    wait_all(cps)
    hidden = dot(low, wu[...], NN)
    phi = 0.5 * (1.0 + lax.erf(hidden * ROOT_HALF))
    act_o[...] = (hidden * phi).astype(bf16)
    slope = phi + hidden * jnp.exp(-0.5 * hidden * hidden) * INV_ROOT_TAU
    dhid = (dot(d2_low, wd[...], NN) * slope).astype(bf16)
    dhid_o[...] = dhid
    part_o[...] = dot(dhid, wu[...], NT).astype(bf16)


def cross5(vec, m, d1, parts, ups, downs):
    n = m.shape[0]
    n_u = ups.shape[2] // 2
    return vmcall(
        cross5_kernel, "cls_ffn_back", [], [vec, m, d1, *parts], [ups, downs],
        [((SEGS, D), f32), ((2, D), f32), ((n, D), f32), ((n, D), bf16), ((n, D), bf16), ((n, n_u), bf16),
         ((n, n_u), bf16), ((n, D), bf16)],
        [pltpu.VMEM((D, n_u), bf16)] * 2 + [pltpu.SemaphoreType.DMA((12,))],
        cost(3e7, 3e6),
    )


def cross6_kernel(vec, m, d2, inv1, p0, p1, d1_o, sums_o, keep):
    s = d2[...] + total((p0, p1))
    h1 = m[:, H1]
    sums_o[0:1, :] = jnp.sum(s * h1, axis=0, keepdims=True)
    sums_o[1:2, :] = jnp.sum(s, axis=0, keepdims=True)
    n = d1_o.shape[0]
    keep[...] = s
    mine = own_rows(keep, n)
    keep[...] = h1
    d1_o[...] = core_order(norm_back_rows(mine, own_rows(keep, n), inv1[:, 0:1], vec[0:1, :]))


def cross6(vec, m, d2, inv1, parts):
    n = m.shape[0]
    return vmcall(
        cross6_kernel, "cls_norm_back", [], [vec, m, d2, inv1, *parts], [],
        [((n // 4, D), f32), ((2, D), f32)], [pltpu.VMEM((n, D), f32)], cost(0, 1e6),
    )


def pack_kernel(count, *refs):
    wides, narrows, (own_o, far_o) = refs[:count], refs[count:-2], refs[-2:]
    c = lax.axis_index("row") & 1
    at = 0
    for w in wides:
        v = w[...].astype(f32)
        s = [v[:, i * SLICE : (i + 1) * SLICE] for i in range(4)]
        own_o[:, at : at + SLICE] = jnp.where(c == 0, s[0], s[1]).astype(bf16)
        far_o[:, at : at + SLICE] = jnp.where(c == 0, s[2], s[3]).astype(bf16)
        at += SLICE
    for w in narrows:
        v = w[...]
        own_o[:, at : at + v.shape[1]] = v
        far_o[:, at : at + v.shape[1]] = v
        at += v.shape[1]


def pack_acts(wides, narrows):
    n = wides[0].shape[0]
    width = len(wides) * SLICE + sum(a.shape[1] for a in narrows)
    return vmcall(
        functools.partial(pack_kernel, len(wides)), "pack_factors", [], [*wides, *narrows], [],
        [((n, width), bf16)] * 2, [], cost(0, 2e6),
    )


def join_rows_kernel(*refs):
    o, at = refs[-1], 0
    for a in refs[:-1]:
        o[at : at + a.shape[0], :] = a[...]
        at += a.shape[0]


def join_rows(*parts):
    rows = sum(a.shape[0] for a in parts)
    return vmcall(join_rows_kernel, "join_rows", [], parts, [], [((rows, parts[0].shape[1]), bf16)], [], cost(0, 1e6))[0]


def factor_kernel(widths, mine, theirs, *outs):
    c = lax.axis_index("row") & 1
    at = len(widths) * SLICE
    for i, (w, o) in enumerate(zip(widths, outs)):
        wide = mine[:, i * SLICE : (i + 1) * SLICE]
        got = [dot(wide, b[:, at : at + w], TN) for b in (mine, theirs)]
        o[:, :w] = jnp.where(c == 0, got[0], got[1])
        o[:, w:] = jnp.where(c == 0, got[1], got[0])
        at += w


def factor_grads(mine, theirs, widths):
    return vmcall(
        functools.partial(factor_kernel, widths), "factor_grads", [], [mine, theirs], [],
        [((SLICE, 2 * w), f32) for w in widths], [], cost(1e9, 8e6),
    )


def row_swap(k):
    def move(a):
        return lax.ppermute(a, "row", [(i, i ^ k) for i in range(4)])

    return move


to_core = row_swap(1)
to_x = row_swap(2)
ALL = ("dp", "row", "col")


def exchange(a, groups):
    return lax.all_to_all(a, ALL, 0, 0, axis_index_groups=groups, tiled=True)


def spots():
    n = lax.axis_size("dp")
    return lambda z, r, y: (z * 4 + r) * 2 + y, n


def to_rows(a):
    at, n = spots()
    return exchange(a, [[at(z, r, y) for r in range(4)] for z in range(n) for y in range(2)])


def to_plane(a):
    at, n = spots()
    return exchange(a, [[at(z, 2 * x + c, y) for x in range(2) for y in range(2)] for z in range(n) for c in range(2)])


def to_y(a):
    return lax.ppermute(a, "col", [(0, 1), (1, 0)])


def to_z(a, k):
    n = lax.axis_size("dp")
    return lax.ppermute(a, "dp", [(i, i ^ k) for i in range(n)])


def after(a, *first):
    return lax.optimization_barrier((a, *first))[0]


class Order:
    def __init__(self):
        self.last = None

    def __call__(self, fn, *args):
        leaves, tree = jax.tree.flatten(args)
        if self.last is not None:
            leaves = lax.optimization_barrier((*leaves, self.last))[:-1]
        out = fn(*jax.tree.unflatten(tree, leaves))
        self.last = jax.tree.leaves(out)[-1]
        return out


def by_index(i, mine, other, axis):
    return jnp.where(
        i == 0,
        jnp.concatenate([mine, other], axis=axis),
        jnp.concatenate([other, mine], axis=axis),
    )


def group_send(run, a):
    a = run(fold, a, to_core(a))
    return (a, to_y(a))


def gather_all(a):
    return lax.all_gather(a, ("row", "col"), axis=0, tiled=False)


def scatter_all(a):
    return lax.psum_scatter(a.reshape(-1, *a.shape[2:]), ("row", "col"), scatter_dimension=0, tiled=False)


def dp_gather(a):
    n = lax.axis_size("dp")
    if n != 4:
        return (lax.all_gather(a, "dp", axis=0, tiled=True),)
    return (a, to_z(a, 1), to_z(a, 2), to_z(a, 3))


def dp_sum(a):
    n = lax.axis_size("dp")
    if n != 4:
        return lax.psum(a, "dp")
    return (a + to_z(a, 1)) + (to_z(a, 2) + to_z(a, 3))


def to_d(a):
    return lax.ppermute(a, ("row", "col"), [(i, i ^ 5) for i in range(8)])


def dp_scatter(run, *parts):
    if lax.axis_size("dp") != 4:
        return (lax.psum(sum(p.astype(f32) for p in parts).astype(bf16), "dp"),)
    q = run(plane_sum, *parts)
    return (q[0], *[to_z(q[k], k) for k in (1, 2, 3)])


def dp_quarters(run, quarters):
    if len(quarters) == 1:
        return quarters
    q = run(quarter_sum, *quarters)
    return (q, *[to_z(q, k) for k in (1, 2, 3)])


def dp_place(run, quarters, cut):
    if len(quarters) == 1:
        a = quarters[0].astype(f32)
        return [a[:, :cut], a[:, cut:]]
    return run(lambda *a: place_quarters(a, cut), *quarters)


def body(
    hidden_in, teacher, lengths, pos_embed,
    seg_qkv, seg_proj, seg_gain1, seg_bias1, seg_up, seg_down, seg_gain2, seg_bias2,
    cross_qkv, cross_proj, cross_gain1, cross_bias1, cross_up, cross_down, cross_gain2, cross_bias2,
):
    run = Order()
    c = lax.axis_index("row") & 1
    n_q, n_o, n_u = seg_qkv.shape[1], seg_proj.shape[1], seg_up.shape[1]
    q_q, q_o, q_u = n_q // 2, n_o // 2, n_u // 2

    vecs = (seg_gain1, seg_bias1, seg_gain2, seg_bias2, cross_gain1, cross_bias1, cross_gain2, cross_bias2)
    wa, xa = run(prep, seg_qkv, seg_proj)
    ax = to_x(xa)
    ay = to_y(wa)
    h = run(token_stack, hidden_in, *vecs, pos_embed)
    ax_ = after(ax, h)
    h = to_rows(h)
    az = to_z(ax_, 1)
    ayx = to_y(ax_)
    wu = gather_all(after(seg_up, ax))
    ayz = to_z(ayx, 1)
    ac1 = to_core(run(join_rows, wa, ay, after(ax, h)))
    h, rel, vab, sg1, sb1, sg2, sb2 = run(unstack, h)
    ac2 = to_core(run(join_rows, az, ayx, ayz))
    pa = (wa, ay, ax, az, ayx, ayz, ac1, ac2)
    cw_mine, cw_give = run(cross_prep, cross_qkv, cross_proj, cross_up, cross_down)
    wd = gather_all(after(seg_down, h))
    cw_got = to_core(cw_give)
    proj, mix, hat1, inv1, low, hatc1, invc1 = run(attn_fwd, lengths, h, sg1, sb1, pa)
    teach = run(token_stack, teacher)
    act, slope = run(ffn_up, low, wu)
    teach = to_rows(teach)
    cw_x = to_x(run(cross_pick, cw_mine, cw_got))
    hat2, inv2, hatc2, invc2 = run(ffn_down, act, hat1, sg1, sb1, sg2, sb2, wd)
    cw_z = to_z(after(cw_x, hatc2), 1)
    cw = (cw_mine, cw_got, cw_x, cw_z)

    msg = run(cls_message, hatc2, invc2, hatc1, teach)
    msg = run(pair_rows, msg, to_core(msg))
    msgs = (msg, to_y(msg))
    d2, d2_low, dhid, sums_a, sq = run(ffn_back, lengths, hat2, inv2, teach, slope, sg2, sb2, wd)
    m, cproj, cmix, part, v_low = run(lambda *a: cross1(*a, q_q, q_o), lengths, vab, msgs, cw)
    part = group_send(run, part)
    grad_d = run(weight_grad, d2_low, act)
    sum_d = scatter_all(grad_d)
    chat1, cinv1, clow, cact, cslope, part = run(lambda *a: cross2(*a, q_u), vab, m, part, cw)
    part = group_send(run, part)
    grad_u = run(weight_grad, low, dhid)
    sum_u = scatter_all(grad_u)
    cls_out, csq, csums_a, cd2, cd2_low, cdhid, part = run(cross3, lengths, vab, m, chat1, cslope, part, cw)
    part = group_send(run, part)
    d1, sums_b = run(up_back, d2, dhid, hat1, inv1, sg1, wu)
    cd1, cd1_low, csums_b, cdproj, part = run(
        lambda *a: cross4(*a, q_o), lengths, vab, cd2, chat1, cinv1, cproj, part, cw
    )
    part = group_send(run, part)
    outs = run(emit_output, hat2, sg2, sb2, cls_out)
    pos_part, ssums_a, sd2, sd2_low, slow, sact, sdhid, part = run(cross5, vab, m, cd1, part, wu, wd)
    part = group_send(run, part)
    s_own, s_far = run(pack_acts, (sd2_low, slow), (sact, sdhid))
    d1c, ssums_b = run(cross6, vab, m, sd2, invc1, part)
    c_own, c_far = run(pack_acts, (v_low, cd1_low, clow, cd2_low), (cdproj, cmix, cdhid, cact))
    s_far = to_x(s_far)
    c_far = to_x(c_far)
    outs = to_rows(outs)
    dproj1, d1_low, dxp = run(lambda *a: attn_back(1, *a), lengths, proj, d1, d1c, pa)
    facts = run(join_rows, s_own, s_far)
    facts_c = to_core(facts)
    keep1, send = run(lambda *a: attn_grad(1, *a), h, d1_low, dproj1, mix)
    got1 = to_core(send)
    acts = run(join_rows, c_own, c_far)
    acts = dp_gather(acts)
    f_d, f_u = run(lambda a, b: factor_grads(a, b, (q_u, q_u)), facts, facts_c)
    a_y, a_d = run(chip_half, keep1, got1)
    a_y, a_d = to_y(a_y), to_d(a_d)
    tot_d = run(lambda a, f: (a.astype(f32) + f).astype(bf16), sum_d, f_d)
    tot_u = run(lambda a, f: (a.astype(f32) + f).astype(bf16), sum_u, f_u)
    tot_d, tot_u = lax.psum((tot_d, tot_u), "dp")
    dproj0, dxs = run(lambda *a: attn_back(0, *a), lengths, proj, dxp, d1_low, pa)
    acts = run(join_rows, *acts) if len(acts) > 1 else acts[0]
    acts_c = to_core(acts)
    output = run(token_join, outs)
    keep0, send = run(lambda *a: attn_grad(0, *a), h, after(d1_low, a_y, a_d), dproj0, mix)
    got0 = to_core(send)
    dxs = to_rows(after(dxs, outs))
    g_cqkv, g_cproj, g_cup, g_cdown = run(
        lambda a, b: factor_grads(a, b, (q_q, q_o, q_u, q_u)), acts, acts_c
    )
    a_0, a_x = run(chip_half, keep0, got0)
    a_x = to_x(a_x)
    dx_out = run(token_join, dxs)
    q_a = dp_scatter(run, a_0, a_y, a_x, a_d)

    def small_one(a, b, d, e, s, t):
        sq_all = jnp.full((1, D), jnp.sum(s) + jnp.sum(t), f32)
        al = jnp.concatenate([b, a, sq_all], axis=0).reshape(5, 4, SLICE)
        return al[:, 0::2], al[:, 1::2]

    def small_two(*parts):
        cp = jnp.concatenate(parts, axis=0)
        cp = cp.reshape(cp.shape[0], 2, 2, SLICE)
        return lax.dynamic_index_in_dim(cp, c, 2, keepdims=False)

    sp_keep, sp_give = run(small_one, sums_a, sums_b, ssums_b, ssums_a, sq, csq)
    cp = run(small_two, ssums_b, ssums_a, csums_b, csums_a, pos_part)
    sp = run(lambda a, b: a + b, sp_keep, to_core(sp_give))
    q_a = dp_quarters(run, q_a)
    sp = run(lambda a, b: a + b, sp, to_y(sp))
    al = jnp.concatenate([sp, cp], axis=0)
    al = run(lambda a, b: a[:, 0] + b, al, to_x(al[:, 1]))
    g_down, g_up = run(lambda a, b: (a.astype(f32), b.astype(f32)), tot_d, tot_u)
    al = dp_sum(al)
    g_qkv, g_proj = dp_place(run, q_a, n_q)
    valid = jnp.sum(lengths).astype(f32)
    seg_small = al[0:4] + al[5:9]
    loss = al[4, 0] / (2.0 * valid)
    return (
        output, loss, dx_out, al[13:],
        g_qkv, g_proj, seg_small[0], seg_small[1], g_up, g_down, seg_small[2], seg_small[3],
        g_cqkv, g_cproj, al[9], al[10], g_cup, g_cdown, al[11], al[12],
    )


def solution(mesh):
    wide, cut, one = P("row", ("dp", "col")), P("row", "col"), P("row")
    block = (cut, cut, one, one, cut, cut, one, one)
    in_specs = (wide, wide, P(), P(None, "row")) + block + block
    out_specs = (wide, P(), wide, P(None, "row")) + block + block
    return jax.shard_map(body, mesh=mesh, in_specs=in_specs, out_specs=out_specs, check_vma=False)
```

```python
import functools
import jax
import jax.numpy as jnp
from jax import lax
from jax.experimental import pallas as pl
from jax.experimental.pallas import tpu as pltpu
from jax.sharding import PartitionSpec as P

D = 768
HEAD_DIM = 64
SEG = 128
SEGS = 16
SEQ_LEN = 2048
SLICE = 192
HALF = 96
EPS = 1e-05
NEG = -1e30
ROOT_HALF = 0.7071067811865476
INV_ROOT_TAU = 0.3989422804014327
bf16 = jnp.bfloat16
f32 = jnp.float32
GROUP = 12
GROUP_BACK = 6
COST = 0.005
VMEM_LIMIT = 60 * 1024 * 1024

NN = (((1,), (0,)), ((), ()))
NT = (((1,), (1,)), ((), ()))
TN = (((0,), (0,)), ((), ()))


def scalars(lengths, tok):
    r, y, z = lax.axis_index("row"), lax.axis_index("col"), lax.axis_index("dp")
    return z & 1, lengths[(z * lax.axis_size("col") + y) * 2 + (r >> 1)], (r & 1) * tok


def scale_of(lengths):
    n = lengths.shape[0]
    total = sum(lengths[i] for i in range(n)) if n <= 16 else lax.fori_loop(0, n, lambda i, a: a + lengths[i], 0)
    return (n * SEQ_LEN) / jnp.full((1, 1), total, jnp.int32).astype(f32)


def rel_rows(ref):
    r = lax.axis_index("row")
    return [ref[pl.ds(pl.multiple_of((r ^ k) * SLICE, 16), SLICE), :] for k in range(4)]


def put_rel_rows(ref, a):
    r = lax.axis_index("row")
    for k in range(4):
        ref[pl.ds(pl.multiple_of((r ^ k) * SLICE, 16), SLICE), :] = a[k * SLICE : (k + 1) * SLICE, :]


def dot(a, b, dims):
    return lax.dot_general(a, b, dims, preferred_element_type=f32)


def params(n=1):
    if n == 0:
        return pltpu.CompilerParams(vmem_limit_bytes=VMEM_LIMIT)
    return pltpu.CompilerParams(dimension_semantics=("arbitrary",) * n, vmem_limit_bytes=VMEM_LIMIT)


ANY = pl.BlockSpec(memory_space=pl.ANY)
SMEM = pl.BlockSpec(memory_space=pltpu.SMEM)


def whole(shape):
    return pl.BlockSpec(shape, lambda *_: (0,) * len(shape))


def piece_plan(refs, p):
    own, y1, x1, z1, y2, z2, c1, c2 = refs
    hi = p * HALF
    ho = (1 - p) * HALF
    x, xc = 2 * SLICE, 3 * SLICE
    return [
        (own, 0, SLICE, 0, 0), (c1, 0, SLICE, SLICE, 0),
        (x1, 0, HALF, x + hi, 0), (z1, 0, HALF, x + ho, 0),
        (c1, 2 * SLICE, HALF, xc + hi, 0), (c2, 0, HALF, xc + ho, 0),
        (y1, 0, SLICE, 0, 1), (c1, SLICE, SLICE, SLICE, 1),
        (y2, 0, HALF, x + hi, 1), (z2, 0, HALF, x + ho, 1),
        (c2, HALF, HALF, xc + hi, 1), (c2, 2 * HALF, HALF, xc + ho, 1),
    ]


def piece_copies(refs, dst, sem, p, src_cols, dst_col, base=0):
    lo, n = src_cols
    return [
        pltpu.make_async_copy(
            src.at[pl.ds(at, rows), pl.ds(lo, n)],
            dst.at[pl.ds(pl.multiple_of(row, 16), rows), pl.ds(dst_col(j), n)],
            sem.at[base + i],
        )
        for i, (src, at, rows, row, j) in enumerate(piece_plan(refs, p))
    ]


def half_copies(refs, dst, sem, p, j, src_cols, base=0):
    lo, n = src_cols
    return [
        pltpu.make_async_copy(
            src.at[pl.ds(at, rows), pl.ds(lo, n)], dst.at[pl.ds(pl.multiple_of(row, 16), rows), :], sem.at[base + i]
        )
        for i, (src, at, rows, row, _) in enumerate([a for a in piece_plan(refs, p) if a[4] == j])
    ]


def gathered_copies(ref, dst, sem):
    r = lax.axis_index("row")
    n = ref.shape[2]
    return [
        pltpu.make_async_copy(
            ref.at[(r ^ k) * 2 + j], dst.at[pl.ds(k * SLICE, SLICE), pl.ds(j * n, n)], sem.at[k * 2 + j]
        )
        for k in range(4)
        for j in range(2)
    ]


def norm_cols(resid):
    center = jnp.sum(resid, axis=0, keepdims=True) * (1.0 / D)
    spread = jnp.sum(resid * resid, axis=0, keepdims=True) * (1.0 / D) - center * center
    inv = lax.rsqrt(spread + EPS)
    return (resid - center) * inv, inv


def norm_back_cols(y, hat, inv, g):
    t = y * g
    m1 = jnp.sum(t, axis=0, keepdims=True) * (1.0 / D)
    m2 = jnp.sum(t * hat, axis=0, keepdims=True) * (1.0 / D)
    return inv * (t - m1 - hat * m2)


def probs_group(qs, ks, ok):
    ss = [dot(k, q, TN) for q, k in zip(qs, ks)]
    ss = [jnp.where(ok, s * HEAD_DIM**-0.5, NEG) for s in ss]
    ms = [jnp.max(s, axis=0, keepdims=True) for s in ss]
    es = [jnp.exp(s - m) for s, m in zip(ss, ms)]
    ts = [1.0 / jnp.sum(e, axis=0, keepdims=True) for e in es]
    return [e * t for e, t in zip(es, ts)]


def key_ok_of(scal, b, tile):
    pos = lax.broadcasted_iota(jnp.int32, (SEG, SEG), 0)
    at = scal[2] + pl.program_id(0) * tile + b * SEG
    return (pos + at < scal[1]) | (pos == 0)


def put_cls(tile, hat, inv, hatc_o, invc_o):
    n = tile // SEG
    for b in range(n):
        at = pl.ds(pl.program_id(0) * n + b, 1)
        hatc_o[at, :] = hat[:, b * SEG : (b + 1) * SEG].T[0:1, :]
        invc_o[at, :] = jnp.broadcast_to(inv[:, b * SEG : b * SEG + 1], (1, SEG))


def attn_fwd_kernel(tile, lengths, xs, g1, b1, *rest):
    refs = rest[:8]
    proj_o, mix_o, hat_o, inv_o, low_o, hatc_o, invc_o, w, wo, sem = rest[8:]
    scal = scalars(lengths, tile * pl.num_programs(0))
    n_q = w.shape[1] // 2
    n_o = wo.shape[1] // 2

    @pl.when(pl.program_id(0) == 0)
    def _():
        cps = piece_copies(refs, w, sem, scal[0], (0, n_q), lambda j: j * n_q)
        cps += piece_copies(refs, wo, sem, scal[0], (n_q, n_o), lambda j: j * n_o, 12)
        for c in cps:
            c.start()
        for c in cps:
            c.wait()

    x = jnp.concatenate(rel_rows(xs), axis=0)
    proj_o[...] = dot(w[...], x, TN).astype(bf16)
    for b in range(tile // SEG):
        ok = key_ok_of(scal, b, tile)
        cols = slice(b * SEG, (b + 1) * SEG)
        for h0 in range(0, D // HEAD_DIM, GROUP):
            qkv = [
                [
                    proj_o[(h * 3 + j) * HEAD_DIM : (h * 3 + j + 1) * HEAD_DIM, cols]
                    for j in range(3)
                ]
                for h in range(h0, h0 + GROUP)
            ]
            pts = probs_group([a[0] for a in qkv], [a[1] for a in qkv], ok)
            mixed = [dot(a[2], p.astype(bf16), NN).astype(bf16) for a, p in zip(qkv, pts)]
            mix_o[h0 * HEAD_DIM : (h0 + GROUP) * HEAD_DIM, cols] = jnp.concatenate(mixed, axis=0)
    hat, inv = norm_cols(x.astype(f32) + dot(wo[...], mix_o[...], NN))
    hat_o[...] = hat
    inv_o[...] = inv
    low_o[...] = (hat * g1[...] + b1[...]).astype(bf16)
    put_cls(tile, hat, inv, hatc_o, invc_o)


def attn_fwd(lengths, xs, g1, b1, parts, tile=256):
    t = xs.shape[1]
    n = parts[0].shape[1]
    n_q = n * 3 // 4
    n_o = n - n_q
    colb = lambda rows: pl.BlockSpec((rows, tile), lambda i: (0, i))
    return pl.pallas_call(
        functools.partial(attn_fwd_kernel, tile),
        grid=(t // tile,),
        in_specs=[SMEM, colb(D)] + [whole((D, 1))] * 2 + [ANY] * 8,
        out_specs=[colb(2 * n_q), colb(D), colb(D), colb(1), colb(D), whole((t // SEG, D)), whole((t // SEG, SEG))],
        out_shape=[
            jax.ShapeDtypeStruct((2 * n_q, t), bf16),
            jax.ShapeDtypeStruct((D, t), bf16),
            jax.ShapeDtypeStruct((D, t), f32),
            jax.ShapeDtypeStruct((1, t), f32),
            jax.ShapeDtypeStruct((D, t), bf16),
            jax.ShapeDtypeStruct((t // SEG, D), f32),
            jax.ShapeDtypeStruct((t // SEG, SEG), f32),
        ],
        scratch_shapes=[
            pltpu.VMEM((D, 2 * n_q), bf16),
            pltpu.VMEM((D, 2 * n_o), bf16),
            pltpu.SemaphoreType.DMA((24,)),
        ],
        compiler_params=params(),
        name="seg_attend",
        cost_estimate=cost(2 * t * D * D * 4 + 4 * t * SEG * D, 20 * 1024 * t, t * SEG * 12),
    )(lengths, xs, g1, b1, *parts)


def ffn_up_kernel(low, wg, act_o, slope_o, w, lt, sem):
    i = pl.program_id(0)

    @pl.when(i == 0)
    def _():
        cps = gathered_copies(wg, w, sem)
        for c in cps:
            c.start()
        lt[...] = low[...].T
        for c in cps:
            c.wait()

    wid = act_o.shape[1]
    at = pl.multiple_of(i * wid, 128)
    hidden = dot(lt[...], w[:, pl.ds(at, wid)], NN)
    phi = 0.5 * (1.0 + lax.erf(hidden * ROOT_HALF))
    act_o[...] = (hidden * phi).astype(bf16)
    slope = phi + hidden * jnp.exp(-0.5 * hidden * hidden) * INV_ROOT_TAU
    slope_o[...] = slope.astype(bf16)


def ffn_up(low, wg, wid=512):
    t = low.shape[1]
    n = wg.shape[2] * 2
    colb = pl.BlockSpec((t, wid), lambda i: (0, i))
    return pl.pallas_call(
        ffn_up_kernel,
        grid=(n // wid,),
        in_specs=[whole((D, t)), ANY],
        out_specs=[colb, colb],
        out_shape=[jax.ShapeDtypeStruct((t, n), bf16)] * 2,
        scratch_shapes=[pltpu.VMEM((D, n), bf16), pltpu.VMEM((t, D), bf16), pltpu.SemaphoreType.DMA((12,))],
        compiler_params=params(),
        name="seg_up",
        cost_estimate=cost(2 * t * D * n, 4 * t * n, 2 * t * n),
    )(low, wg)


def ffn_down_kernel(tile, act, hat1, g1, b1, g2, b2, wg, hat_o, inv_o, hatc_o, invc_o, w, sem):
    i = pl.program_id(0)

    @pl.when(i == 0)
    def _():
        cps = gathered_copies(wg, w, sem)
        for c in cps:
            c.start()
        for c in cps:
            c.wait()

    first = hat1[...] * g1[...] + b1[...]
    hat, inv = norm_cols(first + dot(w[...], act[...], NT))
    hat_o[...] = hat
    inv_o[...] = inv
    put_cls(tile, hat, inv, hatc_o, invc_o)


def ffn_down(act, hat1, g1, b1, g2, b2, wg, tile=256):
    t, n = act.shape
    colb = lambda rows: pl.BlockSpec((rows, tile), lambda i: (0, i))
    return pl.pallas_call(
        functools.partial(ffn_down_kernel, tile),
        grid=(t // tile,),
        in_specs=[pl.BlockSpec((tile, n), lambda i: (i, 0)), colb(D)] + [whole((D, 1))] * 4 + [ANY],
        out_specs=[colb(D), colb(1), whole((t // SEG, D)), whole((t // SEG, SEG))],
        out_shape=[
            jax.ShapeDtypeStruct((D, t), f32),
            jax.ShapeDtypeStruct((1, t), f32),
            jax.ShapeDtypeStruct((t // SEG, D), f32),
            jax.ShapeDtypeStruct((t // SEG, SEG), f32),
        ],
        scratch_shapes=[pltpu.VMEM((D, n), bf16), pltpu.SemaphoreType.DMA((12,))],
        compiler_params=params(),
        name="seg_down",
        cost_estimate=cost(2 * t * D * n, 2 * t * n + 8 * t * D, 0),
    )(act, hat1, g1, b1, g2, b2, wg)


def start_all(cps):
    for c in cps:
        c.start()


def wait_all(cps):
    for c in cps:
        c.wait()


def ffn_back_kernel(tile, lengths, hat2, inv2, xs, slope, g2, b2, wg, d2_o, d2low_o, dhid_o, sums_o, sq_o, wd, acc, sem):
    scal = scalars(lengths, tile * pl.num_programs(0))
    i = pl.program_id(0)
    cd = gathered_copies(wg, wd, sem)

    @pl.when(i == 0)
    def _():
        start_all(cd)
        acc[...] = jnp.zeros_like(acc)
        sq_o[...] = jnp.zeros_like(sq_o)

    lane = lax.broadcasted_iota(jnp.int32, (1, tile), 1) + i * tile
    keep = (lane + scal[2] < scal[1]) & (lane % SEG != 0)
    h2 = hat2[...]
    teach = jnp.concatenate(rel_rows(xs), axis=0).astype(f32)
    diff = jnp.where(keep, h2 * g2[...] + b2[...] - teach, 0.0)
    sq_o[...] += jnp.sum(diff * diff, axis=0, keepdims=True)
    y = (diff * scale_of(lengths)).astype(bf16).astype(f32)
    acc[0] += fold_lanes(y * h2)
    acc[1] += fold_lanes(y)
    d2 = norm_back_cols(y, h2, inv2[...], g2[...])
    d2_o[...] = d2
    d2_low = d2.astype(bf16)
    d2low_o[...] = d2_low

    @pl.when(i == 0)
    def _():
        wait_all(cd)

    dhid_o[...] = (dot(d2_low, wd[...], TN) * slope[...].astype(f32)).astype(bf16)
    lane_sums(acc, sums_o)


def fold_lanes(v):
    return sum(v[:, k * SEG : (k + 1) * SEG] for k in range(v.shape[1] // SEG))


def lane_sums(acc, sums_o):
    @pl.when(pl.program_id(0) == pl.num_programs(0) - 1)
    def _():
        for k in range(2):
            sums_o[k : k + 1, :] = jnp.sum(acc[k].T, axis=0, keepdims=True)


def ffn_back(lengths, hat2, inv2, teach, slope, g2, b2, wg, tile=256):
    t, n = slope.shape
    colb = lambda rows: pl.BlockSpec((rows, tile), lambda i: (0, i))
    rowb = pl.BlockSpec((tile, n), lambda i: (i, 0))
    return pl.pallas_call(
        functools.partial(ffn_back_kernel, tile),
        grid=(t // tile,),
        in_specs=[SMEM, colb(D), colb(1), colb(D), rowb] + [whole((D, 1))] * 2 + [ANY],
        out_specs=[colb(D), colb(D), rowb, whole((2, D)), whole((1, tile))],
        out_shape=[
            jax.ShapeDtypeStruct((D, t), f32),
            jax.ShapeDtypeStruct((D, t), bf16),
            jax.ShapeDtypeStruct((t, n), bf16),
            jax.ShapeDtypeStruct((2, D), f32),
            jax.ShapeDtypeStruct((1, tile), f32),
        ],
        scratch_shapes=[
            pltpu.VMEM((D, n), bf16),
            pltpu.VMEM((2, D, SEG), f32),
            pltpu.SemaphoreType.DMA((12,)),
        ],
        compiler_params=params(),
        name="seg_down_back",
        cost_estimate=cost(2 * t * D * n, 6 * t * n),
    )(lengths, hat2, inv2, teach, slope, g2, b2, wg)


def up_back_kernel(tile, d2, dhid, hat1, inv1, g1, wg, d1_o, sums_o, wu, acc, sem):
    i = pl.program_id(0)

    @pl.when(i == 0)
    def _():
        cu = gathered_copies(wg, wu, sem)
        start_all(cu)
        acc[...] = jnp.zeros_like(acc)
        wait_all(cu)

    s = d2[...] + dot(wu[...], dhid[...], NT)
    h1 = hat1[...]
    acc[0] += fold_lanes(s * h1)
    acc[1] += fold_lanes(s)
    d1_o[...] = norm_back_cols(s, h1, inv1[...], g1[...])
    lane_sums(acc, sums_o)


def up_back(d2, dhid, hat1, inv1, g1, wg, tile=256):
    t, n = dhid.shape
    colb = lambda rows: pl.BlockSpec((rows, tile), lambda i: (0, i))
    return pl.pallas_call(
        functools.partial(up_back_kernel, tile),
        grid=(t // tile,),
        in_specs=[colb(D), pl.BlockSpec((tile, n), lambda i: (i, 0)), colb(D), colb(1), whole((D, 1)), ANY],
        out_specs=[colb(D), whole((2, D))],
        out_shape=[jax.ShapeDtypeStruct((D, t), f32), jax.ShapeDtypeStruct((2, D), f32)],
        scratch_shapes=[
            pltpu.VMEM((D, n), bf16),
            pltpu.VMEM((2, D, SEG), f32),
            pltpu.SemaphoreType.DMA((12,)),
        ],
        compiler_params=params(),
        name="seg_up_back",
        cost_estimate=cost(2 * t * D * n, 4 * t * n),
    )(d2, dhid, hat1, inv1, g1, wg)


def norm_back_rows(y, hat, inv, g):
    t = y * g
    m1 = jnp.sum(t, axis=1, keepdims=True) * (1.0 / D)
    m2 = jnp.sum(t * hat, axis=1, keepdims=True) * (1.0 / D)
    return inv * (t - m1 - hat * m2)


def col_of(rows, k):
    n = rows.shape[0]
    pick = lax.broadcasted_iota(jnp.int32, (n, 1), 0) == k
    row = jnp.sum(jnp.where(pick, rows, 0.0), axis=0, keepdims=True)
    return jnp.broadcast_to(row, (SEG, rows.shape[1])).T


def put_rows(a, cls, tile):
    n = tile // SEG
    lane0 = lax.broadcasted_iota(jnp.int32, (1, SEG), 1) == 0
    return jnp.concatenate(
        [
            jnp.where(lane0, col_of(cls[...], pl.program_id(0) * n + b), a[:, b * SEG : (b + 1) * SEG])
            for b in range(n)
        ],
        axis=1,
    )


def attn_back_kernel(tile, j, lengths, proj, d1, cls, *rest):
    scal = scalars(lengths, tile * pl.num_programs(0))
    refs = rest[:8]
    outs, (w, wo, sem) = rest[8:-3], rest[-3:]
    dproj_o = outs[0]
    i = pl.program_id(0)
    n_q, n_o = w.shape[1], wo.shape[1]
    cq = half_copies(refs, w, sem, scal[0], j, (0, n_q))

    @pl.when(i == 0)
    def _():
        co = half_copies(refs, wo, sem, scal[0], j, (n_q, n_o), 6)
        start_all(co)
        start_all(cq)
        wait_all(co)

    d1_all = put_rows(d1[...], cls, tile) if j == 1 else d1[...]
    d1_low = cls[...] if j == 0 else d1_all.astype(bf16)
    dmix = dot(wo[...], d1_low, TN).astype(bf16)
    for b in range(tile // SEG):
        ok = key_ok_of(scal, b, tile)
        cols = slice(b * SEG, (b + 1) * SEG)
        for h0 in range(0, n_o // HEAD_DIM, GROUP_BACK):
            hs = range(h0, h0 + GROUP_BACK)
            part = lambda k: [proj[(h * 3 + k) * HEAD_DIM : (h * 3 + k + 1) * HEAD_DIM, cols] for h in hs]
            qs, ks, vs = part(0), part(1), part(2)
            dms = [dmix[h * HEAD_DIM : (h + 1) * HEAD_DIM, cols] for h in hs]
            ps = probs_group(qs, ks, ok)
            dps = [dot(v, dm, TN) for v, dm in zip(vs, dms)]
            dvs = [dot(dm, p.astype(bf16), NT) for dm, p in zip(dms, ps)]
            inner = [jnp.sum(p * dp, axis=0, keepdims=True) for p, dp in zip(ps, dps)]
            dss = [(p * (dp - a)).astype(bf16) for p, dp, a in zip(ps, dps, inner)]
            dqs = [dot(k, ds, NN) * HEAD_DIM**-0.5 for k, ds in zip(ks, dss)]
            dks = [dot(q, ds, NT) * HEAD_DIM**-0.5 for q, ds in zip(qs, dss)]
            out = [a.astype(bf16) for trio in zip(dqs, dks, dvs) for a in trio]
            dproj_o[h0 * 3 * HEAD_DIM : (h0 + GROUP_BACK) * 3 * HEAD_DIM, cols] = jnp.concatenate(out, axis=0)

    @pl.when(i == 0)
    def _():
        wait_all(cq)

    dx = d1_all + dot(w[...], dproj_o[...], NN)
    if j == 1:
        outs[1][...] = d1_low
        outs[2][...] = dx
    else:
        put_rel_rows(outs[1], dx.astype(bf16))


def attn_back(j, lengths, proj, d1, cls, parts, tile=256):
    t = proj.shape[1]
    n = parts[0].shape[1]
    n_q = n * 3 // 4
    n_o = n - n_q
    colb = lambda rows, k=0: pl.BlockSpec((rows, tile), lambda i: (k, i))
    wide = [((D, t), bf16, D), ((D, t), f32, D)] if j == 1 else [((D, t), bf16, D)]
    return pl.pallas_call(
        functools.partial(attn_back_kernel, tile, j),
        grid=(t // tile,),
        in_specs=[SMEM, colb(n_q, j), colb(D), whole(cls.shape) if j == 1 else colb(D)] + [ANY] * 8,
        out_specs=[colb(n_q)] + [colb(a[2]) for a in wide],
        out_shape=[jax.ShapeDtypeStruct((n_q, t), bf16)] + [jax.ShapeDtypeStruct(a[0], a[1]) for a in wide],
        scratch_shapes=[
            pltpu.VMEM((D, n_q), bf16),
            pltpu.VMEM((D, n_o), bf16),
            pltpu.SemaphoreType.DMA((16,)),
        ],
        compiler_params=params(),
        name="seg_attend_back",
        cost_estimate=cost(t * D * D * 4 + 6 * t * SEG * D, 10 * 1024 * t, t * SEG * 6),
    )(lengths, proj, d1, cls, *parts)


def split_rows(g, keep_o, send_o):
    keep_o[:SLICE, :] = g[:SLICE]
    send_o[:SLICE, :] = g[SLICE : 2 * SLICE]
    keep_o[SLICE:, :] = g[2 * SLICE : 3 * SLICE]
    send_o[SLICE:, :] = g[3 * SLICE :]


def grad_kernel(a, b, o):
    r = lax.axis_index("row")
    g = dot(a[...], b[...], NN).astype(bf16)
    for k in range(4):
        o[r ^ k, 0] = g[k * SLICE : (k + 1) * SLICE]


def weight_grad(a, b, wid=512):
    t, n = b.shape
    q = n // 2 // wid
    return pl.pallas_call(
        grad_kernel,
        grid=(n // wid,),
        in_specs=[whole((D, t)), pl.BlockSpec((t, wid), lambda i: (0, i))],
        out_specs=pl.BlockSpec((4, 1, SLICE, wid), lambda i: (0, i // q, 0, i % q)),
        out_shape=jax.ShapeDtypeStruct((4, 2, SLICE, n // 2), bf16),
        compiler_params=params(),
        name="weight_grad",
        cost_estimate=cost(2 * t * D * n, 2 * (t + D) * n, 0),
    )(a, b)


def attn_grad_kernel(steps_q, xs, low, dproj, mix, keep_o, send_o):
    i = pl.program_id(0)

    @pl.when(i < steps_q)
    def _():
        x = jnp.concatenate(rel_rows(xs), axis=0)
        split_rows(dot(x, dproj[...], NT).astype(bf16), keep_o, send_o)

    @pl.when(i == steps_q)
    def _():
        split_rows(dot(low[...], mix[...], NT).astype(bf16), keep_o, send_o)


def attn_grad(j, xs, low, dproj, mix):
    t = low.shape[1]
    n_q, n_o = dproj.shape[0], mix.shape[0] // 2
    wid = n_o
    q = n_q // wid
    out = pl.BlockSpec((2 * SLICE, wid), lambda i: (0, i))
    return pl.pallas_call(
        functools.partial(attn_grad_kernel, q),
        grid=(q + 1,),
        in_specs=[whole((D, t)), whole((D, t)), pl.BlockSpec((wid, t), lambda i: (jnp.minimum(i, q - 1), 0)),
                  pl.BlockSpec((wid, t), lambda i: (j, 0))],
        out_specs=[out, out],
        out_shape=[jax.ShapeDtypeStruct((2 * SLICE, n_q + n_o), bf16)] * 2,
        compiler_params=params(),
        name="attend_weight_grad",
        cost_estimate=cost(t * D * 4 * D, (t + D) * 4 * D, 0),
    )(xs, low, dproj, mix)


def add4(refs):
    return sum(a[...].astype(f32) for a in refs)


def chip_kernel(k0, g0, k1, g1, o):
    here = (lax.axis_index("row") >> 1) * 2 + lax.axis_index("col")
    for jj, (k, g) in enumerate(((k0, g0), (k1, g1))):
        a = add4((k, g)).astype(bf16)
        for xx in range(2):
            at = pl.multiple_of((here ^ (xx * 2 + jj)) * SLICE, 16)
            o[pl.ds(at, SLICE), :] = a[xx * SLICE : (xx + 1) * SLICE]


def chip_sum(keep, got, wid=768):
    n = keep.shape[1] // 2
    k = n // wid
    lo = pl.BlockSpec((2 * SLICE, wid), lambda i: (0, i))
    hi = pl.BlockSpec((2 * SLICE, wid), lambda i: (0, i + k))
    return pl.pallas_call(
        chip_kernel,
        grid=(k,),
        in_specs=[lo, lo, hi, hi],
        out_specs=pl.BlockSpec((4 * SLICE, wid), lambda i: (0, i)),
        out_shape=jax.ShapeDtypeStruct((4 * SLICE, n), bf16),
        compiler_params=params(),
        name="chip_sum",
        cost_estimate=cost(0, 12 * SLICE * n),
    )(keep, got, keep, got)


def chip_half_kernel(k0, g0, a_o, b_o):
    a = add4((k0, g0)).astype(bf16)
    a_o[...] = a[:SLICE]
    b_o[...] = a[SLICE:]


def chip_half(keep, got, wid=768):
    n = keep.shape[1]
    lo = pl.BlockSpec((2 * SLICE, wid), lambda i: (0, i))
    return pl.pallas_call(
        chip_half_kernel,
        grid=(n // wid,),
        in_specs=[lo, lo],
        out_specs=[pl.BlockSpec((SLICE, wid), lambda i: (0, i))] * 2,
        out_shape=[jax.ShapeDtypeStruct((SLICE, n), bf16)] * 2,
        compiler_params=params(),
        name="chip_sum",
        cost_estimate=cost(0, 6 * SLICE * n),
    )(keep, got)


def add_stacked(refs):
    out = []
    for a in refs:
        for i in range(0, a.shape[0], SLICE):
            out.append(a[i : i + SLICE, :].astype(f32))
    return sum(out)


FEW = 8


def plane_kernel(*refs):
    parts, sums, outs, total_s = refs[:-6], refs[-6], refs[-5:-1], refs[-1]
    z = lax.axis_index("dp")
    h = outs[0].shape[0] - FEW
    total_s[...] = add_stacked(parts).astype(bf16)
    v = sums[...]
    n = v.shape[0] // FEW
    v = jnp.concatenate([v[n * i : n * (i + 1), :] for i in range(FEW)], axis=1)
    hi = v.astype(bf16)
    both = jnp.concatenate([hi.astype(f32), v - hi.astype(f32)], axis=0).astype(bf16)
    for k, o in enumerate(outs):
        o[:h, :] = total_s[pl.ds(pl.multiple_of((z ^ k) * h, 16), h), :]
        o[h:, :] = both


def plane_sum(sums, *parts):
    n = parts[0].shape[1]
    vm = pl.BlockSpec(memory_space=pltpu.VMEM)
    return pl.pallas_call(
        plane_kernel,
        in_specs=[vm] * (len(parts) + 1),
        out_specs=[vm] * 4,
        out_shape=[jax.ShapeDtypeStruct((SLICE // 4 + FEW, n), bf16)] * 4,
        scratch_shapes=[pltpu.VMEM((SLICE, n), bf16)],
        compiler_params=params(0),
        name="plane_sum",
        cost_estimate=cost(0, 10 * SLICE * n),
    )(*parts, sums)


def pair_split_kernel(a, fa, b, fb, o):
    va, vb = add4((a, fa)).astype(bf16), add4((b, fb)).astype(bf16)
    h = SLICE // 4
    for q in range(4):
        o[2 * q * h : (2 * q + 1) * h, :] = va[q * h : (q + 1) * h]
        o[(2 * q + 1) * h : (2 * q + 2) * h, :] = vb[q * h : (q + 1) * h]


def pair_sum_kernel(p, o):
    h = p.shape[0] // 4
    v = sum(p[q * h : (q + 1) * h, :].astype(f32) for q in range(4)).astype(bf16)
    for q in range(4):
        o[q * h : (q + 1) * h, :] = v


def pair_place_kernel(p, a_o, b_o):
    h = p.shape[0] // 8
    for q in range(4):
        a_o[q * h : (q + 1) * h, :] = p[2 * q * h : (2 * q + 1) * h, :].astype(f32)
        b_o[q * h : (q + 1) * h, :] = p[(2 * q + 1) * h : (2 * q + 2) * h, :].astype(f32)


def pair_call(kernel, args, rows, dtype, count, name):
    n = args[0].shape[1]
    wid = 512
    spec = lambda m: pl.BlockSpec((m, wid), lambda i: (0, i))
    return pl.pallas_call(
        kernel,
        grid=(n // wid,),
        in_specs=[spec(a.shape[0]) for a in args],
        out_specs=[spec(rows)] * count,
        out_shape=[jax.ShapeDtypeStruct((rows, n), dtype)] * count,
        compiler_params=params(),
        name=name,
        cost_estimate=cost(0, 8 * rows * n),
    )(*args)


def quarter_kernel(*refs):
    parts, q_o, small_o = refs[:-2], refs[-2], refs[-1]
    v = add4(parts)
    h = q_o.shape[0]
    q_o[...] = v[:h].astype(bf16)
    n = FEW // 2
    w = v[h : h + n] + v[h + n :]
    c = small_o.shape[1]
    for i in range(FEW):
        small_o[n * i : n * (i + 1), :] = w[:, c * i : c * (i + 1)]


def quarter_sum(*parts):
    vm = pl.BlockSpec(memory_space=pltpu.VMEM)
    h, n = parts[0].shape
    return pl.pallas_call(
        quarter_kernel,
        in_specs=[vm] * len(parts),
        out_specs=[vm] * 2,
        out_shape=[jax.ShapeDtypeStruct((h - FEW, n), bf16), jax.ShapeDtypeStruct((FEW * FEW // 2, n // FEW), f32)],
        compiler_params=params(0),
        name="quarter_sum",
        cost_estimate=cost(0, 1e6),
    )(*parts)


def place_kernel(cut, p0, p1, p2, p3, *outs):
    z = lax.axis_index("dp")
    h = p0.shape[0]
    for k, p in enumerate((p0, p1, p2, p3)):
        rows = pl.ds(pl.multiple_of((z ^ k) * h, 8), h)
        outs[0][rows, :] = p[:, :cut].astype(f32)
        if len(outs) > 1:
            outs[1][rows, :] = p[:, cut:].astype(f32)


def place_quarters(parts, cut):
    vm = pl.BlockSpec(memory_space=pltpu.VMEM)
    h, n = parts[0].shape
    shapes = [(4 * h, cut)] + ([(4 * h, n - cut)] if cut < n else [])
    return pl.pallas_call(
        functools.partial(place_kernel, cut),
        in_specs=[vm] * 4,
        out_specs=[vm] * len(shapes),
        out_shape=[jax.ShapeDtypeStruct(a, f32) for a in shapes],
        compiler_params=params(0),
        name="place_quarters",
        cost_estimate=cost(0, 2e6),
    )(*parts)


def output_kernel(tile, hat2, g2, b2, cls, o):
    put_rel_rows(o, put_rows(hat2[...] * g2[...] + b2[...], cls, tile).astype(bf16))


def emit_output(hat2, g2, b2, cls, tile=256):
    t = hat2.shape[1]
    colb = lambda rows: pl.BlockSpec((rows, tile), lambda i: (0, i))
    return pl.pallas_call(
        functools.partial(output_kernel, tile),
        grid=(t // tile,),
        in_specs=[colb(D)] + [whole((D, 1))] * 2 + [whole(cls.shape)],
        out_specs=colb(D),
        out_shape=jax.ShapeDtypeStruct((D, t), bf16),
        compiler_params=params(),
        name="emit_output",
        cost_estimate=cost(0, 6 * t * D),
    )(hat2, g2, b2, cls)
def cost(flops, nbytes, trans=0):
    return pl.CostEstimate(flops=int(flops * COST), bytes_accessed=int(nbytes * COST), transcendentals=int(trans * COST))


def vmcall(kernel, name, smem, vmem, anys, outs, scratch, c):
    vm = pl.BlockSpec(memory_space=pltpu.VMEM)
    return pl.pallas_call(
        kernel,
        in_specs=[SMEM] * len(smem) + [vm] * len(vmem) + [ANY] * len(anys),
        out_specs=[vm] * len(outs),
        out_shape=[jax.ShapeDtypeStruct(s, d) for s, d in outs],
        scratch_shapes=scratch,
        compiler_params=params(0),
        name=name,
        cost_estimate=c,
    )(*smem, *vmem, *anys)


def axes():
    r = lax.axis_index("row")
    return r, lax.axis_index("col"), lax.axis_index("dp")


def prep_kernel(qkv, proj, a_o, xa_o):
    p = lax.axis_index("dp") & 1
    n_q = qkv.shape[1]
    half = pl.ds(pl.multiple_of(p * HALF, 16), HALF)
    xa_o[:, :n_q] = qkv[half, :]
    xa_o[:, n_q:] = proj[half, :]
    a_o[:, :n_q] = qkv[...]
    a_o[:, n_q:] = proj[...]


def prep(qkv, proj):
    n = qkv.shape[1] + proj.shape[1]
    return vmcall(
        prep_kernel, "prep_weights", [], [qkv, proj], [], [((SLICE, n), bf16), ((HALF, n), bf16)], [], cost(0, 2e6),
    )


VEC = 32


def stack_kernel(x, *rest):
    vecs, o = rest[:-1], rest[-1]
    t = o.shape[1]
    rows = o.shape[0] // 4
    for q in range(4):
        o[q * rows : q * rows + SLICE, :] = x[:, q * t : (q + 1) * t]
    if vecs:
        v = jnp.concatenate([a[...].reshape(1, SLICE).astype(f32) for a in vecs[:-1]] + [vecs[-1][...].astype(f32)], axis=0)
        v = jnp.concatenate([v, jnp.zeros((VEC - v.shape[0], SLICE), f32)], axis=0).astype(bf16)
        for q in range(4):
            o[q * rows + SLICE : (q + 1) * rows, :SLICE] = v
            o[q * rows + SLICE : (q + 1) * rows, SLICE:] = jnp.zeros((VEC, t - SLICE), bf16)


def token_stack(x, *vecs):
    rows = SLICE + (VEC if vecs else 0)
    return vmcall(
        stack_kernel, "token_stack", [], [x, *vecs], [], [((4 * rows, x.shape[1] // 4), bf16)], [], cost(0, 3e6)
    )[0]


def join_kernel(p, o):
    t = p.shape[1]
    for q in range(4):
        o[:, q * t : (q + 1) * t] = p[q * SLICE : (q + 1) * SLICE, :]


def token_join(p):
    return vmcall(join_kernel, "token_join", [], [p], [], [((SLICE, 4 * p.shape[1]), bf16)], [], cost(0, 3e6))[0]


def cross_prep_kernel(qkv, proj, up, down, mine_o, give_o):
    c = lax.axis_index("row") & 1
    at = 0
    for w in (qkv, proj, up, down):
        q = w.shape[1] // 2
        a, b = w[:, :q].astype(f32), w[:, q:].astype(f32)
        mine_o[:, at : at + q] = jnp.where(c == 0, a, b).astype(bf16)
        give_o[:, at : at + q] = jnp.where(c == 0, b, a).astype(bf16)
        at += q


def cross_prep(qkv, proj, up, down):
    vm = pl.BlockSpec(memory_space=pltpu.VMEM)
    n = (qkv.shape[1] + proj.shape[1] + up.shape[1] + down.shape[1]) // 2
    return pl.pallas_call(
        cross_prep_kernel,
        in_specs=[vm] * 4,
        out_specs=[vm] * 2,
        out_shape=[jax.ShapeDtypeStruct((SLICE, n), bf16)] * 2,
        compiler_params=params(0),
        name="cross_prep",
        cost_estimate=cost(0, 4e6),
    )(qkv, proj, up, down)


def pick_kernel(mine, got, o):
    c, p = lax.axis_index("row") & 1, lax.axis_index("dp") & 1

    @pl.when(c == p)
    def _():
        o[...] = mine[...]

    @pl.when(c != p)
    def _():
        o[...] = got[...]


def cross_pick(mine, got):
    vm = pl.BlockSpec(memory_space=pltpu.VMEM)
    return pl.pallas_call(
        pick_kernel,
        in_specs=[vm] * 2,
        out_specs=vm,
        out_shape=jax.ShapeDtypeStruct(mine.shape, bf16),
        compiler_params=params(0),
        name="cross_pick",
        cost_estimate=cost(0, 3e6),
    )(mine, got)


def swap_cores(v):
    s = SLICE
    return jnp.concatenate([v[:, s : 2 * s], v[:, :s], v[:, 3 * s :], v[:, 2 * s : 3 * s]], axis=1)


def core_order(v):
    c = lax.axis_index("row") & 1
    return jnp.where(c == 0, v, swap_cores(v))


def vec_kernel(h, x_o, rel_o, abs_o, c0, c1, c2, c3):
    rows = h.shape[0] // 4
    for q in range(4):
        x_o[q * SLICE : (q + 1) * SLICE, :] = h[q * rows : q * rows + SLICE, :]
    r = lax.axis_index("row")
    part = [
        h[pl.ds(pl.multiple_of((r ^ k) * rows + SLICE, 16), VEC), :][:, : 2 * SEG].astype(f32)[:24, :SLICE] for k in range(4)
    ]
    rel = jnp.concatenate(part, axis=1)
    rel_o[...] = rel
    abs_o[...] = core_order(rel)
    cols = rel[:8].T
    for i, o in enumerate((c0, c1, c2, c3)):
        o[...] = cols[:, i : i + 1]


def unstack(h):
    n = 8 + SEGS
    return vmcall(
        vec_kernel, "unstack", [], [h], [],
        [((D, h.shape[1]), bf16)] + [((n, D), f32)] * 2 + [((D, 1), f32)] * 4, [], cost(0, 3e6),
    )


H2, H1, TE, IV = slice(0, D), slice(D, 2 * D), slice(2 * D, 3 * D), slice(3 * D, 3 * D + SEG)
MSG = 3 * D + SEG


def msg_kernel(hat2, inv2, hat1, teach, o):
    n = hat2.shape[0]
    o[:, H2] = core_order(hat2[...])
    o[:, H1] = core_order(hat1[...])
    o[:, IV] = inv2[...]
    rows = []
    parts = rel_rows(teach)
    for b in range(n):
        at = slice(b * SEG, (b + 1) * SEG)
        rows.append(jnp.concatenate([t[:, at].astype(f32).T[0:1, :] for t in parts], axis=1))
    o[:, TE] = core_order(jnp.concatenate(rows, axis=0))


def cls_message(hat2, inv2, hat1, teach):
    vm = pl.BlockSpec(memory_space=pltpu.VMEM)
    return pl.pallas_call(
        msg_kernel,
        in_specs=[vm] * 4,
        out_specs=vm,
        out_shape=jax.ShapeDtypeStruct((hat2.shape[0], MSG), f32),
        compiler_params=params(0),
        name="cls_message",
        cost_estimate=cost(0, 2e6),
    )(hat2, inv2, hat1, teach)


def pair_kernel(a, b, o):
    n = a.shape[0]
    c = lax.axis_index("row") & 1
    o[pl.ds(pl.multiple_of(c * n, 8), n), :] = a[...]
    o[pl.ds(pl.multiple_of((1 - c) * n, 8), n), :] = b[...]


def pair_rows(a, b):
    return vmcall(pair_kernel, "core_pair", [], [a, b], [], [((2 * a.shape[0], a.shape[1]), a.dtype)], [], cost(0, 1e6))[0]


def fold_kernel(a, b, o):
    o[...] = add4((a, b)).astype(o.dtype)


def fold(a, b):
    return vmcall(fold_kernel, "core_fold", [], [a, b], [], [(a.shape, a.dtype)], [], cost(0, 1e5))[0]


def cross_copies(refs, dst, sem, lo, n, base=0):
    c, p = lax.axis_index("row") & 1, lax.axis_index("dp") & 1
    at = [c * SLICE, (1 - c) * SLICE, 2 * SLICE + p * SLICE, 2 * SLICE + (1 - p) * SLICE]
    return [
        pltpu.make_async_copy(
            src.at[:, pl.ds(lo, n)], dst.at[pl.ds(pl.multiple_of(row, 16), SLICE), :], sem.at[base + i]
        )
        for i, (src, row) in enumerate(zip(refs, at))
    ]


def norm_rows(resid):
    center = jnp.sum(resid, axis=1, keepdims=True) * (1.0 / D)
    spread = jnp.sum(resid * resid, axis=1, keepdims=True) * (1.0 / D) - center * center
    inv = lax.rsqrt(spread + EPS)
    return (resid - center) * inv, inv


def total(parts):
    return sum(p[...].astype(f32) for p in parts)


def cls_rows(vec, m):
    pos = vec[8 : 8 + SEGS, :]
    return m[:, H2] * vec[2:3, :] + vec[3:4, :] + jnp.concatenate([pos] * (m.shape[0] // SEGS), axis=0)


def cross_probs(cproj, lens):
    n = cproj.shape[0]
    qi = lax.broadcasted_iota(jnp.int32, (n, n), 0)
    ki = lax.broadcasted_iota(jnp.int32, (n, n), 1)
    limit = jnp.where(ki < SEGS, lens[0], lens[1])
    ok = (qi // SEGS == ki // SEGS) & ((ki % SEGS) * SEG < limit)
    out = []
    for h in range(cproj.shape[1] // (3 * HEAD_DIM)):
        q, k, v = [cproj[:, (3 * h + j) * HEAD_DIM : (3 * h + j + 1) * HEAD_DIM] for j in range(3)]
        s = jnp.where(ok, dot(q, k, NT) * HEAD_DIM**-0.5, NEG)
        e = jnp.exp(s - jnp.max(s, axis=1, keepdims=True))
        out.append((q, k, v, e / jnp.sum(e, axis=1, keepdims=True)))
    return out


def group_lens(lengths, rows):
    r, _, z = axes()
    here = lax.axis_size("col")
    return [lengths[(z * here + j) * 2 + (r >> 1)] for j in range(2)]


def cross1_kernel(lengths, vec, m0, m1, *rest):
    refs = rest[:4]
    m_o, cproj_o, cmix_o, part_o, vlow_o, w, sem = rest[4:]
    _, y, _ = axes()
    n_q = cproj_o.shape[1]
    cps = cross_copies(refs, w, sem, 0, w.shape[1])
    start_all(cps)
    n = m0.shape[0]
    for m, yy in ((m0, y), (m1, 1 - y)):
        m_o[pl.ds(pl.multiple_of(yy * n, 8), n), :] = m[...]
    v_low = cls_rows(vec[...], m_o[...]).astype(bf16)
    vlow_o[...] = v_low
    wait_all(cps)
    cproj = dot(v_low, w[:, :n_q], NN).astype(bf16)
    cproj_o[...] = cproj
    mix = [dot(p.astype(bf16), v, NN) for _, _, v, p in cross_probs(cproj, group_lens(lengths, None))]
    mix = jnp.concatenate(mix, axis=1).astype(bf16)
    cmix_o[...] = mix
    part_o[...] = dot(mix, w[:, n_q:], NT).astype(bf16)


def cross1(lengths, vec, msgs, refs, n_q, n_o):
    n = 2 * msgs[0].shape[0]
    return vmcall(
        cross1_kernel, "cross_attend", [lengths], [vec, *msgs], refs,
        [((n, MSG), f32), ((n, n_q), bf16), ((n, n_o), bf16), ((n, D), bf16), ((n, D), bf16)],
        [pltpu.VMEM((D, n_q + n_o), bf16), pltpu.SemaphoreType.DMA((4,))],
        cost(2e7, 2e6),
    )


def cross2_kernel(vec, m, p0, p1, *rest):
    refs = rest[:4]
    hat_o, inv_o, low_o, act_o, slope_o, part_o, wu, wd, sem = rest[4:]
    n = wu.shape[1]
    lo = refs[0].shape[1] - 2 * n
    cps = cross_copies(refs, wu, sem, lo, n) + cross_copies(refs, wd, sem, lo + n, n, 4)
    start_all(cps)
    hat, inv = norm_rows(cls_rows(vec[...], m[...]) + total((p0, p1)))
    hat_o[...] = hat
    inv_o[...] = jnp.broadcast_to(inv, inv_o.shape)
    low = (hat * vec[4:5, :] + vec[5:6, :]).astype(bf16)
    low_o[...] = low
    wait_all(cps)
    hidden = dot(low, wu[...], NN)
    phi = 0.5 * (1.0 + lax.erf(hidden * ROOT_HALF))
    act = (hidden * phi).astype(bf16)
    act_o[...] = act
    slope_o[...] = phi + hidden * jnp.exp(-0.5 * hidden * hidden) * INV_ROOT_TAU
    part_o[...] = dot(act, wd[...], NT).astype(bf16)


def cross2(vec, m, parts, refs, n_u):
    n = m.shape[0]
    return vmcall(
        cross2_kernel, "cross_ffn", [], [vec, m, *parts], refs,
        [((n, D), f32), ((n, SEG), f32), ((n, D), bf16), ((n, n_u), bf16), ((n, n_u), f32), ((n, D), bf16)],
        [pltpu.VMEM((D, n_u), bf16)] * 2 + [pltpu.SemaphoreType.DMA((8,))],
        cost(2e7, 3e6),
    )


def own_rows(ref, n):
    r, y, _ = axes()
    return ref[pl.ds(pl.multiple_of((y * 2 + (r & 1)) * n, 8), n), :]


def cross3_kernel(lengths, vec, m, hat1, slope, p0, p1, *rest):
    refs = rest[:4]
    cls_o, sq_o, sums_o, d2_o, d2low_o, dhid_o, part_o, wu, wd, keep, sem = rest[4:]
    n = wu.shape[1]
    lo = refs[0].shape[1] - 2 * n
    cps = cross_copies(refs, wu, sem, lo, n) + cross_copies(refs, wd, sem, lo + n, n, 4)
    start_all(cps)
    first = hat1[...] * vec[4:5, :] + vec[5:6, :]
    hat2, inv2 = norm_rows(first + total((p0, p1)))
    out = hat2 * vec[6:7, :] + vec[7:8, :]
    rows = out.shape[0]
    ti = lax.broadcasted_iota(jnp.int32, (rows, 1), 0)
    lens = group_lens(lengths, rows)
    live = (ti % SEGS) * SEG < jnp.where(ti < SEGS, lens[0], lens[1])
    diff = jnp.where(live, out - m[:, TE], 0.0)
    k = cls_o.shape[0]
    keep[...] = out
    cls_o[...] = core_order(own_rows(keep, k))
    keep[...] = diff
    mine = own_rows(keep, k)
    sq_o[...] = jnp.sum(mine * mine, axis=0, keepdims=True)
    yv = diff * scale_of(lengths)
    sums_o[0:1, :] = jnp.sum(yv * hat2, axis=0, keepdims=True)
    sums_o[1:2, :] = jnp.sum(yv, axis=0, keepdims=True)
    d2 = norm_back_rows(yv, hat2, inv2, vec[6:7, :])
    d2_o[...] = d2
    d2_low = d2.astype(bf16)
    d2low_o[...] = d2_low
    wait_all(cps)
    dhid = (dot(d2_low, wd[...], NN) * slope[...]).astype(bf16)
    dhid_o[...] = dhid
    part_o[...] = dot(dhid, wu[...], NT).astype(bf16)


def cross3(lengths, vec, m, hat1, slope, parts, refs):
    n, n_u = slope.shape
    return vmcall(
        cross3_kernel, "cross_ffn_back", [lengths], [vec, m, hat1, slope, *parts], refs,
        [((n // 4, D), f32), ((1, D), f32), ((2, D), f32), ((n, D), f32), ((n, D), bf16), ((n, n_u), bf16), ((n, D), bf16)],
        [pltpu.VMEM((D, n_u), bf16)] * 2 + [pltpu.VMEM((n, D), f32), pltpu.SemaphoreType.DMA((8,))],
        cost(2e7, 3e6),
    )


def cross4_kernel(lengths, vec, d2, hat1, inv1, cproj, p0, p1, *rest):
    refs = rest[:4]
    d1_o, d1low_o, sums_o, dproj_o, part_o, w, sem = rest[4:]
    n_q = dproj_o.shape[1]
    cps = cross_copies(refs, w, sem, 0, w.shape[1])
    start_all(cps)
    s = d2[...] + total((p0, p1))
    h1 = hat1[...]
    sums_o[0:1, :] = jnp.sum(s * h1, axis=0, keepdims=True)
    sums_o[1:2, :] = jnp.sum(s, axis=0, keepdims=True)
    d1 = norm_back_rows(s, h1, inv1[:, 0:1], vec[4:5, :])
    d1_o[...] = d1
    d1_low = d1.astype(bf16)
    d1low_o[...] = d1_low
    wait_all(cps)
    dmix = dot(d1_low, w[:, n_q:], NN).astype(bf16)
    outs = []
    for h, (q, k, v, p) in enumerate(cross_probs(cproj[...], group_lens(lengths, None))):
        dm = dmix[:, h * HEAD_DIM : (h + 1) * HEAD_DIM]
        dv = dot(p.astype(bf16), dm, TN)
        dp = dot(dm, v, NT)
        ds = (p * (dp - jnp.sum(p * dp, axis=1, keepdims=True))).astype(bf16)
        outs += [dot(ds, k, NN) * HEAD_DIM**-0.5, dot(ds, q, TN) * HEAD_DIM**-0.5, dv]
    dproj = jnp.concatenate(outs, axis=1).astype(bf16)
    dproj_o[...] = dproj
    part_o[...] = dot(dproj, w[:, :n_q], NT).astype(bf16)


def cross4(lengths, vec, d2, hat1, inv1, cproj, parts, refs, n_o):
    n, n_q = cproj.shape
    return vmcall(
        cross4_kernel, "cross_attend_back", [lengths], [vec, d2, hat1, inv1, cproj, *parts], refs,
        [((n, D), f32), ((n, D), bf16), ((2, D), f32), ((n, n_q), bf16), ((n, D), bf16)],
        [pltpu.VMEM((D, n_q + n_o), bf16), pltpu.SemaphoreType.DMA((4,))],
        cost(2e7, 2e6),
    )


def quarter_copies(ref, dst, sem, base=0):
    r, y, _ = axes()
    n = dst.shape[1]
    cols = pl.ds(pl.multiple_of((r & 1) * n, 128), n)
    return [
        pltpu.make_async_copy(
            ref.at[(((r >> 1) ^ (s >> 1)) * 2 + (s & 1)) * 2 + y, :, cols],
            dst.at[pl.ds(s * SLICE, SLICE), :],
            sem.at[base + s],
        )
        for s in range(4)
    ]


def cross5_kernel(vec, m, d1, p0, p1, *rest):
    ups, downs, pos_o, sums_o, d2_o, d2low_o, low_o, act_o, dhid_o, part_o, wu, wd, sem = rest
    cps = quarter_copies(ups, wu, sem) + quarter_copies(downs, wd, sem, 4)
    start_all(cps)
    dcls = d1[...] + total((p0, p1))
    pos_o[...] = sum(dcls[i : i + SEGS] for i in range(0, dcls.shape[0], SEGS))
    yv = dcls.astype(bf16).astype(f32)
    h2 = m[:, H2]
    sums_o[0:1, :] = jnp.sum(yv * h2, axis=0, keepdims=True)
    sums_o[1:2, :] = jnp.sum(yv, axis=0, keepdims=True)
    d2 = norm_back_rows(yv, h2, m[:, 3 * D : 3 * D + 1], vec[2:3, :])
    d2_o[...] = d2
    d2_low = d2.astype(bf16)
    d2low_o[...] = d2_low
    low = (m[:, H1] * vec[0:1, :] + vec[1:2, :]).astype(bf16)
    low_o[...] = low
    wait_all(cps)
    hidden = dot(low, wu[...], NN)
    phi = 0.5 * (1.0 + lax.erf(hidden * ROOT_HALF))
    act_o[...] = (hidden * phi).astype(bf16)
    slope = phi + hidden * jnp.exp(-0.5 * hidden * hidden) * INV_ROOT_TAU
    dhid = (dot(d2_low, wd[...], NN) * slope).astype(bf16)
    dhid_o[...] = dhid
    part_o[...] = dot(dhid, wu[...], NT).astype(bf16)


def cross5(vec, m, d1, parts, ups, downs):
    n = m.shape[0]
    n_u = ups.shape[2] // 2
    return vmcall(
        cross5_kernel, "cls_ffn_back", [], [vec, m, d1, *parts], [ups, downs],
        [((SEGS, D), f32), ((2, D), f32), ((n, D), f32), ((n, D), bf16), ((n, D), bf16), ((n, n_u), bf16),
         ((n, n_u), bf16), ((n, D), bf16)],
        [pltpu.VMEM((D, n_u), bf16)] * 2 + [pltpu.SemaphoreType.DMA((12,))],
        cost(3e7, 3e6),
    )


def cross6_kernel(vec, m, d2, inv1, p0, p1, d1_o, sums_o, keep):
    s = d2[...] + total((p0, p1))
    h1 = m[:, H1]
    sums_o[0:1, :] = jnp.sum(s * h1, axis=0, keepdims=True)
    sums_o[1:2, :] = jnp.sum(s, axis=0, keepdims=True)
    n = d1_o.shape[0]
    keep[...] = s
    mine = own_rows(keep, n)
    keep[...] = h1
    d1_o[...] = core_order(norm_back_rows(mine, own_rows(keep, n), inv1[:, 0:1], vec[0:1, :]))


def cross6(vec, m, d2, inv1, parts):
    n = m.shape[0]
    return vmcall(
        cross6_kernel, "cls_norm_back", [], [vec, m, d2, inv1, *parts], [],
        [((n // 4, D), f32), ((2, D), f32)], [pltpu.VMEM((n, D), f32)], cost(0, 1e6),
    )


def pack_kernel(count, *refs):
    wides, narrows, (own_o, far_o) = refs[:count], refs[count:-2], refs[-2:]
    c = lax.axis_index("row") & 1
    at = 0
    for w in wides:
        v = w[...].astype(f32)
        s = [v[:, i * SLICE : (i + 1) * SLICE] for i in range(4)]
        own_o[:, at : at + SLICE] = jnp.where(c == 0, s[0], s[1]).astype(bf16)
        far_o[:, at : at + SLICE] = jnp.where(c == 0, s[2], s[3]).astype(bf16)
        at += SLICE
    for w in narrows:
        v = w[...]
        own_o[:, at : at + v.shape[1]] = v
        far_o[:, at : at + v.shape[1]] = v
        at += v.shape[1]


def pack_acts(wides, narrows):
    n = wides[0].shape[0]
    width = len(wides) * SLICE + sum(a.shape[1] for a in narrows)
    return vmcall(
        functools.partial(pack_kernel, len(wides)), "pack_factors", [], [*wides, *narrows], [],
        [((n, width), bf16)] * 2, [], cost(0, 2e6),
    )


def join_rows_kernel(*refs):
    o, at = refs[-1], 0
    for a in refs[:-1]:
        o[at : at + a.shape[0], :] = a[...]
        at += a.shape[0]


def join_rows(*parts):
    rows = sum(a.shape[0] for a in parts)
    return vmcall(join_rows_kernel, "join_rows", [], parts, [], [((rows, parts[0].shape[1]), bf16)], [], cost(0, 1e6))[0]


def factor_kernel(widths, mine, theirs, *outs):
    c = lax.axis_index("row") & 1
    at = len(widths) * SLICE
    for i, (w, o) in enumerate(zip(widths, outs)):
        wide = mine[:, i * SLICE : (i + 1) * SLICE]
        got = [dot(wide, b[:, at : at + w], TN) for b in (mine, theirs)]
        o[:, :w] = jnp.where(c == 0, got[0], got[1])
        o[:, w:] = jnp.where(c == 0, got[1], got[0])
        at += w


def factor_grads(mine, theirs, widths):
    return vmcall(
        functools.partial(factor_kernel, widths), "factor_grads", [], [mine, theirs], [],
        [((SLICE, 2 * w), f32) for w in widths], [], cost(1e9, 8e6),
    )


def add_kernel(a, b, o):
    o[...] = a[...] + b[...]


def add_rows(a, b):
    return vmcall(add_kernel, "add_sums", [], [a, b], [], [(a.shape, f32)], [], cost(0, 1e5))[0]


def small_kernel(sb, sa, gb, ga, cb, ca, pos, sq, csq, o):
    r, y, _ = axes()
    one = jnp.where((r & 1) + y == 0, 1.0, 0.0)
    rel = jnp.concatenate([sb[...], sa[...]], axis=0)
    total = jnp.sum(sq[...], axis=1, keepdims=True) + jnp.sum(csq[...], axis=1, keepdims=True)
    seg = core_order(rel) + one * jnp.concatenate([gb[...], ga[...]], axis=0)
    rows = jnp.concatenate(
        [seg, one * jnp.concatenate([cb[...], ca[...]], axis=0), jnp.broadcast_to(total, (1, D)), one * pos[...]], axis=0
    )
    h = 2 * SLICE
    o[:25, :] = jnp.where(r >> 1 == 0, rows, jnp.concatenate([rows[:, h:], rows[:, :h]], axis=1))
    o[25:, :] = jnp.zeros((7, D), f32)


def small_sums(*parts):
    return vmcall(small_kernel, "small_sums", [], parts, [], [((32, D), f32)], [], cost(0, 1e5))[0]


def own_kernel(a, o):
    r = lax.axis_index("row")
    v = a[...]
    o[...] = sum(jnp.where(r == q, v[:, q * SLICE : (q + 1) * SLICE], 0.0) for q in range(4))


def own_sums(a):
    return vmcall(own_kernel, "own_sums", [], [a], [], [((32, SLICE), f32)], [], cost(0, 1e5))[0]


def row_swap(k):
    def move(a):
        return lax.ppermute(a, "row", [(i, i ^ k) for i in range(4)])

    return move


to_core = row_swap(1)
to_x = row_swap(2)
ALL = ("dp", "row", "col")


def exchange(a, groups):
    return lax.all_to_all(a, ALL, 0, 0, axis_index_groups=groups, tiled=True)


def spots():
    n = lax.axis_size("dp")
    return lambda z, r, y: (z * 4 + r) * 2 + y, n


def to_rows(a):
    at, n = spots()
    return exchange(a, [[at(z, r, y) for r in range(4)] for z in range(n) for y in range(2)])


def to_plane(a):
    at, n = spots()
    return exchange(a, [[at(z, 2 * x + c, y) for x in range(2) for y in range(2)] for z in range(n) for c in range(2)])


def to_y(a):
    return lax.ppermute(a, "col", [(0, 1), (1, 0)])


def to_z(a, k):
    n = lax.axis_size("dp")
    return lax.ppermute(a, "dp", [(i, i ^ k) for i in range(n)])


def after(a, *first):
    return lax.optimization_barrier((a, *first))[0]


class Order:
    def __init__(self):
        self.last = None

    def __call__(self, fn, *args):
        leaves, tree = jax.tree.flatten(args)
        if self.last is not None:
            leaves = lax.optimization_barrier((*leaves, self.last))[:-1]
        out = fn(*jax.tree.unflatten(tree, leaves))
        self.last = jax.tree.leaves(out)[-1]
        return out


def by_index(i, mine, other, axis):
    return jnp.where(
        i == 0,
        jnp.concatenate([mine, other], axis=axis),
        jnp.concatenate([other, mine], axis=axis),
    )


def group_send(run, a):
    a = run(fold, a, to_core(a))
    return (a, to_y(a))


def gather_all(a):
    return lax.all_gather(a, ("row", "col"), axis=0, tiled=False)


def scatter_all(a):
    return lax.psum_scatter(a.reshape(-1, *a.shape[2:]), ("row", "col"), scatter_dimension=0, tiled=False)


def dp_gather(a):
    n = lax.axis_size("dp")
    if n != 4:
        return (lax.all_gather(a, "dp", axis=0, tiled=True),)
    return (a, to_z(a, 1), to_z(a, 2), to_z(a, 3))


def to_d(a):
    return lax.ppermute(a, ("row", "col"), [(i, i ^ 5) for i in range(8)])


def dp_scatter(run, sums, *parts):
    if lax.axis_size("dp") != 4:
        return (lax.psum(sum(p.astype(f32) for p in parts).astype(bf16), "dp"), lax.psum(sums, "dp"))
    q = run(plane_sum, sums, *parts)
    return (q[0], *[to_z(q[k], k) for k in (1, 2, 3)])


def to_depth(a):
    at, n = spots()
    return exchange(a, [[at(z, r, y) for z in range(n)] for r in range(4) for y in range(2)])


def pair_scatter(run, a, fa, b, fb, first):
    if lax.axis_size("dp") != 4:
        return lax.psum(jnp.concatenate([(a + fa).astype(bf16), (b + fb).astype(bf16)]), "dp")
    return to_depth(after(run(lambda *a: pair_call(pair_split_kernel, a, 2 * SLICE, bf16, 1, "pair_split")[0], a, fa, b, fb), first))


def pair_total(run, parts):
    if lax.axis_size("dp") != 4:
        return parts
    return to_depth(run(lambda a: pair_call(pair_sum_kernel, (a,), 2 * SLICE, bf16, 1, "pair_sum")[0], parts))


def pair_result(run, parts):
    if lax.axis_size("dp") != 4:
        a = parts.astype(f32)
        return a[:SLICE], a[SLICE:]
    return run(lambda a: pair_call(pair_place_kernel, (a,), SLICE, f32, 2, "pair_place"), parts)


def dp_quarters(run, quarters):
    if len(quarters) == 2:
        return quarters[:1], quarters[1]
    q, sums = run(quarter_sum, *quarters)
    return (q, *[to_z(q, k) for k in (1, 2, 3)]), sums


def dp_place(run, quarters, cut):
    if len(quarters) == 1:
        a = quarters[0].astype(f32)
        return [a[:, :cut], a[:, cut:]]
    return run(lambda *a: place_quarters(a, cut), *quarters)


def body(
    hidden_in, teacher, lengths, pos_embed,
    seg_qkv, seg_proj, seg_gain1, seg_bias1, seg_up, seg_down, seg_gain2, seg_bias2,
    cross_qkv, cross_proj, cross_gain1, cross_bias1, cross_up, cross_down, cross_gain2, cross_bias2,
):
    run = Order()
    c = lax.axis_index("row") & 1
    n_q, n_o, n_u = seg_qkv.shape[1], seg_proj.shape[1], seg_up.shape[1]
    q_q, q_o, q_u = n_q // 2, n_o // 2, n_u // 2

    vecs = (seg_gain1, seg_bias1, seg_gain2, seg_bias2, cross_gain1, cross_bias1, cross_gain2, cross_bias2)
    wa, xa = run(prep, seg_qkv, seg_proj)
    ax = to_x(xa)
    ay = to_y(wa)
    h = run(token_stack, hidden_in, *vecs, pos_embed)
    ax_ = after(ax, h)
    h = to_rows(h)
    wu = gather_all(after(seg_up, ax))
    az = to_z(ax_, 1)
    ayx = to_y(ax_)
    ac1 = to_core(run(join_rows, wa, ay, ax))
    ayz = to_z(ayx, 1)
    ac2 = to_core(run(join_rows, az, ayx, ayz))
    pa = (wa, ay, ax, az, ayx, ayz, ac1, ac2)
    h, rel, vab, sg1, sb1, sg2, sb2 = run(unstack, h)
    teach = to_rows(run(token_stack, teacher))
    cw_mine, cw_give = run(cross_prep, cross_qkv, cross_proj, cross_up, cross_down)
    wd = gather_all(after(seg_down, h))
    cw_got = to_core(cw_give)
    proj, mix, hat1, inv1, low, hatc1, invc1 = run(attn_fwd, lengths, h, sg1, sb1, pa)
    cw_x = to_x(run(cross_pick, cw_mine, cw_got))
    act, slope = run(ffn_up, after(low, teach), wu)
    hat2, inv2, hatc2, invc2 = run(ffn_down, act, hat1, sg1, sb1, sg2, sb2, wd)
    cw_z = to_z(after(cw_x, hatc2), 1)
    cw = (cw_mine, cw_got, cw_x, cw_z)

    msg = run(cls_message, hatc2, invc2, hatc1, teach)
    msg = run(pair_rows, msg, to_core(msg))
    msgs = (msg, to_y(msg))
    d2, d2_low, dhid, sums_a, sq = run(ffn_back, lengths, hat2, inv2, teach, slope, sg2, sb2, wd)
    m, cproj, cmix, part, v_low = run(lambda *a: cross1(*a, q_q, q_o), lengths, vab, msgs, cw)
    part = group_send(run, part)
    grad_d = run(weight_grad, d2_low, act)
    sum_d = scatter_all(grad_d)
    chat1, cinv1, clow, cact, cslope, part = run(lambda *a: cross2(*a, q_u), vab, m, part, cw)
    part = group_send(run, part)
    grad_u = run(weight_grad, low, dhid)
    sum_u = scatter_all(grad_u)
    cls_out, csq, csums_a, cd2, cd2_low, cdhid, part = run(cross3, lengths, vab, m, chat1, cslope, part, cw)
    part = group_send(run, part)
    d1, sums_b = run(up_back, d2, dhid, hat1, inv1, sg1, wu)
    cd1, cd1_low, csums_b, cdproj, part = run(
        lambda *a: cross4(*a, q_o), lengths, vab, cd2, chat1, cinv1, cproj, part, cw
    )
    part = group_send(run, part)
    outs = run(emit_output, hat2, sg2, sb2, cls_out)
    c_own, c_far = run(pack_acts, (v_low, cd1_low, clow, cd2_low), (cdproj, cmix, cdhid, cact))
    c_far = to_x(c_far)
    pos_part, ssums_a, sd2, sd2_low, slow, sact, sdhid, part = run(cross5, vab, m, cd1, part, wu, wd)
    part = group_send(run, part)
    s_own, s_far = run(pack_acts, (sd2_low, slow), (sact, sdhid))
    s_far = to_x(s_far)
    acts = dp_gather(run(join_rows, c_own, c_far))
    d1c, ssums_b = run(cross6, vab, m, sd2, invc1, part)
    facts = run(join_rows, s_own, s_far)
    facts_c = to_core(facts)
    sums = run(small_sums, sums_b, sums_a, ssums_b, ssums_a, csums_b, csums_a, pos_part, sq, csq)
    dproj1, d1_low, dxp = run(lambda *a: attn_back(1, *a), lengths, proj, d1, d1c, pa)
    f_d, f_u = run(lambda a, b: factor_grads(a, b, (q_u, q_u)), facts, facts_c)
    keep1, send = run(lambda *a: attn_grad(1, *a), h, d1_low, dproj1, mix)
    got1 = to_core(send)
    acts = run(join_rows, *acts) if len(acts) > 1 else acts[0]
    q_f = pair_scatter(run, sum_d, f_d, sum_u, f_u, keep1)
    a_y, a_d = run(chip_half, keep1, got1)
    a_y, a_d = to_y(a_y), to_d(a_d)
    dproj0, dxs = run(lambda *a: attn_back(0, *a), lengths, proj, dxp, d1_low, pa)
    outs = to_rows(after(outs, dproj0))
    sums = run(add_rows, sums, to_core(sums))
    keep0, send = run(lambda *a: attn_grad(0, *a), h, after(d1_low, a_y, a_d), dproj0, mix)
    got0 = to_core(send)
    q_f = pair_total(run, q_f)
    a_0, a_x = run(chip_half, keep0, got0)
    a_x = to_x(a_x)
    acts_c = to_core(after(acts, a_0))
    sums = run(add_rows, sums, to_y(sums))
    sums = run(add_rows, sums, to_x(sums))
    sums = run(own_sums, sums)
    q_a = dp_scatter(run, sums, a_0, a_y, a_x, a_d)
    output = run(token_join, outs)
    g_cqkv, g_cproj, g_cup, g_cdown = run(
        lambda a, b: factor_grads(a, b, (q_q, q_o, q_u, q_u)), acts, acts_c
    )
    g_down, g_up = pair_result(run, q_f)
    q_a, al = dp_quarters(run, q_a)
    dxs = to_rows(after(dxs, g_up, al))
    dx_out = run(token_join, dxs)
    g_qkv, g_proj = dp_place(run, q_a, n_q)
    valid = jnp.sum(lengths).astype(f32)
    loss = al[8, 0] / (2.0 * valid)
    return (
        output, loss, dx_out, al[9:25],
        g_qkv, g_proj, al[0], al[1], g_up, g_down, al[2], al[3],
        g_cqkv, g_cproj, al[4], al[5], g_cup, g_cdown, al[6], al[7],
    )


def solution(mesh):
    wide, cut, one = P("row", ("dp", "col")), P("row", "col"), P("row")
    block = (cut, cut, one, one, cut, cut, one, one)
    in_specs = (wide, wide, P(), P(None, "row")) + block + block
    out_specs = (wide, P(), wide, P(None, "row")) + block + block
    return jax.shard_map(body, mesh=mesh, in_specs=in_specs, out_specs=out_specs, check_vma=False)
```

```python
import functools
import jax
import jax.numpy as jnp
from jax import lax
from jax.experimental import pallas as pl
from jax.experimental.pallas import tpu as pltpu
from jax.sharding import PartitionSpec as P

D = 768
HEAD_DIM = 64
SEG = 128
SEGS = 16
SEQ_LEN = 2048
SLICE = 192
HALF = 96
EPS = 1e-05
NEG = -1e30
ROOT_HALF = 0.7071067811865476
INV_ROOT_TAU = 0.3989422804014327
bf16 = jnp.bfloat16
f32 = jnp.float32
GROUP = 12
GROUP_BACK = 6
COST = 0.005
VMEM_LIMIT = 60 * 1024 * 1024

NN = (((1,), (0,)), ((), ()))
NT = (((1,), (1,)), ((), ()))
TN = (((0,), (0,)), ((), ()))


def scalars(lengths, tok):
    r, y, z = lax.axis_index("row"), lax.axis_index("col"), lax.axis_index("dp")
    return z & 1, lengths[(z * lax.axis_size("col") + y) * 2 + (r >> 1)], (r & 1) * tok


def scale_of(lengths):
    n = lengths.shape[0]
    total = sum(lengths[i] for i in range(n)) if n <= 16 else lax.fori_loop(0, n, lambda i, a: a + lengths[i], 0)
    return (n * SEQ_LEN) / jnp.full((1, 1), total, jnp.int32).astype(f32)


def rel_rows(ref):
    r = lax.axis_index("row")
    return [ref[pl.ds(pl.multiple_of((r ^ k) * SLICE, 16), SLICE), :] for k in range(4)]


def put_rel_rows(ref, a):
    r = lax.axis_index("row")
    for k in range(4):
        ref[pl.ds(pl.multiple_of((r ^ k) * SLICE, 16), SLICE), :] = a[k * SLICE : (k + 1) * SLICE, :]


def dot(a, b, dims):
    return lax.dot_general(a, b, dims, preferred_element_type=f32)


def params(n=1):
    if n == 0:
        return pltpu.CompilerParams(vmem_limit_bytes=VMEM_LIMIT)
    return pltpu.CompilerParams(dimension_semantics=("arbitrary",) * n, vmem_limit_bytes=VMEM_LIMIT)


ANY = pl.BlockSpec(memory_space=pl.ANY)
SMEM = pl.BlockSpec(memory_space=pltpu.SMEM)


def whole(shape):
    return pl.BlockSpec(shape, lambda *_: (0,) * len(shape))


def piece_plan(refs, p):
    own, y1, x1, z1, y2, z2, c1, c2 = refs
    hi = p * HALF
    ho = (1 - p) * HALF
    x, xc = 2 * SLICE, 3 * SLICE
    return [
        (own, 0, SLICE, 0, 0), (c1, 0, SLICE, SLICE, 0),
        (x1, 0, HALF, x + hi, 0), (z1, 0, HALF, x + ho, 0),
        (c1, 2 * SLICE, HALF, xc + hi, 0), (c2, 0, HALF, xc + ho, 0),
        (y1, 0, SLICE, 0, 1), (c1, SLICE, SLICE, SLICE, 1),
        (y2, 0, HALF, x + hi, 1), (z2, 0, HALF, x + ho, 1),
        (c2, HALF, HALF, xc + hi, 1), (c2, 2 * HALF, HALF, xc + ho, 1),
    ]


def piece_copies(refs, dst, sem, p, src_cols, dst_col, base=0):
    lo, n = src_cols
    return [
        pltpu.make_async_copy(
            src.at[pl.ds(at, rows), pl.ds(lo, n)],
            dst.at[pl.ds(pl.multiple_of(row, 16), rows), pl.ds(dst_col(j), n)],
            sem.at[base + i],
        )
        for i, (src, at, rows, row, j) in enumerate(piece_plan(refs, p))
    ]


def half_copies(refs, dst, sem, p, j, src_cols, base=0):
    lo, n = src_cols
    return [
        pltpu.make_async_copy(
            src.at[pl.ds(at, rows), pl.ds(lo, n)], dst.at[pl.ds(pl.multiple_of(row, 16), rows), :], sem.at[base + i]
        )
        for i, (src, at, rows, row, _) in enumerate([a for a in piece_plan(refs, p) if a[4] == j])
    ]


def gathered_copies(ref, dst, sem):
    r = lax.axis_index("row")
    n = ref.shape[2]
    return [
        pltpu.make_async_copy(
            ref.at[(r ^ k) * 2 + j], dst.at[pl.ds(k * SLICE, SLICE), pl.ds(j * n, n)], sem.at[k * 2 + j]
        )
        for k in range(4)
        for j in range(2)
    ]


def norm_cols(resid):
    center = jnp.sum(resid, axis=0, keepdims=True) * (1.0 / D)
    spread = jnp.sum(resid * resid, axis=0, keepdims=True) * (1.0 / D) - center * center
    inv = lax.rsqrt(spread + EPS)
    return (resid - center) * inv, inv


def norm_back_cols(y, hat, inv, g):
    t = y * g
    m1 = jnp.sum(t, axis=0, keepdims=True) * (1.0 / D)
    m2 = jnp.sum(t * hat, axis=0, keepdims=True) * (1.0 / D)
    return inv * (t - m1 - hat * m2)


def probs_group(qs, ks, ok):
    ss = [dot(k, q, TN) for q, k in zip(qs, ks)]
    ss = [jnp.where(ok, s * HEAD_DIM**-0.5, NEG) for s in ss]
    ms = [jnp.max(s, axis=0, keepdims=True) for s in ss]
    es = [jnp.exp(s - m) for s, m in zip(ss, ms)]
    ts = [1.0 / jnp.sum(e, axis=0, keepdims=True) for e in es]
    return [e * t for e, t in zip(es, ts)]


def key_ok_of(scal, b, tile):
    pos = lax.broadcasted_iota(jnp.int32, (SEG, SEG), 0)
    at = scal[2] + pl.program_id(0) * tile + b * SEG
    return (pos + at < scal[1]) | (pos == 0)


def put_cls(tile, hat, inv, hatc_o, invc_o):
    n = tile // SEG
    for b in range(n):
        at = pl.ds(pl.program_id(0) * n + b, 1)
        hatc_o[at, :] = hat[:, b * SEG : (b + 1) * SEG].T[0:1, :]
        invc_o[at, :] = jnp.broadcast_to(inv[:, b * SEG : b * SEG + 1], (1, SEG))


def attn_fwd_kernel(tile, lengths, xs, g1, b1, *rest):
    refs = rest[:8]
    proj_o, mix_o, hat_o, inv_o, low_o, hatc_o, invc_o, w, wo, sem = rest[8:]
    scal = scalars(lengths, tile * pl.num_programs(0))
    n_q = w.shape[1] // 2
    n_o = wo.shape[1] // 2

    @pl.when(pl.program_id(0) == 0)
    def _():
        cps = piece_copies(refs, w, sem, scal[0], (0, n_q), lambda j: j * n_q)
        cps += piece_copies(refs, wo, sem, scal[0], (n_q, n_o), lambda j: j * n_o, 12)
        for c in cps:
            c.start()
        for c in cps:
            c.wait()

    x = jnp.concatenate(rel_rows(xs), axis=0)
    proj_o[...] = dot(w[...], x, TN).astype(bf16)
    for b in range(tile // SEG):
        ok = key_ok_of(scal, b, tile)
        cols = slice(b * SEG, (b + 1) * SEG)
        for h0 in range(0, D // HEAD_DIM, GROUP):
            qkv = [
                [
                    proj_o[(h * 3 + j) * HEAD_DIM : (h * 3 + j + 1) * HEAD_DIM, cols]
                    for j in range(3)
                ]
                for h in range(h0, h0 + GROUP)
            ]
            pts = probs_group([a[0] for a in qkv], [a[1] for a in qkv], ok)
            mixed = [dot(a[2], p.astype(bf16), NN).astype(bf16) for a, p in zip(qkv, pts)]
            mix_o[h0 * HEAD_DIM : (h0 + GROUP) * HEAD_DIM, cols] = jnp.concatenate(mixed, axis=0)
    hat, inv = norm_cols(x.astype(f32) + dot(wo[...], mix_o[...], NN))
    hat_o[...] = hat
    inv_o[...] = inv
    low_o[...] = (hat * g1[...] + b1[...]).astype(bf16)
    put_cls(tile, hat, inv, hatc_o, invc_o)


def attn_fwd(lengths, xs, g1, b1, parts, tile=256):
    t = xs.shape[1]
    n = parts[0].shape[1]
    n_q = n * 3 // 4
    n_o = n - n_q
    colb = lambda rows: pl.BlockSpec((rows, tile), lambda i: (0, i))
    return pl.pallas_call(
        functools.partial(attn_fwd_kernel, tile),
        grid=(t // tile,),
        in_specs=[SMEM, colb(D)] + [whole((D, 1))] * 2 + [ANY] * 8,
        out_specs=[colb(2 * n_q), colb(D), colb(D), colb(1), colb(D), whole((t // SEG, D)), whole((t // SEG, SEG))],
        out_shape=[
            jax.ShapeDtypeStruct((2 * n_q, t), bf16),
            jax.ShapeDtypeStruct((D, t), bf16),
            jax.ShapeDtypeStruct((D, t), f32),
            jax.ShapeDtypeStruct((1, t), f32),
            jax.ShapeDtypeStruct((D, t), bf16),
            jax.ShapeDtypeStruct((t // SEG, D), f32),
            jax.ShapeDtypeStruct((t // SEG, SEG), f32),
        ],
        scratch_shapes=[
            pltpu.VMEM((D, 2 * n_q), bf16),
            pltpu.VMEM((D, 2 * n_o), bf16),
            pltpu.SemaphoreType.DMA((24,)),
        ],
        compiler_params=params(),
        name="seg_attend",
        cost_estimate=cost(2 * t * D * D * 4 + 4 * t * SEG * D, 20 * 1024 * t, t * SEG * 12),
    )(lengths, xs, g1, b1, *parts)


def ffn_up_kernel(low, wg, act_o, slope_o, w, lt, sem):
    i = pl.program_id(0)

    @pl.when(i == 0)
    def _():
        cps = gathered_copies(wg, w, sem)
        for c in cps:
            c.start()
        lt[...] = low[...].T
        for c in cps:
            c.wait()

    wid = act_o.shape[1]
    at = pl.multiple_of(i * wid, 128)
    hidden = dot(lt[...], w[:, pl.ds(at, wid)], NN)
    phi = 0.5 * (1.0 + lax.erf(hidden * ROOT_HALF))
    act_o[...] = (hidden * phi).astype(bf16)
    slope = phi + hidden * jnp.exp(-0.5 * hidden * hidden) * INV_ROOT_TAU
    slope_o[...] = slope.astype(bf16)


def ffn_up(low, wg, wid=512):
    t = low.shape[1]
    n = wg.shape[2] * 2
    colb = pl.BlockSpec((t, wid), lambda i: (0, i))
    return pl.pallas_call(
        ffn_up_kernel,
        grid=(n // wid,),
        in_specs=[whole((D, t)), ANY],
        out_specs=[colb, colb],
        out_shape=[jax.ShapeDtypeStruct((t, n), bf16)] * 2,
        scratch_shapes=[pltpu.VMEM((D, n), bf16), pltpu.VMEM((t, D), bf16), pltpu.SemaphoreType.DMA((12,))],
        compiler_params=params(),
        name="seg_up",
        cost_estimate=cost(2 * t * D * n, 4 * t * n, 2 * t * n),
    )(low, wg)


def ffn_down_kernel(tile, act, hat1, g1, b1, g2, b2, wg, hat_o, inv_o, hatc_o, invc_o, w, sem):
    i = pl.program_id(0)

    @pl.when(i == 0)
    def _():
        cps = gathered_copies(wg, w, sem)
        for c in cps:
            c.start()
        for c in cps:
            c.wait()

    first = hat1[...] * g1[...] + b1[...]
    hat, inv = norm_cols(first + dot(w[...], act[...], NT))
    hat_o[...] = hat
    inv_o[...] = inv
    put_cls(tile, hat, inv, hatc_o, invc_o)


def ffn_down(act, hat1, g1, b1, g2, b2, wg, tile=256):
    t, n = act.shape
    colb = lambda rows: pl.BlockSpec((rows, tile), lambda i: (0, i))
    return pl.pallas_call(
        functools.partial(ffn_down_kernel, tile),
        grid=(t // tile,),
        in_specs=[pl.BlockSpec((tile, n), lambda i: (i, 0)), colb(D)] + [whole((D, 1))] * 4 + [ANY],
        out_specs=[colb(D), colb(1), whole((t // SEG, D)), whole((t // SEG, SEG))],
        out_shape=[
            jax.ShapeDtypeStruct((D, t), f32),
            jax.ShapeDtypeStruct((1, t), f32),
            jax.ShapeDtypeStruct((t // SEG, D), f32),
            jax.ShapeDtypeStruct((t // SEG, SEG), f32),
        ],
        scratch_shapes=[pltpu.VMEM((D, n), bf16), pltpu.SemaphoreType.DMA((12,))],
        compiler_params=params(),
        name="seg_down",
        cost_estimate=cost(2 * t * D * n, 2 * t * n + 8 * t * D, 0),
    )(act, hat1, g1, b1, g2, b2, wg)


def start_all(cps):
    for c in cps:
        c.start()


def wait_all(cps):
    for c in cps:
        c.wait()


def ffn_back_kernel(tile, lengths, hat2, inv2, xs, slope, g2, b2, wg, d2_o, d2low_o, dhid_o, sums_o, sq_o, wd, acc, sem):
    scal = scalars(lengths, tile * pl.num_programs(0))
    i = pl.program_id(0)
    cd = gathered_copies(wg, wd, sem)

    @pl.when(i == 0)
    def _():
        start_all(cd)
        acc[...] = jnp.zeros_like(acc)
        sq_o[...] = jnp.zeros_like(sq_o)

    lane = lax.broadcasted_iota(jnp.int32, (1, tile), 1) + i * tile
    keep = (lane + scal[2] < scal[1]) & (lane % SEG != 0)
    h2 = hat2[...]
    teach = jnp.concatenate(rel_rows(xs), axis=0).astype(f32)
    diff = jnp.where(keep, h2 * g2[...] + b2[...] - teach, 0.0)
    sq_o[...] += jnp.sum(diff * diff, axis=0, keepdims=True)
    y = (diff * scale_of(lengths)).astype(bf16).astype(f32)
    acc[0] += fold_lanes(y * h2)
    acc[1] += fold_lanes(y)
    d2 = norm_back_cols(y, h2, inv2[...], g2[...])
    d2_o[...] = d2
    d2_low = d2.astype(bf16)
    d2low_o[...] = d2_low

    @pl.when(i == 0)
    def _():
        wait_all(cd)

    dhid_o[...] = (dot(d2_low, wd[...], TN) * slope[...].astype(f32)).astype(bf16)
    lane_sums(acc, sums_o)


def fold_lanes(v):
    return sum(v[:, k * SEG : (k + 1) * SEG] for k in range(v.shape[1] // SEG))


def lane_sums(acc, sums_o):
    @pl.when(pl.program_id(0) == pl.num_programs(0) - 1)
    def _():
        for k in range(2):
            sums_o[k : k + 1, :] = jnp.sum(acc[k].T, axis=0, keepdims=True)


def ffn_back(lengths, hat2, inv2, teach, slope, g2, b2, wg, tile=256):
    t, n = slope.shape
    colb = lambda rows: pl.BlockSpec((rows, tile), lambda i: (0, i))
    rowb = pl.BlockSpec((tile, n), lambda i: (i, 0))
    return pl.pallas_call(
        functools.partial(ffn_back_kernel, tile),
        grid=(t // tile,),
        in_specs=[SMEM, colb(D), colb(1), colb(D), rowb] + [whole((D, 1))] * 2 + [ANY],
        out_specs=[colb(D), colb(D), rowb, whole((2, D)), whole((1, tile))],
        out_shape=[
            jax.ShapeDtypeStruct((D, t), f32),
            jax.ShapeDtypeStruct((D, t), bf16),
            jax.ShapeDtypeStruct((t, n), bf16),
            jax.ShapeDtypeStruct((2, D), f32),
            jax.ShapeDtypeStruct((1, tile), f32),
        ],
        scratch_shapes=[
            pltpu.VMEM((D, n), bf16),
            pltpu.VMEM((2, D, SEG), f32),
            pltpu.SemaphoreType.DMA((12,)),
        ],
        compiler_params=params(),
        name="seg_down_back",
        cost_estimate=cost(2 * t * D * n, 6 * t * n),
    )(lengths, hat2, inv2, teach, slope, g2, b2, wg)


def up_back_kernel(tile, d2, dhid, hat1, inv1, g1, wg, d1_o, sums_o, wu, acc, sem):
    i = pl.program_id(0)

    @pl.when(i == 0)
    def _():
        cu = gathered_copies(wg, wu, sem)
        start_all(cu)
        acc[...] = jnp.zeros_like(acc)
        wait_all(cu)

    s = d2[...] + dot(wu[...], dhid[...], NT)
    h1 = hat1[...]
    acc[0] += fold_lanes(s * h1)
    acc[1] += fold_lanes(s)
    d1_o[...] = norm_back_cols(s, h1, inv1[...], g1[...])
    lane_sums(acc, sums_o)


def up_back(d2, dhid, hat1, inv1, g1, wg, tile=256):
    t, n = dhid.shape
    colb = lambda rows: pl.BlockSpec((rows, tile), lambda i: (0, i))
    return pl.pallas_call(
        functools.partial(up_back_kernel, tile),
        grid=(t // tile,),
        in_specs=[colb(D), pl.BlockSpec((tile, n), lambda i: (i, 0)), colb(D), colb(1), whole((D, 1)), ANY],
        out_specs=[colb(D), whole((2, D))],
        out_shape=[jax.ShapeDtypeStruct((D, t), f32), jax.ShapeDtypeStruct((2, D), f32)],
        scratch_shapes=[
            pltpu.VMEM((D, n), bf16),
            pltpu.VMEM((2, D, SEG), f32),
            pltpu.SemaphoreType.DMA((12,)),
        ],
        compiler_params=params(),
        name="seg_up_back",
        cost_estimate=cost(2 * t * D * n, 4 * t * n),
    )(d2, dhid, hat1, inv1, g1, wg)


def norm_back_rows(y, hat, inv, g):
    t = y * g
    m1 = jnp.sum(t, axis=1, keepdims=True) * (1.0 / D)
    m2 = jnp.sum(t * hat, axis=1, keepdims=True) * (1.0 / D)
    return inv * (t - m1 - hat * m2)


def col_of(rows, k):
    n = rows.shape[0]
    pick = lax.broadcasted_iota(jnp.int32, (n, 1), 0) == k
    row = jnp.sum(jnp.where(pick, rows, 0.0), axis=0, keepdims=True)
    return jnp.broadcast_to(row, (SEG, rows.shape[1])).T


def put_rows(a, cls, tile):
    n = tile // SEG
    lane0 = lax.broadcasted_iota(jnp.int32, (1, SEG), 1) == 0
    return jnp.concatenate(
        [
            jnp.where(lane0, col_of(cls[...], pl.program_id(0) * n + b), a[:, b * SEG : (b + 1) * SEG])
            for b in range(n)
        ],
        axis=1,
    )


def attn_back_kernel(tile, j, lengths, proj, d1, cls, *rest):
    scal = scalars(lengths, tile * pl.num_programs(0))
    refs = rest[:8]
    outs, (w, wo, sem) = rest[8:-3], rest[-3:]
    dproj_o = outs[0]
    i = pl.program_id(0)
    n_q, n_o = w.shape[1], wo.shape[1]
    cq = half_copies(refs, w, sem, scal[0], j, (0, n_q))

    @pl.when(i == 0)
    def _():
        co = half_copies(refs, wo, sem, scal[0], j, (n_q, n_o), 6)
        start_all(co)
        start_all(cq)
        wait_all(co)

    d1_all = put_rows(d1[...], cls, tile) if j == 1 else d1[...]
    d1_low = cls[...] if j == 0 else d1_all.astype(bf16)
    dmix = dot(wo[...], d1_low, TN).astype(bf16)
    for b in range(tile // SEG):
        ok = key_ok_of(scal, b, tile)
        cols = slice(b * SEG, (b + 1) * SEG)
        for h0 in range(0, n_o // HEAD_DIM, GROUP_BACK):
            hs = range(h0, h0 + GROUP_BACK)
            part = lambda k: [proj[(h * 3 + k) * HEAD_DIM : (h * 3 + k + 1) * HEAD_DIM, cols] for h in hs]
            qs, ks, vs = part(0), part(1), part(2)
            dms = [dmix[h * HEAD_DIM : (h + 1) * HEAD_DIM, cols] for h in hs]
            ps = probs_group(qs, ks, ok)
            dps = [dot(v, dm, TN) for v, dm in zip(vs, dms)]
            dvs = [dot(dm, p.astype(bf16), NT) for dm, p in zip(dms, ps)]
            inner = [jnp.sum(p * dp, axis=0, keepdims=True) for p, dp in zip(ps, dps)]
            dss = [(p * (dp - a)).astype(bf16) for p, dp, a in zip(ps, dps, inner)]
            dqs = [dot(k, ds, NN) * HEAD_DIM**-0.5 for k, ds in zip(ks, dss)]
            dks = [dot(q, ds, NT) * HEAD_DIM**-0.5 for q, ds in zip(qs, dss)]
            out = [a.astype(bf16) for trio in zip(dqs, dks, dvs) for a in trio]
            dproj_o[h0 * 3 * HEAD_DIM : (h0 + GROUP_BACK) * 3 * HEAD_DIM, cols] = jnp.concatenate(out, axis=0)

    @pl.when(i == 0)
    def _():
        wait_all(cq)

    dx = d1_all + dot(w[...], dproj_o[...], NN)
    if j == 1:
        outs[1][...] = d1_low
        outs[2][...] = dx
    else:
        put_rel_rows(outs[1], dx.astype(bf16))


def attn_back(j, lengths, proj, d1, cls, parts, tile=256):
    t = proj.shape[1]
    n = parts[0].shape[1]
    n_q = n * 3 // 4
    n_o = n - n_q
    colb = lambda rows, k=0: pl.BlockSpec((rows, tile), lambda i: (k, i))
    wide = [((D, t), bf16, D), ((D, t), f32, D)] if j == 1 else [((D, t), bf16, D)]
    return pl.pallas_call(
        functools.partial(attn_back_kernel, tile, j),
        grid=(t // tile,),
        in_specs=[SMEM, colb(n_q, j), colb(D), whole(cls.shape) if j == 1 else colb(D)] + [ANY] * 8,
        out_specs=[colb(n_q)] + [colb(a[2]) for a in wide],
        out_shape=[jax.ShapeDtypeStruct((n_q, t), bf16)] + [jax.ShapeDtypeStruct(a[0], a[1]) for a in wide],
        scratch_shapes=[
            pltpu.VMEM((D, n_q), bf16),
            pltpu.VMEM((D, n_o), bf16),
            pltpu.SemaphoreType.DMA((16,)),
        ],
        compiler_params=params(),
        name="seg_attend_back",
        cost_estimate=cost(t * D * D * 4 + 6 * t * SEG * D, 10 * 1024 * t, t * SEG * 6),
    )(lengths, proj, d1, cls, *parts)


def split_rows(g, keep_o, send_o):
    keep_o[:SLICE, :] = g[:SLICE]
    send_o[:SLICE, :] = g[SLICE : 2 * SLICE]
    keep_o[SLICE:, :] = g[2 * SLICE : 3 * SLICE]
    send_o[SLICE:, :] = g[3 * SLICE :]


def grad_kernel(a, b, o):
    r = lax.axis_index("row")
    g = dot(a[...], b[...], NN).astype(bf16)
    for k in range(4):
        o[r ^ k, 0] = g[k * SLICE : (k + 1) * SLICE]


def weight_grad(a, b, wid=512):
    t, n = b.shape
    q = n // 2 // wid
    return pl.pallas_call(
        grad_kernel,
        grid=(n // wid,),
        in_specs=[whole((D, t)), pl.BlockSpec((t, wid), lambda i: (0, i))],
        out_specs=pl.BlockSpec((4, 1, SLICE, wid), lambda i: (0, i // q, 0, i % q)),
        out_shape=jax.ShapeDtypeStruct((4, 2, SLICE, n // 2), bf16),
        compiler_params=params(),
        name="weight_grad",
        cost_estimate=cost(2 * t * D * n, 2 * (t + D) * n, 0),
    )(a, b)


def attn_grad_kernel(steps_q, xs, low, dproj, mix, keep_o, send_o):
    i = pl.program_id(0)

    @pl.when(i < steps_q)
    def _():
        x = jnp.concatenate(rel_rows(xs), axis=0)
        split_rows(dot(x, dproj[...], NT).astype(bf16), keep_o, send_o)

    @pl.when(i == steps_q)
    def _():
        split_rows(dot(low[...], mix[...], NT).astype(bf16), keep_o, send_o)


def attn_grad(j, xs, low, dproj, mix):
    t = low.shape[1]
    n_q, n_o = dproj.shape[0], mix.shape[0] // 2
    wid = n_o
    q = n_q // wid
    out = pl.BlockSpec((2 * SLICE, wid), lambda i: (0, i))
    return pl.pallas_call(
        functools.partial(attn_grad_kernel, q),
        grid=(q + 1,),
        in_specs=[whole((D, t)), whole((D, t)), pl.BlockSpec((wid, t), lambda i: (jnp.minimum(i, q - 1), 0)),
                  pl.BlockSpec((wid, t), lambda i: (j, 0))],
        out_specs=[out, out],
        out_shape=[jax.ShapeDtypeStruct((2 * SLICE, n_q + n_o), bf16)] * 2,
        compiler_params=params(),
        name="attend_weight_grad",
        cost_estimate=cost(t * D * 4 * D, (t + D) * 4 * D, 0),
    )(xs, low, dproj, mix)


def add4(refs):
    return sum(a[...].astype(f32) for a in refs)


def chip_kernel(k0, g0, k1, g1, o):
    here = (lax.axis_index("row") >> 1) * 2 + lax.axis_index("col")
    for jj, (k, g) in enumerate(((k0, g0), (k1, g1))):
        a = add4((k, g)).astype(bf16)
        for xx in range(2):
            at = pl.multiple_of((here ^ (xx * 2 + jj)) * SLICE, 16)
            o[pl.ds(at, SLICE), :] = a[xx * SLICE : (xx + 1) * SLICE]


def chip_sum(keep, got, wid=768):
    n = keep.shape[1] // 2
    k = n // wid
    lo = pl.BlockSpec((2 * SLICE, wid), lambda i: (0, i))
    hi = pl.BlockSpec((2 * SLICE, wid), lambda i: (0, i + k))
    return pl.pallas_call(
        chip_kernel,
        grid=(k,),
        in_specs=[lo, lo, hi, hi],
        out_specs=pl.BlockSpec((4 * SLICE, wid), lambda i: (0, i)),
        out_shape=jax.ShapeDtypeStruct((4 * SLICE, n), bf16),
        compiler_params=params(),
        name="chip_sum",
        cost_estimate=cost(0, 12 * SLICE * n),
    )(keep, got, keep, got)


def chip_half_kernel(k0, g0, a_o, b_o):
    a = add4((k0, g0)).astype(bf16)
    a_o[...] = a[:SLICE]
    b_o[...] = a[SLICE:]


def chip_half(keep, got, wid=768):
    n = keep.shape[1]
    lo = pl.BlockSpec((2 * SLICE, wid), lambda i: (0, i))
    return pl.pallas_call(
        chip_half_kernel,
        grid=(n // wid,),
        in_specs=[lo, lo],
        out_specs=[pl.BlockSpec((SLICE, wid), lambda i: (0, i))] * 2,
        out_shape=[jax.ShapeDtypeStruct((SLICE, n), bf16)] * 2,
        compiler_params=params(),
        name="chip_sum",
        cost_estimate=cost(0, 6 * SLICE * n),
    )(keep, got)


def add_stacked(refs):
    out = []
    for a in refs:
        for i in range(0, a.shape[0], SLICE):
            out.append(a[i : i + SLICE, :].astype(f32))
    return sum(out)


FEW = 8


def plane_kernel(*refs):
    parts, sums, got, outs, total_s = refs[:-7], refs[-7], refs[-6], refs[-5:-1], refs[-1]
    r = lax.axis_index("row")
    z = lax.axis_index("dp")
    h = outs[0].shape[0] - FEW
    total_s[...] = add_stacked(parts).astype(bf16)
    v = sums[...] + got[...]
    v = sum(jnp.where(r == q, v[:, q * SLICE : (q + 1) * SLICE], 0.0) for q in range(4))
    n = v.shape[0] // FEW
    v = jnp.concatenate([v[n * i : n * (i + 1), :] for i in range(FEW)], axis=1)
    hi = v.astype(bf16)
    both = jnp.concatenate([hi.astype(f32), v - hi.astype(f32)], axis=0).astype(bf16)
    for k, o in enumerate(outs):
        o[:h, :] = total_s[pl.ds(pl.multiple_of((z ^ k) * h, 16), h), :]
        o[h:, :] = both


def plane_sum(sums, got, *parts):
    n = parts[0].shape[1]
    vm = pl.BlockSpec(memory_space=pltpu.VMEM)
    return pl.pallas_call(
        plane_kernel,
        in_specs=[vm] * (len(parts) + 2),
        out_specs=[vm] * 4,
        out_shape=[jax.ShapeDtypeStruct((SLICE // 4 + FEW, n), bf16)] * 4,
        scratch_shapes=[pltpu.VMEM((SLICE, n), bf16)],
        compiler_params=params(0),
        name="plane_sum",
        cost_estimate=cost(0, 10 * SLICE * n),
    )(*parts, sums, got)


def pair_split_kernel(a, fa, b, fb, o):
    va, vb = add4((a, fa)).astype(bf16), add4((b, fb)).astype(bf16)
    h = SLICE // 4
    for q in range(4):
        o[2 * q * h : (2 * q + 1) * h, :] = va[q * h : (q + 1) * h]
        o[(2 * q + 1) * h : (2 * q + 2) * h, :] = vb[q * h : (q + 1) * h]


def pair_sum_kernel(p, o):
    h = p.shape[0] // 4
    v = sum(p[q * h : (q + 1) * h, :].astype(f32) for q in range(4)).astype(bf16)
    for q in range(4):
        o[q * h : (q + 1) * h, :] = v


def pair_place_kernel(p, a_o, b_o):
    h = p.shape[0] // 8
    for q in range(4):
        a_o[q * h : (q + 1) * h, :] = p[2 * q * h : (2 * q + 1) * h, :].astype(f32)
        b_o[q * h : (q + 1) * h, :] = p[(2 * q + 1) * h : (2 * q + 2) * h, :].astype(f32)


def pair_call(kernel, args, rows, dtype, count, name):
    n = args[0].shape[1]
    wid = 512
    spec = lambda m: pl.BlockSpec((m, wid), lambda i: (0, i))
    return pl.pallas_call(
        kernel,
        grid=(n // wid,),
        in_specs=[spec(a.shape[0]) for a in args],
        out_specs=[spec(rows)] * count,
        out_shape=[jax.ShapeDtypeStruct((rows, n), dtype)] * count,
        compiler_params=params(),
        name=name,
        cost_estimate=cost(0, 8 * rows * n),
    )(*args)


def quarter_kernel(*refs):
    parts, q_o, small_o = refs[:-2], refs[-2], refs[-1]
    v = add4(parts)
    h = q_o.shape[0]
    q_o[...] = v[:h].astype(bf16)
    n = FEW // 2
    w = v[h : h + n] + v[h + n :]
    c = small_o.shape[1]
    for i in range(FEW):
        small_o[n * i : n * (i + 1), :] = w[:, c * i : c * (i + 1)]


def quarter_sum(*parts):
    vm = pl.BlockSpec(memory_space=pltpu.VMEM)
    h, n = parts[0].shape
    return pl.pallas_call(
        quarter_kernel,
        in_specs=[vm] * len(parts),
        out_specs=[vm] * 2,
        out_shape=[jax.ShapeDtypeStruct((h - FEW, n), bf16), jax.ShapeDtypeStruct((FEW * FEW // 2, n // FEW), f32)],
        compiler_params=params(0),
        name="quarter_sum",
        cost_estimate=cost(0, 1e6),
    )(*parts)


def place_kernel(cut, p0, p1, p2, p3, *outs):
    z = lax.axis_index("dp")
    h = p0.shape[0]
    for k, p in enumerate((p0, p1, p2, p3)):
        rows = pl.ds(pl.multiple_of((z ^ k) * h, 8), h)
        outs[0][rows, :] = p[:, :cut].astype(f32)
        if len(outs) > 1:
            outs[1][rows, :] = p[:, cut:].astype(f32)


def place_quarters(parts, cut):
    vm = pl.BlockSpec(memory_space=pltpu.VMEM)
    h, n = parts[0].shape
    shapes = [(4 * h, cut)] + ([(4 * h, n - cut)] if cut < n else [])
    return pl.pallas_call(
        functools.partial(place_kernel, cut),
        in_specs=[vm] * 4,
        out_specs=[vm] * len(shapes),
        out_shape=[jax.ShapeDtypeStruct(a, f32) for a in shapes],
        compiler_params=params(0),
        name="place_quarters",
        cost_estimate=cost(0, 2e6),
    )(*parts)


def output_kernel(tile, hat2, g2, b2, cls, o):
    put_rel_rows(o, put_rows(hat2[...] * g2[...] + b2[...], cls, tile).astype(bf16))


def emit_output(hat2, g2, b2, cls, tile=256):
    t = hat2.shape[1]
    colb = lambda rows: pl.BlockSpec((rows, tile), lambda i: (0, i))
    return pl.pallas_call(
        functools.partial(output_kernel, tile),
        grid=(t // tile,),
        in_specs=[colb(D)] + [whole((D, 1))] * 2 + [whole(cls.shape)],
        out_specs=colb(D),
        out_shape=jax.ShapeDtypeStruct((D, t), bf16),
        compiler_params=params(),
        name="emit_output",
        cost_estimate=cost(0, 6 * t * D),
    )(hat2, g2, b2, cls)
def cost(flops, nbytes, trans=0):
    return pl.CostEstimate(flops=int(flops * COST), bytes_accessed=int(nbytes * COST), transcendentals=int(trans * COST))


def vmcall(kernel, name, smem, vmem, anys, outs, scratch, c):
    vm = pl.BlockSpec(memory_space=pltpu.VMEM)
    return pl.pallas_call(
        kernel,
        in_specs=[SMEM] * len(smem) + [vm] * len(vmem) + [ANY] * len(anys),
        out_specs=[vm] * len(outs),
        out_shape=[jax.ShapeDtypeStruct(s, d) for s, d in outs],
        scratch_shapes=scratch,
        compiler_params=params(0),
        name=name,
        cost_estimate=c,
    )(*smem, *vmem, *anys)


def axes():
    r = lax.axis_index("row")
    return r, lax.axis_index("col"), lax.axis_index("dp")


def prep_kernel(qkv, proj, a_o, xa_o):
    p = lax.axis_index("dp") & 1
    n_q = qkv.shape[1]
    half = pl.ds(pl.multiple_of(p * HALF, 16), HALF)
    xa_o[:, :n_q] = qkv[half, :]
    xa_o[:, n_q:] = proj[half, :]
    a_o[:, :n_q] = qkv[...]
    a_o[:, n_q:] = proj[...]


def prep(qkv, proj):
    n = qkv.shape[1] + proj.shape[1]
    return vmcall(
        prep_kernel, "prep_weights", [], [qkv, proj], [], [((SLICE, n), bf16), ((HALF, n), bf16)], [], cost(0, 2e6),
    )


VEC = 32


def stack_kernel(x, *rest):
    vecs, o = rest[:-1], rest[-1]
    t = o.shape[1]
    rows = o.shape[0] // 4
    for q in range(4):
        o[q * rows : q * rows + SLICE, :] = x[:, q * t : (q + 1) * t]
    if vecs:
        v = jnp.concatenate([a[...].reshape(1, SLICE).astype(f32) for a in vecs[:-1]] + [vecs[-1][...].astype(f32)], axis=0)
        v = jnp.concatenate([v, jnp.zeros((VEC - v.shape[0], SLICE), f32)], axis=0).astype(bf16)
        for q in range(4):
            o[q * rows + SLICE : (q + 1) * rows, :SLICE] = v
            o[q * rows + SLICE : (q + 1) * rows, SLICE:] = jnp.zeros((VEC, t - SLICE), bf16)


def token_stack(x, *vecs):
    rows = SLICE + (VEC if vecs else 0)
    return vmcall(
        stack_kernel, "token_stack", [], [x, *vecs], [], [((4 * rows, x.shape[1] // 4), bf16)], [], cost(0, 3e6)
    )[0]


def join_kernel(p, o):
    t = p.shape[1]
    for q in range(4):
        o[:, q * t : (q + 1) * t] = p[q * SLICE : (q + 1) * SLICE, :]


def token_join(p):
    return vmcall(join_kernel, "token_join", [], [p], [], [((SLICE, 4 * p.shape[1]), bf16)], [], cost(0, 3e6))[0]


def cross_prep_kernel(qkv, proj, up, down, mine_o, give_o):
    c = lax.axis_index("row") & 1
    at = 0
    for w in (qkv, proj, up, down):
        q = w.shape[1] // 2
        a, b = w[:, :q].astype(f32), w[:, q:].astype(f32)
        mine_o[:, at : at + q] = jnp.where(c == 0, a, b).astype(bf16)
        give_o[:, at : at + q] = jnp.where(c == 0, b, a).astype(bf16)
        at += q


def cross_prep(qkv, proj, up, down):
    vm = pl.BlockSpec(memory_space=pltpu.VMEM)
    n = (qkv.shape[1] + proj.shape[1] + up.shape[1] + down.shape[1]) // 2
    return pl.pallas_call(
        cross_prep_kernel,
        in_specs=[vm] * 4,
        out_specs=[vm] * 2,
        out_shape=[jax.ShapeDtypeStruct((SLICE, n), bf16)] * 2,
        compiler_params=params(0),
        name="cross_prep",
        cost_estimate=cost(0, 4e6),
    )(qkv, proj, up, down)


def pick_kernel(mine, got, o):
    c, p = lax.axis_index("row") & 1, lax.axis_index("dp") & 1

    @pl.when(c == p)
    def _():
        o[...] = mine[...]

    @pl.when(c != p)
    def _():
        o[...] = got[...]


def cross_pick(mine, got):
    vm = pl.BlockSpec(memory_space=pltpu.VMEM)
    return pl.pallas_call(
        pick_kernel,
        in_specs=[vm] * 2,
        out_specs=vm,
        out_shape=jax.ShapeDtypeStruct(mine.shape, bf16),
        compiler_params=params(0),
        name="cross_pick",
        cost_estimate=cost(0, 3e6),
    )(mine, got)


def swap_cores(v):
    s = SLICE
    return jnp.concatenate([v[:, s : 2 * s], v[:, :s], v[:, 3 * s :], v[:, 2 * s : 3 * s]], axis=1)


def core_order(v):
    c = lax.axis_index("row") & 1
    return jnp.where(c == 0, v, swap_cores(v))


def vec_kernel(h, x_o, rel_o, abs_o, c0, c1, c2, c3):
    rows = h.shape[0] // 4
    for q in range(4):
        x_o[q * SLICE : (q + 1) * SLICE, :] = h[q * rows : q * rows + SLICE, :]
    r = lax.axis_index("row")
    part = [
        h[pl.ds(pl.multiple_of((r ^ k) * rows + SLICE, 16), VEC), :][:, : 2 * SEG].astype(f32)[:24, :SLICE] for k in range(4)
    ]
    rel = jnp.concatenate(part, axis=1)
    rel_o[...] = rel
    abs_o[...] = core_order(rel)
    cols = rel[:8].T
    for i, o in enumerate((c0, c1, c2, c3)):
        o[...] = cols[:, i : i + 1]


def unstack(h):
    n = 8 + SEGS
    return vmcall(
        vec_kernel, "unstack", [], [h], [],
        [((D, h.shape[1]), bf16)] + [((n, D), f32)] * 2 + [((D, 1), f32)] * 4, [], cost(0, 3e6),
    )


H2, H1, TE, IV = slice(0, D), slice(D, 2 * D), slice(2 * D, 3 * D), slice(3 * D, 3 * D + SEG)
MSG = 3 * D + SEG


def msg_kernel(hat2, inv2, hat1, teach, o):
    n = hat2.shape[0]
    o[:, H2] = core_order(hat2[...])
    o[:, H1] = core_order(hat1[...])
    o[:, IV] = inv2[...]
    rows = []
    parts = rel_rows(teach)
    for b in range(n):
        at = slice(b * SEG, (b + 1) * SEG)
        rows.append(jnp.concatenate([t[:, at].astype(f32).T[0:1, :] for t in parts], axis=1))
    o[:, TE] = core_order(jnp.concatenate(rows, axis=0))


def cls_message(hat2, inv2, hat1, teach):
    vm = pl.BlockSpec(memory_space=pltpu.VMEM)
    return pl.pallas_call(
        msg_kernel,
        in_specs=[vm] * 4,
        out_specs=vm,
        out_shape=jax.ShapeDtypeStruct((hat2.shape[0], MSG), f32),
        compiler_params=params(0),
        name="cls_message",
        cost_estimate=cost(0, 2e6),
    )(hat2, inv2, hat1, teach)


def pair_kernel(a, b, o):
    n = a.shape[0]
    c = lax.axis_index("row") & 1
    o[pl.ds(pl.multiple_of(c * n, 8), n), :] = a[...]
    o[pl.ds(pl.multiple_of((1 - c) * n, 8), n), :] = b[...]


def pair_rows(a, b):
    return vmcall(pair_kernel, "core_pair", [], [a, b], [], [((2 * a.shape[0], a.shape[1]), a.dtype)], [], cost(0, 1e6))[0]


def fold_kernel(a, b, o):
    o[...] = add4((a, b)).astype(o.dtype)


def fold(a, b):
    return vmcall(fold_kernel, "core_fold", [], [a, b], [], [(a.shape, a.dtype)], [], cost(0, 1e5))[0]


def cross_copies(refs, dst, sem, lo, n, base=0):
    c, p = lax.axis_index("row") & 1, lax.axis_index("dp") & 1
    at = [c * SLICE, (1 - c) * SLICE, 2 * SLICE + p * SLICE, 2 * SLICE + (1 - p) * SLICE]
    return [
        pltpu.make_async_copy(
            src.at[:, pl.ds(lo, n)], dst.at[pl.ds(pl.multiple_of(row, 16), SLICE), :], sem.at[base + i]
        )
        for i, (src, row) in enumerate(zip(refs, at))
    ]


def norm_rows(resid):
    center = jnp.sum(resid, axis=1, keepdims=True) * (1.0 / D)
    spread = jnp.sum(resid * resid, axis=1, keepdims=True) * (1.0 / D) - center * center
    inv = lax.rsqrt(spread + EPS)
    return (resid - center) * inv, inv


def total(parts):
    return sum(p[...].astype(f32) for p in parts)


def cls_rows(vec, m):
    pos = vec[8 : 8 + SEGS, :]
    return m[:, H2] * vec[2:3, :] + vec[3:4, :] + jnp.concatenate([pos] * (m.shape[0] // SEGS), axis=0)


def cross_probs(cproj, lens):
    n = cproj.shape[0]
    qi = lax.broadcasted_iota(jnp.int32, (n, n), 0)
    ki = lax.broadcasted_iota(jnp.int32, (n, n), 1)
    limit = jnp.where(ki < SEGS, lens[0], lens[1])
    ok = (qi // SEGS == ki // SEGS) & ((ki % SEGS) * SEG < limit)
    out = []
    for h in range(cproj.shape[1] // (3 * HEAD_DIM)):
        q, k, v = [cproj[:, (3 * h + j) * HEAD_DIM : (3 * h + j + 1) * HEAD_DIM] for j in range(3)]
        s = jnp.where(ok, dot(q, k, NT) * HEAD_DIM**-0.5, NEG)
        e = jnp.exp(s - jnp.max(s, axis=1, keepdims=True))
        out.append((q, k, v, e / jnp.sum(e, axis=1, keepdims=True)))
    return out


def group_lens(lengths, rows):
    r, _, z = axes()
    here = lax.axis_size("col")
    return [lengths[(z * here + j) * 2 + (r >> 1)] for j in range(2)]


def cross1_kernel(lengths, vec, m0, m1, *rest):
    refs = rest[:4]
    m_o, cproj_o, cmix_o, part_o, vlow_o, w, sem = rest[4:]
    _, y, _ = axes()
    n_q = cproj_o.shape[1]
    cps = cross_copies(refs, w, sem, 0, w.shape[1])
    start_all(cps)
    n = m0.shape[0]
    for m, yy in ((m0, y), (m1, 1 - y)):
        m_o[pl.ds(pl.multiple_of(yy * n, 8), n), :] = m[...]
    v_low = cls_rows(vec[...], m_o[...]).astype(bf16)
    vlow_o[...] = v_low
    wait_all(cps)
    cproj = dot(v_low, w[:, :n_q], NN).astype(bf16)
    cproj_o[...] = cproj
    mix = [dot(p.astype(bf16), v, NN) for _, _, v, p in cross_probs(cproj, group_lens(lengths, None))]
    mix = jnp.concatenate(mix, axis=1).astype(bf16)
    cmix_o[...] = mix
    part_o[...] = dot(mix, w[:, n_q:], NT).astype(bf16)


def cross1(lengths, vec, msgs, refs, n_q, n_o):
    n = 2 * msgs[0].shape[0]
    return vmcall(
        cross1_kernel, "cross_attend", [lengths], [vec, *msgs], refs,
        [((n, MSG), f32), ((n, n_q), bf16), ((n, n_o), bf16), ((n, D), bf16), ((n, D), bf16)],
        [pltpu.VMEM((D, n_q + n_o), bf16), pltpu.SemaphoreType.DMA((4,))],
        cost(2e7, 2e6),
    )


def cross2_kernel(vec, m, p0, p1, *rest):
    refs = rest[:4]
    hat_o, inv_o, low_o, act_o, slope_o, part_o, wu, wd, sem = rest[4:]
    n = wu.shape[1]
    lo = refs[0].shape[1] - 2 * n
    cps = cross_copies(refs, wu, sem, lo, n) + cross_copies(refs, wd, sem, lo + n, n, 4)
    start_all(cps)
    hat, inv = norm_rows(cls_rows(vec[...], m[...]) + total((p0, p1)))
    hat_o[...] = hat
    inv_o[...] = jnp.broadcast_to(inv, inv_o.shape)
    low = (hat * vec[4:5, :] + vec[5:6, :]).astype(bf16)
    low_o[...] = low
    wait_all(cps)
    hidden = dot(low, wu[...], NN)
    phi = 0.5 * (1.0 + lax.erf(hidden * ROOT_HALF))
    act = (hidden * phi).astype(bf16)
    act_o[...] = act
    slope_o[...] = phi + hidden * jnp.exp(-0.5 * hidden * hidden) * INV_ROOT_TAU
    part_o[...] = dot(act, wd[...], NT).astype(bf16)


def cross2(vec, m, parts, refs, n_u):
    n = m.shape[0]
    return vmcall(
        cross2_kernel, "cross_ffn", [], [vec, m, *parts], refs,
        [((n, D), f32), ((n, SEG), f32), ((n, D), bf16), ((n, n_u), bf16), ((n, n_u), f32), ((n, D), bf16)],
        [pltpu.VMEM((D, n_u), bf16)] * 2 + [pltpu.SemaphoreType.DMA((8,))],
        cost(2e7, 3e6),
    )


def own_rows(ref, n):
    r, y, _ = axes()
    return ref[pl.ds(pl.multiple_of((y * 2 + (r & 1)) * n, 8), n), :]


def cross3_kernel(lengths, vec, m, hat1, slope, p0, p1, *rest):
    refs = rest[:4]
    cls_o, sq_o, sums_o, d2_o, d2low_o, dhid_o, part_o, wu, wd, keep, sem = rest[4:]
    n = wu.shape[1]
    lo = refs[0].shape[1] - 2 * n
    cps = cross_copies(refs, wu, sem, lo, n) + cross_copies(refs, wd, sem, lo + n, n, 4)
    start_all(cps)
    first = hat1[...] * vec[4:5, :] + vec[5:6, :]
    hat2, inv2 = norm_rows(first + total((p0, p1)))
    out = hat2 * vec[6:7, :] + vec[7:8, :]
    rows = out.shape[0]
    ti = lax.broadcasted_iota(jnp.int32, (rows, 1), 0)
    lens = group_lens(lengths, rows)
    live = (ti % SEGS) * SEG < jnp.where(ti < SEGS, lens[0], lens[1])
    diff = jnp.where(live, out - m[:, TE], 0.0)
    k = cls_o.shape[0]
    keep[...] = out
    cls_o[...] = core_order(own_rows(keep, k))
    keep[...] = diff
    mine = own_rows(keep, k)
    sq_o[...] = jnp.sum(mine * mine, axis=0, keepdims=True)
    yv = diff * scale_of(lengths)
    sums_o[0:1, :] = jnp.sum(yv * hat2, axis=0, keepdims=True)
    sums_o[1:2, :] = jnp.sum(yv, axis=0, keepdims=True)
    d2 = norm_back_rows(yv, hat2, inv2, vec[6:7, :])
    d2_o[...] = d2
    d2_low = d2.astype(bf16)
    d2low_o[...] = d2_low
    wait_all(cps)
    dhid = (dot(d2_low, wd[...], NN) * slope[...]).astype(bf16)
    dhid_o[...] = dhid
    part_o[...] = dot(dhid, wu[...], NT).astype(bf16)


def cross3(lengths, vec, m, hat1, slope, parts, refs):
    n, n_u = slope.shape
    return vmcall(
        cross3_kernel, "cross_ffn_back", [lengths], [vec, m, hat1, slope, *parts], refs,
        [((n // 4, D), f32), ((1, D), f32), ((2, D), f32), ((n, D), f32), ((n, D), bf16), ((n, n_u), bf16), ((n, D), bf16)],
        [pltpu.VMEM((D, n_u), bf16)] * 2 + [pltpu.VMEM((n, D), f32), pltpu.SemaphoreType.DMA((8,))],
        cost(2e7, 3e6),
    )


def cross4_kernel(lengths, vec, d2, hat1, inv1, cproj, p0, p1, *rest):
    refs = rest[:4]
    d1_o, d1low_o, sums_o, dproj_o, part_o, w, sem = rest[4:]
    n_q = dproj_o.shape[1]
    cps = cross_copies(refs, w, sem, 0, w.shape[1])
    start_all(cps)
    s = d2[...] + total((p0, p1))
    h1 = hat1[...]
    sums_o[0:1, :] = jnp.sum(s * h1, axis=0, keepdims=True)
    sums_o[1:2, :] = jnp.sum(s, axis=0, keepdims=True)
    d1 = norm_back_rows(s, h1, inv1[:, 0:1], vec[4:5, :])
    d1_o[...] = d1
    d1_low = d1.astype(bf16)
    d1low_o[...] = d1_low
    wait_all(cps)
    dmix = dot(d1_low, w[:, n_q:], NN).astype(bf16)
    outs = []
    for h, (q, k, v, p) in enumerate(cross_probs(cproj[...], group_lens(lengths, None))):
        dm = dmix[:, h * HEAD_DIM : (h + 1) * HEAD_DIM]
        dv = dot(p.astype(bf16), dm, TN)
        dp = dot(dm, v, NT)
        ds = (p * (dp - jnp.sum(p * dp, axis=1, keepdims=True))).astype(bf16)
        outs += [dot(ds, k, NN) * HEAD_DIM**-0.5, dot(ds, q, TN) * HEAD_DIM**-0.5, dv]
    dproj = jnp.concatenate(outs, axis=1).astype(bf16)
    dproj_o[...] = dproj
    part_o[...] = dot(dproj, w[:, :n_q], NT).astype(bf16)


def cross4(lengths, vec, d2, hat1, inv1, cproj, parts, refs, n_o):
    n, n_q = cproj.shape
    return vmcall(
        cross4_kernel, "cross_attend_back", [lengths], [vec, d2, hat1, inv1, cproj, *parts], refs,
        [((n, D), f32), ((n, D), bf16), ((2, D), f32), ((n, n_q), bf16), ((n, D), bf16)],
        [pltpu.VMEM((D, n_q + n_o), bf16), pltpu.SemaphoreType.DMA((4,))],
        cost(2e7, 2e6),
    )


def quarter_copies(ref, dst, sem, base=0):
    r, y, _ = axes()
    n = dst.shape[1]
    cols = pl.ds(pl.multiple_of((r & 1) * n, 128), n)
    return [
        pltpu.make_async_copy(
            ref.at[(((r >> 1) ^ (s >> 1)) * 2 + (s & 1)) * 2 + y, :, cols],
            dst.at[pl.ds(s * SLICE, SLICE), :],
            sem.at[base + s],
        )
        for s in range(4)
    ]


def cross5_kernel(vec, m, d1, p0, p1, *rest):
    ups, downs, pos_o, sums_o, d2_o, d2low_o, low_o, act_o, dhid_o, part_o, wu, wd, sem = rest
    cps = quarter_copies(ups, wu, sem) + quarter_copies(downs, wd, sem, 4)
    start_all(cps)
    dcls = d1[...] + total((p0, p1))
    pos_o[...] = sum(dcls[i : i + SEGS] for i in range(0, dcls.shape[0], SEGS))
    yv = dcls.astype(bf16).astype(f32)
    h2 = m[:, H2]
    sums_o[0:1, :] = jnp.sum(yv * h2, axis=0, keepdims=True)
    sums_o[1:2, :] = jnp.sum(yv, axis=0, keepdims=True)
    d2 = norm_back_rows(yv, h2, m[:, 3 * D : 3 * D + 1], vec[2:3, :])
    d2_o[...] = d2
    d2_low = d2.astype(bf16)
    d2low_o[...] = d2_low
    low = (m[:, H1] * vec[0:1, :] + vec[1:2, :]).astype(bf16)
    low_o[...] = low
    wait_all(cps)
    hidden = dot(low, wu[...], NN)
    phi = 0.5 * (1.0 + lax.erf(hidden * ROOT_HALF))
    act_o[...] = (hidden * phi).astype(bf16)
    slope = phi + hidden * jnp.exp(-0.5 * hidden * hidden) * INV_ROOT_TAU
    dhid = (dot(d2_low, wd[...], NN) * slope).astype(bf16)
    dhid_o[...] = dhid
    part_o[...] = dot(dhid, wu[...], NT).astype(bf16)


def cross5(vec, m, d1, parts, ups, downs):
    n = m.shape[0]
    n_u = ups.shape[2] // 2
    return vmcall(
        cross5_kernel, "cls_ffn_back", [], [vec, m, d1, *parts], [ups, downs],
        [((SEGS, D), f32), ((2, D), f32), ((n, D), f32), ((n, D), bf16), ((n, D), bf16), ((n, n_u), bf16),
         ((n, n_u), bf16), ((n, D), bf16)],
        [pltpu.VMEM((D, n_u), bf16)] * 2 + [pltpu.SemaphoreType.DMA((12,))],
        cost(3e7, 3e6),
    )


def cross6_kernel(vec, m, d2, inv1, p0, p1, d1_o, sums_o, keep):
    s = d2[...] + total((p0, p1))
    h1 = m[:, H1]
    sums_o[0:1, :] = jnp.sum(s * h1, axis=0, keepdims=True)
    sums_o[1:2, :] = jnp.sum(s, axis=0, keepdims=True)
    n = d1_o.shape[0]
    keep[...] = s
    mine = own_rows(keep, n)
    keep[...] = h1
    d1_o[...] = core_order(norm_back_rows(mine, own_rows(keep, n), inv1[:, 0:1], vec[0:1, :]))


def cross6(vec, m, d2, inv1, parts):
    n = m.shape[0]
    return vmcall(
        cross6_kernel, "cls_norm_back", [], [vec, m, d2, inv1, *parts], [],
        [((n // 4, D), f32), ((2, D), f32)], [pltpu.VMEM((n, D), f32)], cost(0, 1e6),
    )


def pack_kernel(count, *refs):
    wides, narrows, (own_o, far_o) = refs[:count], refs[count:-2], refs[-2:]
    c = lax.axis_index("row") & 1
    at = 0
    for w in wides:
        v = w[...].astype(f32)
        s = [v[:, i * SLICE : (i + 1) * SLICE] for i in range(4)]
        own_o[:, at : at + SLICE] = jnp.where(c == 0, s[0], s[1]).astype(bf16)
        far_o[:, at : at + SLICE] = jnp.where(c == 0, s[2], s[3]).astype(bf16)
        at += SLICE
    for w in narrows:
        v = w[...]
        own_o[:, at : at + v.shape[1]] = v
        far_o[:, at : at + v.shape[1]] = v
        at += v.shape[1]


def pack_acts(wides, narrows):
    n = wides[0].shape[0]
    width = len(wides) * SLICE + sum(a.shape[1] for a in narrows)
    return vmcall(
        functools.partial(pack_kernel, len(wides)), "pack_factors", [], [*wides, *narrows], [],
        [((n, width), bf16)] * 2, [], cost(0, 2e6),
    )


def join_rows_kernel(*refs):
    o, at = refs[-1], 0
    for a in refs[:-1]:
        o[at : at + a.shape[0], :] = a[...]
        at += a.shape[0]


def join_rows(*parts):
    rows = sum(a.shape[0] for a in parts)
    return vmcall(join_rows_kernel, "join_rows", [], parts, [], [((rows, parts[0].shape[1]), bf16)], [], cost(0, 1e6))[0]


def factor_kernel(widths, mine, theirs, *outs):
    c = lax.axis_index("row") & 1
    at = len(widths) * SLICE
    for i, (w, o) in enumerate(zip(widths, outs)):
        wide = mine[:, i * SLICE : (i + 1) * SLICE]
        got = [dot(wide, b[:, at : at + w], TN) for b in (mine, theirs)]
        o[:, :w] = jnp.where(c == 0, got[0], got[1])
        o[:, w:] = jnp.where(c == 0, got[1], got[0])
        at += w


def factor_grads(mine, theirs, widths):
    return vmcall(
        functools.partial(factor_kernel, widths), "factor_grads", [], [mine, theirs], [],
        [((SLICE, 2 * w), f32) for w in widths], [], cost(1e9, 8e6),
    )


def add_kernel(a, b, o):
    o[...] = a[...] + b[...]


def add_rows(a, b):
    return vmcall(add_kernel, "add_sums", [], [a, b], [], [(a.shape, f32)], [], cost(0, 1e5))[0]


def small_kernel(sb, sa, gb, ga, cb, ca, pos, sq, csq, o):
    r, y, _ = axes()
    one = jnp.where((r & 1) + y == 0, 1.0, 0.0)
    rel = jnp.concatenate([sb[...], sa[...]], axis=0)
    total = jnp.sum(sq[...], axis=1, keepdims=True) + jnp.sum(csq[...], axis=1, keepdims=True)
    seg = core_order(rel) + one * jnp.concatenate([gb[...], ga[...]], axis=0)
    rows = jnp.concatenate(
        [seg, one * jnp.concatenate([cb[...], ca[...]], axis=0), jnp.broadcast_to(total, (1, D)), one * pos[...]], axis=0
    )
    h = 2 * SLICE
    o[:25, :] = jnp.where(r >> 1 == 0, rows, jnp.concatenate([rows[:, h:], rows[:, :h]], axis=1))
    o[25:, :] = jnp.zeros((7, D), f32)


def small_sums(*parts):
    return vmcall(small_kernel, "small_sums", [], parts, [], [((32, D), f32)], [], cost(0, 1e5))[0]


def own_kernel(a, o):
    r = lax.axis_index("row")
    v = a[...]
    o[...] = sum(jnp.where(r == q, v[:, q * SLICE : (q + 1) * SLICE], 0.0) for q in range(4))


def own_sums(a):
    return vmcall(own_kernel, "own_sums", [], [a], [], [((32, SLICE), f32)], [], cost(0, 1e5))[0]


def row_swap(k):
    def move(a):
        return lax.ppermute(a, "row", [(i, i ^ k) for i in range(4)])

    return move


to_core = row_swap(1)
to_x = row_swap(2)
ALL = ("dp", "row", "col")


def exchange(a, groups):
    return lax.all_to_all(a, ALL, 0, 0, axis_index_groups=groups, tiled=True)


def spots():
    n = lax.axis_size("dp")
    return lambda z, r, y: (z * 4 + r) * 2 + y, n


def to_rows(a):
    at, n = spots()
    return exchange(a, [[at(z, r, y) for r in range(4)] for z in range(n) for y in range(2)])


def to_plane(a):
    at, n = spots()
    return exchange(a, [[at(z, 2 * x + c, y) for x in range(2) for y in range(2)] for z in range(n) for c in range(2)])


def to_y(a):
    return lax.ppermute(a, "col", [(0, 1), (1, 0)])


def to_z(a, k):
    n = lax.axis_size("dp")
    return lax.ppermute(a, "dp", [(i, i ^ k) for i in range(n)])


def after(a, *first):
    return lax.optimization_barrier((a, *first))[0]


class Order:
    def __init__(self):
        self.last = None

    def __call__(self, fn, *args):
        leaves, tree = jax.tree.flatten(args)
        if self.last is not None:
            leaves = lax.optimization_barrier((*leaves, self.last))[:-1]
        out = fn(*jax.tree.unflatten(tree, leaves))
        self.last = jax.tree.leaves(out)[-1]
        return out


def by_index(i, mine, other, axis):
    return jnp.where(
        i == 0,
        jnp.concatenate([mine, other], axis=axis),
        jnp.concatenate([other, mine], axis=axis),
    )


def group_send(run, a):
    a = run(fold, a, to_core(a))
    return (a, to_y(a))


def gather_all(a):
    return lax.all_gather(a, ("row", "col"), axis=0, tiled=False)


def scatter_all(a):
    return lax.psum_scatter(a.reshape(-1, *a.shape[2:]), ("row", "col"), scatter_dimension=0, tiled=False)


def dp_gather(a):
    n = lax.axis_size("dp")
    if n != 4:
        return (lax.all_gather(a, "dp", axis=0, tiled=True),)
    return (a, to_z(a, 1), to_z(a, 2), to_z(a, 3))


def to_d(a):
    return lax.ppermute(a, ("row", "col"), [(i, i ^ 5) for i in range(8)])


def dp_scatter(run, sums, got, *parts):
    if lax.axis_size("dp") != 4:
        return (lax.psum(sum(p.astype(f32) for p in parts).astype(bf16), "dp"), lax.psum(own_sums(sums + got), "dp"))
    q = run(plane_sum, sums, got, *parts)
    return (q[0], *[to_z(q[k], k) for k in (1, 2, 3)])


def to_depth(a):
    at, n = spots()
    return exchange(a, [[at(z, r, y) for z in range(n)] for r in range(4) for y in range(2)])


def pair_scatter(run, a, fa, b, fb, first):
    if lax.axis_size("dp") != 4:
        return lax.psum(jnp.concatenate([(a + fa).astype(bf16), (b + fb).astype(bf16)]), "dp")
    return to_depth(after(run(lambda *a: pair_call(pair_split_kernel, a, 2 * SLICE, bf16, 1, "pair_split")[0], a, fa, b, fb), first))


def pair_total(run, parts):
    if lax.axis_size("dp") != 4:
        return parts
    return to_depth(run(lambda a: pair_call(pair_sum_kernel, (a,), 2 * SLICE, bf16, 1, "pair_sum")[0], parts))


def pair_result(run, parts):
    if lax.axis_size("dp") != 4:
        a = parts.astype(f32)
        return a[:SLICE], a[SLICE:]
    return run(lambda a: pair_call(pair_place_kernel, (a,), SLICE, f32, 2, "pair_place"), parts)


def dp_quarters(run, quarters):
    if len(quarters) == 2:
        return quarters[:1], quarters[1]
    q, sums = run(quarter_sum, *quarters)
    return (q, *[to_z(q, k) for k in (1, 2, 3)]), sums


def dp_place(run, quarters, cut):
    if len(quarters) == 1:
        a = quarters[0].astype(f32)
        return [a[:, :cut], a[:, cut:]]
    return run(lambda *a: place_quarters(a, cut), *quarters)


def body(
    hidden_in, teacher, lengths, pos_embed,
    seg_qkv, seg_proj, seg_gain1, seg_bias1, seg_up, seg_down, seg_gain2, seg_bias2,
    cross_qkv, cross_proj, cross_gain1, cross_bias1, cross_up, cross_down, cross_gain2, cross_bias2,
):
    run = Order()
    c = lax.axis_index("row") & 1
    n_q, n_o, n_u = seg_qkv.shape[1], seg_proj.shape[1], seg_up.shape[1]
    q_q, q_o, q_u = n_q // 2, n_o // 2, n_u // 2

    vecs = (seg_gain1, seg_bias1, seg_gain2, seg_bias2, cross_gain1, cross_bias1, cross_gain2, cross_bias2)
    wa, xa = run(prep, seg_qkv, seg_proj)
    ax = to_x(xa)
    ay = to_y(wa)
    h = run(token_stack, hidden_in, *vecs, pos_embed)
    ax_ = after(ax, h)
    h = to_rows(h)
    wu = gather_all(after(seg_up, ax))
    az = to_z(ax_, 1)
    ayx = to_y(ax_)
    ac1 = to_core(run(join_rows, wa, ay, ax))
    ayz = to_z(ayx, 1)
    ac2 = to_core(run(join_rows, az, ayx, ayz))
    pa = (wa, ay, ax, az, ayx, ayz, ac1, ac2)
    h, rel, vab, sg1, sb1, sg2, sb2 = run(unstack, h)
    teach = to_rows(run(token_stack, teacher))
    cw_mine, cw_give = run(cross_prep, cross_qkv, cross_proj, cross_up, cross_down)
    wd = gather_all(after(seg_down, h))
    cw_got = to_core(cw_give)
    proj, mix, hat1, inv1, low, hatc1, invc1 = run(attn_fwd, lengths, h, sg1, sb1, pa)
    cw_x = to_x(run(cross_pick, cw_mine, cw_got))
    act, slope = run(ffn_up, after(low, teach), wu)
    hat2, inv2, hatc2, invc2 = run(ffn_down, act, hat1, sg1, sb1, sg2, sb2, wd)
    cw_z = to_z(after(cw_x, hatc2), 1)
    cw = (cw_mine, cw_got, cw_x, cw_z)

    msg = run(cls_message, hatc2, invc2, hatc1, teach)
    msg = run(pair_rows, msg, to_core(msg))
    msgs = (msg, to_y(msg))
    d2, d2_low, dhid, sums_a, sq = run(ffn_back, lengths, hat2, inv2, teach, slope, sg2, sb2, wd)
    m, cproj, cmix, part, v_low = run(lambda *a: cross1(*a, q_q, q_o), lengths, vab, msgs, cw)
    part = group_send(run, part)
    grad_d = run(weight_grad, d2_low, act)
    sum_d = scatter_all(grad_d)
    chat1, cinv1, clow, cact, cslope, part = run(lambda *a: cross2(*a, q_u), vab, m, part, cw)
    part = group_send(run, part)
    grad_u = run(weight_grad, low, dhid)
    sum_u = scatter_all(grad_u)
    cls_out, csq, csums_a, cd2, cd2_low, cdhid, part = run(cross3, lengths, vab, m, chat1, cslope, part, cw)
    part = group_send(run, part)
    d1, sums_b = run(up_back, d2, dhid, hat1, inv1, sg1, wu)
    cd1, cd1_low, csums_b, cdproj, part = run(
        lambda *a: cross4(*a, q_o), lengths, vab, cd2, chat1, cinv1, cproj, part, cw
    )
    part = group_send(run, part)
    outs = run(emit_output, hat2, sg2, sb2, cls_out)
    c_own, c_far = run(pack_acts, (v_low, cd1_low, clow, cd2_low), (cdproj, cmix, cdhid, cact))
    c_far = to_x(c_far)
    pos_part, ssums_a, sd2, sd2_low, slow, sact, sdhid, part = run(cross5, vab, m, cd1, part, wu, wd)
    part = group_send(run, part)
    s_own, s_far = run(pack_acts, (sd2_low, slow), (sact, sdhid))
    s_far = to_x(s_far)
    acts = dp_gather(run(join_rows, c_own, c_far))
    d1c, ssums_b = run(cross6, vab, m, sd2, invc1, part)
    facts = run(join_rows, s_own, s_far)
    facts_c = to_core(facts)
    sums = run(small_sums, sums_b, sums_a, ssums_b, ssums_a, csums_b, csums_a, pos_part, sq, csq)
    dproj1, d1_low, dxp = run(lambda *a: attn_back(1, *a), lengths, proj, d1, d1c, pa)
    f_d, f_u = run(lambda a, b: factor_grads(a, b, (q_u, q_u)), facts, facts_c)
    keep1, send = run(lambda *a: attn_grad(1, *a), h, d1_low, dproj1, mix)
    got1 = to_core(send)
    acts = run(join_rows, *acts) if len(acts) > 1 else acts[0]
    q_f = pair_scatter(run, sum_d, f_d, sum_u, f_u, keep1)
    a_y, a_d = run(chip_half, keep1, got1)
    a_y, a_d = to_y(a_y), to_d(a_d)
    dproj0, dxs = run(lambda *a: attn_back(0, *a), lengths, proj, dxp, d1_low, pa)
    outs = to_rows(after(outs, dproj0))
    sums = run(add_rows, sums, to_core(sums))
    keep0, send = run(lambda *a: attn_grad(0, *a), h, after(d1_low, a_y, a_d), dproj0, mix)
    got0 = to_core(send)
    q_f = pair_total(run, q_f)
    a_0, a_x = run(chip_half, keep0, got0)
    a_x = to_x(a_x)
    acts_c = to_core(after(acts, a_0))
    sums = run(add_rows, sums, to_y(sums))
    q_a = dp_scatter(run, sums, to_x(sums), a_0, a_y, a_x, a_d)
    output = run(token_join, outs)
    g_cqkv, g_cproj, g_cup, g_cdown = run(
        lambda a, b: factor_grads(a, b, (q_q, q_o, q_u, q_u)), acts, acts_c
    )
    g_down, g_up = pair_result(run, q_f)
    q_a, al = dp_quarters(run, q_a)
    dxs = to_rows(after(dxs, g_up, al))
    dx_out = run(token_join, dxs)
    g_qkv, g_proj = dp_place(run, q_a, n_q)
    valid = jnp.sum(lengths).astype(f32)
    loss = al[8, 0] / (2.0 * valid)
    return (
        output, loss, dx_out, al[9:25],
        g_qkv, g_proj, al[0], al[1], g_up, g_down, al[2], al[3],
        g_cqkv, g_cproj, al[4], al[5], g_cup, g_cdown, al[6], al[7],
    )


def solution(mesh):
    wide, cut, one = P("row", ("dp", "col")), P("row", "col"), P("row")
    block = (cut, cut, one, one, cut, cut, one, one)
    in_specs = (wide, wide, P(), P(None, "row")) + block + block
    out_specs = (wide, P(), wide, P(None, "row")) + block + block
    return jax.shard_map(body, mesh=mesh, in_specs=in_specs, out_specs=out_specs, check_vma=False)
```

```python
import functools
import jax
import jax.numpy as jnp
from jax import lax
from jax.experimental import pallas as pl
from jax.experimental.pallas import tpu as pltpu
from jax.sharding import PartitionSpec as P

D = 768
HEAD_DIM = 64
SEG = 128
SEGS = 16
SEQ_LEN = 2048
SLICE = 192
HALF = 96
EPS = 1e-05
NEG = -1e30
ROOT_HALF = 0.7071067811865476
INV_ROOT_TAU = 0.3989422804014327
bf16 = jnp.bfloat16
f32 = jnp.float32
GROUP = 12
GROUP_BACK = 6
COST = 0.005
VMEM_LIMIT = 60 * 1024 * 1024

NN = (((1,), (0,)), ((), ()))
NT = (((1,), (1,)), ((), ()))
TN = (((0,), (0,)), ((), ()))


def scalars(lengths, tok):
    r, y, z = lax.axis_index("row"), lax.axis_index("col"), lax.axis_index("dp")
    return z & 1, lengths[(z * lax.axis_size("col") + y) * 2 + (r >> 1)], (r & 1) * tok


def scale_of(lengths):
    n = lengths.shape[0]
    total = sum(lengths[i] for i in range(n)) if n <= 16 else lax.fori_loop(0, n, lambda i, a: a + lengths[i], 0)
    return (n * SEQ_LEN) / jnp.full((1, 1), total, jnp.int32).astype(f32)


def rel_rows(ref):
    r = lax.axis_index("row")
    return [ref[pl.ds(pl.multiple_of((r ^ k) * SLICE, 16), SLICE), :] for k in range(4)]


def put_rel_rows(ref, a):
    r = lax.axis_index("row")
    for k in range(4):
        ref[pl.ds(pl.multiple_of((r ^ k) * SLICE, 16), SLICE), :] = a[k * SLICE : (k + 1) * SLICE, :]


def dot(a, b, dims):
    return lax.dot_general(a, b, dims, preferred_element_type=f32)


def params(n=1):
    if n == 0:
        return pltpu.CompilerParams(vmem_limit_bytes=VMEM_LIMIT)
    return pltpu.CompilerParams(dimension_semantics=("arbitrary",) * n, vmem_limit_bytes=VMEM_LIMIT)


ANY = pl.BlockSpec(memory_space=pl.ANY)
SMEM = pl.BlockSpec(memory_space=pltpu.SMEM)


def whole(shape):
    return pl.BlockSpec(shape, lambda *_: (0,) * len(shape))


def piece_plan(refs, p):
    own, y1, x1, z1, y2, z2, c1, c2 = refs
    hi = p * HALF
    ho = (1 - p) * HALF
    x, xc = 2 * SLICE, 3 * SLICE
    return [
        (own, 0, SLICE, 0, 0), (c1, 0, SLICE, SLICE, 0),
        (x1, 0, HALF, x + hi, 0), (z1, 0, HALF, x + ho, 0),
        (c1, 2 * SLICE, HALF, xc + hi, 0), (c2, 0, HALF, xc + ho, 0),
        (y1, 0, SLICE, 0, 1), (c1, SLICE, SLICE, SLICE, 1),
        (y2, 0, HALF, x + hi, 1), (z2, 0, HALF, x + ho, 1),
        (c2, HALF, HALF, xc + hi, 1), (c2, 2 * HALF, HALF, xc + ho, 1),
    ]


def piece_copies(refs, dst, sem, p, src_cols, dst_col, base=0):
    lo, n = src_cols
    return [
        pltpu.make_async_copy(
            src.at[pl.ds(at, rows), pl.ds(lo, n)],
            dst.at[pl.ds(pl.multiple_of(row, 16), rows), pl.ds(dst_col(j), n)],
            sem.at[base + i],
        )
        for i, (src, at, rows, row, j) in enumerate(piece_plan(refs, p))
    ]


def half_copies(refs, dst, sem, p, j, src_cols, base=0):
    lo, n = src_cols
    return [
        pltpu.make_async_copy(
            src.at[pl.ds(at, rows), pl.ds(lo, n)], dst.at[pl.ds(pl.multiple_of(row, 16), rows), :], sem.at[base + i]
        )
        for i, (src, at, rows, row, _) in enumerate([a for a in piece_plan(refs, p) if a[4] == j])
    ]


def gathered_copies(ref, dst, sem):
    r = lax.axis_index("row")
    n = ref.shape[2]
    return [
        pltpu.make_async_copy(
            ref.at[(r ^ k) * 2 + j], dst.at[pl.ds(k * SLICE, SLICE), pl.ds(j * n, n)], sem.at[k * 2 + j]
        )
        for k in range(4)
        for j in range(2)
    ]


def norm_cols(resid):
    center = jnp.sum(resid, axis=0, keepdims=True) * (1.0 / D)
    spread = jnp.sum(resid * resid, axis=0, keepdims=True) * (1.0 / D) - center * center
    inv = lax.rsqrt(spread + EPS)
    return (resid - center) * inv, inv


def norm_back_cols(y, hat, inv, g):
    t = y * g
    m1 = jnp.sum(t, axis=0, keepdims=True) * (1.0 / D)
    m2 = jnp.sum(t * hat, axis=0, keepdims=True) * (1.0 / D)
    return inv * (t - m1 - hat * m2)


def probs_group(qs, ks, ok):
    ss = [dot(k, q, TN) for q, k in zip(qs, ks)]
    ss = [jnp.where(ok, s * HEAD_DIM**-0.5, NEG) for s in ss]
    ms = [jnp.max(s, axis=0, keepdims=True) for s in ss]
    es = [jnp.exp(s - m) for s, m in zip(ss, ms)]
    ts = [1.0 / jnp.sum(e, axis=0, keepdims=True) for e in es]
    return [e * t for e, t in zip(es, ts)]


def key_ok_of(scal, b, tile):
    pos = lax.broadcasted_iota(jnp.int32, (SEG, SEG), 0)
    at = scal[2] + pl.program_id(0) * tile + b * SEG
    return (pos + at < scal[1]) | (pos == 0)


def put_cls(tile, hat, inv, hatc_o, invc_o):
    n = tile // SEG
    for b in range(n):
        at = pl.ds(pl.program_id(0) * n + b, 1)
        hatc_o[at, :] = hat[:, b * SEG : (b + 1) * SEG].T[0:1, :]
        invc_o[at, :] = jnp.broadcast_to(inv[:, b * SEG : b * SEG + 1], (1, SEG))


def attn_fwd_kernel(tile, lengths, xs, g1, b1, *rest):
    refs = rest[:8]
    proj_o, mix_o, hat_o, inv_o, low_o, hatc_o, invc_o, w, wo, sem = rest[8:]
    scal = scalars(lengths, tile * pl.num_programs(0))
    n_q = w.shape[1] // 2
    n_o = wo.shape[1] // 2

    @pl.when(pl.program_id(0) == 0)
    def _():
        cps = piece_copies(refs, w, sem, scal[0], (0, n_q), lambda j: j * n_q)
        cps += piece_copies(refs, wo, sem, scal[0], (n_q, n_o), lambda j: j * n_o, 12)
        for c in cps:
            c.start()
        for c in cps:
            c.wait()

    x = jnp.concatenate(rel_rows(xs), axis=0)
    proj_o[...] = dot(w[...], x, TN).astype(bf16)
    for b in range(tile // SEG):
        ok = key_ok_of(scal, b, tile)
        cols = slice(b * SEG, (b + 1) * SEG)
        for h0 in range(0, D // HEAD_DIM, GROUP):
            qkv = [
                [
                    proj_o[(h * 3 + j) * HEAD_DIM : (h * 3 + j + 1) * HEAD_DIM, cols]
                    for j in range(3)
                ]
                for h in range(h0, h0 + GROUP)
            ]
            pts = probs_group([a[0] for a in qkv], [a[1] for a in qkv], ok)
            mixed = [dot(a[2], p.astype(bf16), NN).astype(bf16) for a, p in zip(qkv, pts)]
            mix_o[h0 * HEAD_DIM : (h0 + GROUP) * HEAD_DIM, cols] = jnp.concatenate(mixed, axis=0)
    hat, inv = norm_cols(x.astype(f32) + dot(wo[...], mix_o[...], NN))
    hat_o[...] = hat
    inv_o[...] = inv
    low_o[...] = (hat * g1[...] + b1[...]).astype(bf16)
    put_cls(tile, hat, inv, hatc_o, invc_o)


def attn_fwd(lengths, xs, g1, b1, parts, tile=256):
    t = xs.shape[1]
    n = parts[0].shape[1]
    n_q = n * 3 // 4
    n_o = n - n_q
    colb = lambda rows: pl.BlockSpec((rows, tile), lambda i: (0, i))
    return pl.pallas_call(
        functools.partial(attn_fwd_kernel, tile),
        grid=(t // tile,),
        in_specs=[SMEM, colb(D)] + [whole((D, 1))] * 2 + [ANY] * 8,
        out_specs=[colb(2 * n_q), colb(D), colb(D), colb(1), colb(D), whole((t // SEG, D)), whole((t // SEG, SEG))],
        out_shape=[
            jax.ShapeDtypeStruct((2 * n_q, t), bf16),
            jax.ShapeDtypeStruct((D, t), bf16),
            jax.ShapeDtypeStruct((D, t), f32),
            jax.ShapeDtypeStruct((1, t), f32),
            jax.ShapeDtypeStruct((D, t), bf16),
            jax.ShapeDtypeStruct((t // SEG, D), f32),
            jax.ShapeDtypeStruct((t // SEG, SEG), f32),
        ],
        scratch_shapes=[
            pltpu.VMEM((D, 2 * n_q), bf16),
            pltpu.VMEM((D, 2 * n_o), bf16),
            pltpu.SemaphoreType.DMA((24,)),
        ],
        compiler_params=params(),
        name="seg_attend",
        cost_estimate=cost(2 * t * D * D * 4 + 4 * t * SEG * D, 20 * 1024 * t, t * SEG * 12),
    )(lengths, xs, g1, b1, *parts)


def ffn_up_kernel(low, wg, act_o, slope_o, w, lt, sem):
    i = pl.program_id(0)

    @pl.when(i == 0)
    def _():
        cps = gathered_copies(wg, w, sem)
        for c in cps:
            c.start()
        lt[...] = low[...].T
        for c in cps:
            c.wait()

    wid = act_o.shape[1]
    at = pl.multiple_of(i * wid, 128)
    hidden = dot(lt[...], w[:, pl.ds(at, wid)], NN)
    phi = 0.5 * (1.0 + lax.erf(hidden * ROOT_HALF))
    act_o[...] = (hidden * phi).astype(bf16)
    slope = phi + hidden * jnp.exp(-0.5 * hidden * hidden) * INV_ROOT_TAU
    slope_o[...] = slope.astype(bf16)


def ffn_up(low, wg, wid=512):
    t = low.shape[1]
    n = wg.shape[2] * 2
    colb = pl.BlockSpec((t, wid), lambda i: (0, i))
    return pl.pallas_call(
        ffn_up_kernel,
        grid=(n // wid,),
        in_specs=[whole((D, t)), ANY],
        out_specs=[colb, colb],
        out_shape=[jax.ShapeDtypeStruct((t, n), bf16)] * 2,
        scratch_shapes=[pltpu.VMEM((D, n), bf16), pltpu.VMEM((t, D), bf16), pltpu.SemaphoreType.DMA((12,))],
        compiler_params=params(),
        name="seg_up",
        cost_estimate=cost(2 * t * D * n, 4 * t * n, 2 * t * n),
    )(low, wg)


def ffn_down_kernel(tile, act, hat1, g1, b1, g2, b2, wg, hat_o, inv_o, hatc_o, invc_o, w, sem):
    i = pl.program_id(0)

    @pl.when(i == 0)
    def _():
        cps = gathered_copies(wg, w, sem)
        for c in cps:
            c.start()
        for c in cps:
            c.wait()

    first = hat1[...] * g1[...] + b1[...]
    hat, inv = norm_cols(first + dot(w[...], act[...], NT))
    hat_o[...] = hat
    inv_o[...] = inv
    put_cls(tile, hat, inv, hatc_o, invc_o)


def ffn_down(act, hat1, g1, b1, g2, b2, wg, tile=256):
    t, n = act.shape
    colb = lambda rows: pl.BlockSpec((rows, tile), lambda i: (0, i))
    return pl.pallas_call(
        functools.partial(ffn_down_kernel, tile),
        grid=(t // tile,),
        in_specs=[pl.BlockSpec((tile, n), lambda i: (i, 0)), colb(D)] + [whole((D, 1))] * 4 + [ANY],
        out_specs=[colb(D), colb(1), whole((t // SEG, D)), whole((t // SEG, SEG))],
        out_shape=[
            jax.ShapeDtypeStruct((D, t), f32),
            jax.ShapeDtypeStruct((1, t), f32),
            jax.ShapeDtypeStruct((t // SEG, D), f32),
            jax.ShapeDtypeStruct((t // SEG, SEG), f32),
        ],
        scratch_shapes=[pltpu.VMEM((D, n), bf16), pltpu.SemaphoreType.DMA((12,))],
        compiler_params=params(),
        name="seg_down",
        cost_estimate=cost(2 * t * D * n, 2 * t * n + 8 * t * D, 0),
    )(act, hat1, g1, b1, g2, b2, wg)


def start_all(cps):
    for c in cps:
        c.start()


def wait_all(cps):
    for c in cps:
        c.wait()


def ffn_back_kernel(tile, lengths, hat2, inv2, xs, slope, g2, b2, wg, d2_o, d2low_o, dhid_o, sums_o, sq_o, wd, acc, sem):
    scal = scalars(lengths, tile * pl.num_programs(0))
    i = pl.program_id(0)
    cd = gathered_copies(wg, wd, sem)

    @pl.when(i == 0)
    def _():
        start_all(cd)
        acc[...] = jnp.zeros_like(acc)
        sq_o[...] = jnp.zeros_like(sq_o)

    lane = lax.broadcasted_iota(jnp.int32, (1, tile), 1) + i * tile
    keep = (lane + scal[2] < scal[1]) & (lane % SEG != 0)
    h2 = hat2[...]
    teach = jnp.concatenate(rel_rows(xs), axis=0).astype(f32)
    diff = jnp.where(keep, h2 * g2[...] + b2[...] - teach, 0.0)
    sq_o[...] += jnp.sum(diff * diff, axis=0, keepdims=True)
    y = (diff * scale_of(lengths)).astype(bf16).astype(f32)
    acc[0] += fold_lanes(y * h2)
    acc[1] += fold_lanes(y)
    d2 = norm_back_cols(y, h2, inv2[...], g2[...])
    d2_o[...] = d2
    d2_low = d2.astype(bf16)
    d2low_o[...] = d2_low

    @pl.when(i == 0)
    def _():
        wait_all(cd)

    dhid_o[...] = (dot(d2_low, wd[...], TN) * slope[...].astype(f32)).astype(bf16)
    lane_sums(acc, sums_o)


def fold_lanes(v):
    return sum(v[:, k * SEG : (k + 1) * SEG] for k in range(v.shape[1] // SEG))


def lane_sums(acc, sums_o):
    @pl.when(pl.program_id(0) == pl.num_programs(0) - 1)
    def _():
        for k in range(2):
            sums_o[k : k + 1, :] = jnp.sum(acc[k].T, axis=0, keepdims=True)


def ffn_back(lengths, hat2, inv2, teach, slope, g2, b2, wg, tile=256):
    t, n = slope.shape
    colb = lambda rows: pl.BlockSpec((rows, tile), lambda i: (0, i))
    rowb = pl.BlockSpec((tile, n), lambda i: (i, 0))
    return pl.pallas_call(
        functools.partial(ffn_back_kernel, tile),
        grid=(t // tile,),
        in_specs=[SMEM, colb(D), colb(1), colb(D), rowb] + [whole((D, 1))] * 2 + [ANY],
        out_specs=[colb(D), colb(D), rowb, whole((2, D)), whole((1, tile))],
        out_shape=[
            jax.ShapeDtypeStruct((D, t), f32),
            jax.ShapeDtypeStruct((D, t), bf16),
            jax.ShapeDtypeStruct((t, n), bf16),
            jax.ShapeDtypeStruct((2, D), f32),
            jax.ShapeDtypeStruct((1, tile), f32),
        ],
        scratch_shapes=[
            pltpu.VMEM((D, n), bf16),
            pltpu.VMEM((2, D, SEG), f32),
            pltpu.SemaphoreType.DMA((12,)),
        ],
        compiler_params=params(),
        name="seg_down_back",
        cost_estimate=cost(2 * t * D * n, 6 * t * n),
    )(lengths, hat2, inv2, teach, slope, g2, b2, wg)


def up_back_kernel(tile, d2, dhid, hat1, inv1, g1, wg, d1_o, sums_o, wu, acc, sem):
    i = pl.program_id(0)

    @pl.when(i == 0)
    def _():
        cu = gathered_copies(wg, wu, sem)
        start_all(cu)
        acc[...] = jnp.zeros_like(acc)
        wait_all(cu)

    s = d2[...] + dot(wu[...], dhid[...], NT)
    h1 = hat1[...]
    acc[0] += fold_lanes(s * h1)
    acc[1] += fold_lanes(s)
    d1_o[...] = norm_back_cols(s, h1, inv1[...], g1[...])
    lane_sums(acc, sums_o)


def up_back(d2, dhid, hat1, inv1, g1, wg, tile=256):
    t, n = dhid.shape
    colb = lambda rows: pl.BlockSpec((rows, tile), lambda i: (0, i))
    return pl.pallas_call(
        functools.partial(up_back_kernel, tile),
        grid=(t // tile,),
        in_specs=[colb(D), pl.BlockSpec((tile, n), lambda i: (i, 0)), colb(D), colb(1), whole((D, 1)), ANY],
        out_specs=[colb(D), whole((2, D))],
        out_shape=[jax.ShapeDtypeStruct((D, t), f32), jax.ShapeDtypeStruct((2, D), f32)],
        scratch_shapes=[
            pltpu.VMEM((D, n), bf16),
            pltpu.VMEM((2, D, SEG), f32),
            pltpu.SemaphoreType.DMA((12,)),
        ],
        compiler_params=params(),
        name="seg_up_back",
        cost_estimate=cost(2 * t * D * n, 4 * t * n),
    )(d2, dhid, hat1, inv1, g1, wg)


def norm_back_rows(y, hat, inv, g):
    t = y * g
    m1 = jnp.sum(t, axis=1, keepdims=True) * (1.0 / D)
    m2 = jnp.sum(t * hat, axis=1, keepdims=True) * (1.0 / D)
    return inv * (t - m1 - hat * m2)


def col_of(rows, k):
    n = rows.shape[0]
    pick = lax.broadcasted_iota(jnp.int32, (n, 1), 0) == k
    row = jnp.sum(jnp.where(pick, rows, 0.0), axis=0, keepdims=True)
    return jnp.broadcast_to(row, (SEG, rows.shape[1])).T


def put_rows(a, cls, tile):
    n = tile // SEG
    lane0 = lax.broadcasted_iota(jnp.int32, (1, SEG), 1) == 0
    return jnp.concatenate(
        [
            jnp.where(lane0, col_of(cls[...], pl.program_id(0) * n + b), a[:, b * SEG : (b + 1) * SEG])
            for b in range(n)
        ],
        axis=1,
    )


def attn_back_kernel(tile, j, lengths, proj, d1, cls, *rest):
    scal = scalars(lengths, tile * pl.num_programs(0))
    refs = rest[:8]
    outs, (w, wo, sem) = rest[8:-3], rest[-3:]
    dproj_o = outs[0]
    i = pl.program_id(0)
    n_q, n_o = w.shape[1], wo.shape[1]
    cq = half_copies(refs, w, sem, scal[0], j, (0, n_q))

    @pl.when(i == 0)
    def _():
        co = half_copies(refs, wo, sem, scal[0], j, (n_q, n_o), 6)
        start_all(co)
        start_all(cq)
        wait_all(co)

    d1_all = put_rows(d1[...], cls, tile) if j == 1 else d1[...]
    d1_low = cls[...] if j == 0 else d1_all.astype(bf16)
    dmix = dot(wo[...], d1_low, TN).astype(bf16)
    for b in range(tile // SEG):
        ok = key_ok_of(scal, b, tile)
        cols = slice(b * SEG, (b + 1) * SEG)
        for h0 in range(0, n_o // HEAD_DIM, GROUP_BACK):
            hs = range(h0, h0 + GROUP_BACK)
            part = lambda k: [proj[(h * 3 + k) * HEAD_DIM : (h * 3 + k + 1) * HEAD_DIM, cols] for h in hs]
            qs, ks, vs = part(0), part(1), part(2)
            dms = [dmix[h * HEAD_DIM : (h + 1) * HEAD_DIM, cols] for h in hs]
            ps = probs_group(qs, ks, ok)
            dps = [dot(v, dm, TN) for v, dm in zip(vs, dms)]
            dvs = [dot(dm, p.astype(bf16), NT) for dm, p in zip(dms, ps)]
            inner = [jnp.sum(p * dp, axis=0, keepdims=True) for p, dp in zip(ps, dps)]
            dss = [(p * (dp - a)).astype(bf16) for p, dp, a in zip(ps, dps, inner)]
            dqs = [dot(k, ds, NN) * HEAD_DIM**-0.5 for k, ds in zip(ks, dss)]
            dks = [dot(q, ds, NT) * HEAD_DIM**-0.5 for q, ds in zip(qs, dss)]
            out = [a.astype(bf16) for trio in zip(dqs, dks, dvs) for a in trio]
            dproj_o[h0 * 3 * HEAD_DIM : (h0 + GROUP_BACK) * 3 * HEAD_DIM, cols] = jnp.concatenate(out, axis=0)

    @pl.when(i == 0)
    def _():
        wait_all(cq)

    dx = d1_all + dot(w[...], dproj_o[...], NN)
    if j == 1:
        outs[1][...] = d1_low
        outs[2][...] = dx
    else:
        put_rel_rows(outs[1], dx.astype(bf16))


def attn_back(j, lengths, proj, d1, cls, parts, tile=256):
    t = proj.shape[1]
    n = parts[0].shape[1]
    n_q = n * 3 // 4
    n_o = n - n_q
    colb = lambda rows, k=0: pl.BlockSpec((rows, tile), lambda i: (k, i))
    wide = [((D, t), bf16, D), ((D, t), f32, D)] if j == 1 else [((D, t), bf16, D)]
    return pl.pallas_call(
        functools.partial(attn_back_kernel, tile, j),
        grid=(t // tile,),
        in_specs=[SMEM, colb(n_q, j), colb(D), whole(cls.shape) if j == 1 else colb(D)] + [ANY] * 8,
        out_specs=[colb(n_q)] + [colb(a[2]) for a in wide],
        out_shape=[jax.ShapeDtypeStruct((n_q, t), bf16)] + [jax.ShapeDtypeStruct(a[0], a[1]) for a in wide],
        scratch_shapes=[
            pltpu.VMEM((D, n_q), bf16),
            pltpu.VMEM((D, n_o), bf16),
            pltpu.SemaphoreType.DMA((16,)),
        ],
        compiler_params=params(),
        name="seg_attend_back",
        cost_estimate=cost(t * D * D * 4 + 6 * t * SEG * D, 10 * 1024 * t, t * SEG * 6),
    )(lengths, proj, d1, cls, *parts)


def split_rows(g, keep_o, send_o):
    keep_o[:SLICE, :] = g[:SLICE]
    send_o[:SLICE, :] = g[SLICE : 2 * SLICE]
    keep_o[SLICE:, :] = g[2 * SLICE : 3 * SLICE]
    send_o[SLICE:, :] = g[3 * SLICE :]


def grad_kernel(a, b, o):
    r = lax.axis_index("row")
    g = dot(a[...], b[...], NN).astype(bf16)
    for k in range(4):
        o[r ^ k, 0] = g[k * SLICE : (k + 1) * SLICE]


def weight_grad(a, b, wid=512):
    t, n = b.shape
    q = n // 2 // wid
    return pl.pallas_call(
        grad_kernel,
        grid=(n // wid,),
        in_specs=[whole((D, t)), pl.BlockSpec((t, wid), lambda i: (0, i))],
        out_specs=pl.BlockSpec((4, 1, SLICE, wid), lambda i: (0, i // q, 0, i % q)),
        out_shape=jax.ShapeDtypeStruct((4, 2, SLICE, n // 2), bf16),
        compiler_params=params(),
        name="weight_grad",
        cost_estimate=cost(2 * t * D * n, 2 * (t + D) * n, 0),
    )(a, b)


def attn_grad_kernel(steps_q, xs, low, dproj, mix, keep_o, send_o):
    i = pl.program_id(0)

    @pl.when(i < steps_q)
    def _():
        x = jnp.concatenate(rel_rows(xs), axis=0)
        split_rows(dot(x, dproj[...], NT).astype(bf16), keep_o, send_o)

    @pl.when(i == steps_q)
    def _():
        split_rows(dot(low[...], mix[...], NT).astype(bf16), keep_o, send_o)


def attn_grad(j, xs, low, dproj, mix):
    t = low.shape[1]
    n_q, n_o = dproj.shape[0], mix.shape[0] // 2
    wid = n_o
    q = n_q // wid
    out = pl.BlockSpec((2 * SLICE, wid), lambda i: (0, i))
    return pl.pallas_call(
        functools.partial(attn_grad_kernel, q),
        grid=(q + 1,),
        in_specs=[whole((D, t)), whole((D, t)), pl.BlockSpec((wid, t), lambda i: (jnp.minimum(i, q - 1), 0)),
                  pl.BlockSpec((wid, t), lambda i: (j, 0))],
        out_specs=[out, out],
        out_shape=[jax.ShapeDtypeStruct((2 * SLICE, n_q + n_o), bf16)] * 2,
        compiler_params=params(),
        name="attend_weight_grad",
        cost_estimate=cost(t * D * 4 * D, (t + D) * 4 * D, 0),
    )(xs, low, dproj, mix)


def add4(refs):
    return sum(a[...].astype(f32) for a in refs)


def chip_kernel(k0, g0, k1, g1, o):
    here = (lax.axis_index("row") >> 1) * 2 + lax.axis_index("col")
    for jj, (k, g) in enumerate(((k0, g0), (k1, g1))):
        a = add4((k, g)).astype(bf16)
        for xx in range(2):
            at = pl.multiple_of((here ^ (xx * 2 + jj)) * SLICE, 16)
            o[pl.ds(at, SLICE), :] = a[xx * SLICE : (xx + 1) * SLICE]


def chip_sum(keep, got, wid=768):
    n = keep.shape[1] // 2
    k = n // wid
    lo = pl.BlockSpec((2 * SLICE, wid), lambda i: (0, i))
    hi = pl.BlockSpec((2 * SLICE, wid), lambda i: (0, i + k))
    return pl.pallas_call(
        chip_kernel,
        grid=(k,),
        in_specs=[lo, lo, hi, hi],
        out_specs=pl.BlockSpec((4 * SLICE, wid), lambda i: (0, i)),
        out_shape=jax.ShapeDtypeStruct((4 * SLICE, n), bf16),
        compiler_params=params(),
        name="chip_sum",
        cost_estimate=cost(0, 12 * SLICE * n),
    )(keep, got, keep, got)


def chip_half_kernel(k0, g0, a_o, b_o):
    a = add4((k0, g0)).astype(bf16)
    a_o[...] = a[:SLICE]
    b_o[...] = a[SLICE:]


def chip_half(keep, got, wid=768):
    n = keep.shape[1]
    lo = pl.BlockSpec((2 * SLICE, wid), lambda i: (0, i))
    return pl.pallas_call(
        chip_half_kernel,
        grid=(n // wid,),
        in_specs=[lo, lo],
        out_specs=[pl.BlockSpec((SLICE, wid), lambda i: (0, i))] * 2,
        out_shape=[jax.ShapeDtypeStruct((SLICE, n), bf16)] * 2,
        compiler_params=params(),
        name="chip_sum",
        cost_estimate=cost(0, 6 * SLICE * n),
    )(keep, got)


def add_stacked(refs):
    out = []
    for a in refs:
        for i in range(0, a.shape[0], SLICE):
            out.append(a[i : i + SLICE, :].astype(f32))
    return sum(out)


FEW = 8


def plane_kernel(*refs):
    parts, sums, got, outs, total_s = refs[:-7], refs[-7], refs[-6], refs[-5:-1], refs[-1]
    r = lax.axis_index("row")
    z = lax.axis_index("dp")
    h = outs[0].shape[0] - FEW
    total_s[...] = add_stacked(parts).astype(bf16)
    v = sums[...] + got[...]
    v = sum(jnp.where(r == q, v[:, q * SLICE : (q + 1) * SLICE], 0.0) for q in range(4))
    n = v.shape[0] // FEW
    v = jnp.concatenate([v[n * i : n * (i + 1), :] for i in range(FEW)], axis=1)
    hi = v.astype(bf16)
    both = jnp.concatenate([hi.astype(f32), v - hi.astype(f32)], axis=0).astype(bf16)
    for k, o in enumerate(outs):
        o[:h, :] = total_s[pl.ds(pl.multiple_of((z ^ k) * h, 16), h), :]
        o[h:, :] = both


def plane_sum(sums, got, *parts):
    n = parts[0].shape[1]
    vm = pl.BlockSpec(memory_space=pltpu.VMEM)
    return pl.pallas_call(
        plane_kernel,
        in_specs=[vm] * (len(parts) + 2),
        out_specs=[vm] * 4,
        out_shape=[jax.ShapeDtypeStruct((SLICE // 4 + FEW, n), bf16)] * 4,
        scratch_shapes=[pltpu.VMEM((SLICE, n), bf16)],
        compiler_params=params(0),
        name="plane_sum",
        cost_estimate=cost(0, 10 * SLICE * n),
    )(*parts, sums, got)


def pair_split_kernel(a, fa, b, fb, o):
    va, vb = add4((a, fa)).astype(bf16), add4((b, fb)).astype(bf16)
    h = SLICE // 4
    for q in range(4):
        o[2 * q * h : (2 * q + 1) * h, :] = va[q * h : (q + 1) * h]
        o[(2 * q + 1) * h : (2 * q + 2) * h, :] = vb[q * h : (q + 1) * h]


def pair_sum_kernel(p, o):
    h = p.shape[0] // 4
    v = sum(p[q * h : (q + 1) * h, :].astype(f32) for q in range(4)).astype(bf16)
    for q in range(4):
        o[q * h : (q + 1) * h, :] = v


def pair_place_kernel(p, a_o, b_o):
    h = p.shape[0] // 8
    for q in range(4):
        a_o[q * h : (q + 1) * h, :] = p[2 * q * h : (2 * q + 1) * h, :].astype(f32)
        b_o[q * h : (q + 1) * h, :] = p[(2 * q + 1) * h : (2 * q + 2) * h, :].astype(f32)


def pair_call(kernel, args, rows, dtype, count, name):
    n = args[0].shape[1]
    wid = 512
    spec = lambda m: pl.BlockSpec((m, wid), lambda i: (0, i))
    return pl.pallas_call(
        kernel,
        grid=(n // wid,),
        in_specs=[spec(a.shape[0]) for a in args],
        out_specs=[spec(rows)] * count,
        out_shape=[jax.ShapeDtypeStruct((rows, n), dtype)] * count,
        compiler_params=params(),
        name=name,
        cost_estimate=cost(0, 8 * rows * n),
    )(*args)


def quarter_kernel(*refs):
    parts, q_o, small_o = refs[:-2], refs[-2], refs[-1]
    v = add4(parts)
    h = q_o.shape[0]
    q_o[...] = v[:h].astype(bf16)
    n = FEW // 2
    w = v[h : h + n] + v[h + n :]
    c = small_o.shape[1]
    for i in range(FEW):
        small_o[n * i : n * (i + 1), :] = w[:, c * i : c * (i + 1)]


def quarter_sum(*parts):
    vm = pl.BlockSpec(memory_space=pltpu.VMEM)
    h, n = parts[0].shape
    return pl.pallas_call(
        quarter_kernel,
        in_specs=[vm] * len(parts),
        out_specs=[vm] * 2,
        out_shape=[jax.ShapeDtypeStruct((h - FEW, n), bf16), jax.ShapeDtypeStruct((FEW * FEW // 2, n // FEW), f32)],
        compiler_params=params(0),
        name="quarter_sum",
        cost_estimate=cost(0, 1e6),
    )(*parts)


def place_kernel(cut, p0, p1, p2, p3, *outs):
    z = lax.axis_index("dp")
    h = p0.shape[0]
    for k, p in enumerate((p0, p1, p2, p3)):
        rows = pl.ds(pl.multiple_of((z ^ k) * h, 8), h)
        outs[0][rows, :] = p[:, :cut].astype(f32)
        if len(outs) > 1:
            outs[1][rows, :] = p[:, cut:].astype(f32)


def place_quarters(parts, cut):
    vm = pl.BlockSpec(memory_space=pltpu.VMEM)
    h, n = parts[0].shape
    shapes = [(4 * h, cut)] + ([(4 * h, n - cut)] if cut < n else [])
    return pl.pallas_call(
        functools.partial(place_kernel, cut),
        in_specs=[vm] * 4,
        out_specs=[vm] * len(shapes),
        out_shape=[jax.ShapeDtypeStruct(a, f32) for a in shapes],
        compiler_params=params(0),
        name="place_quarters",
        cost_estimate=cost(0, 2e6),
    )(*parts)


def output_kernel(tile, hat2, g2, b2, cls, o):
    put_rel_rows(o, put_rows(hat2[...] * g2[...] + b2[...], cls, tile).astype(bf16))


def emit_output(hat2, g2, b2, cls, tile=256):
    t = hat2.shape[1]
    colb = lambda rows: pl.BlockSpec((rows, tile), lambda i: (0, i))
    return pl.pallas_call(
        functools.partial(output_kernel, tile),
        grid=(t // tile,),
        in_specs=[colb(D)] + [whole((D, 1))] * 2 + [whole(cls.shape)],
        out_specs=colb(D),
        out_shape=jax.ShapeDtypeStruct((D, t), bf16),
        compiler_params=params(),
        name="emit_output",
        cost_estimate=cost(0, 6 * t * D),
    )(hat2, g2, b2, cls)
def cost(flops, nbytes, trans=0):
    return pl.CostEstimate(flops=int(flops * COST), bytes_accessed=int(nbytes * COST), transcendentals=int(trans * COST))


def vmcall(kernel, name, smem, vmem, anys, outs, scratch, c):
    vm = pl.BlockSpec(memory_space=pltpu.VMEM)
    return pl.pallas_call(
        kernel,
        in_specs=[SMEM] * len(smem) + [vm] * len(vmem) + [ANY] * len(anys),
        out_specs=[vm] * len(outs),
        out_shape=[jax.ShapeDtypeStruct(s, d) for s, d in outs],
        scratch_shapes=scratch,
        compiler_params=params(0),
        name=name,
        cost_estimate=c,
    )(*smem, *vmem, *anys)


def axes():
    r = lax.axis_index("row")
    return r, lax.axis_index("col"), lax.axis_index("dp")


def prep_kernel(qkv, proj, a_o, xa_o):
    p = lax.axis_index("dp") & 1
    n_q = qkv.shape[1]
    half = pl.ds(pl.multiple_of(p * HALF, 16), HALF)
    xa_o[:, :n_q] = qkv[half, :]
    xa_o[:, n_q:] = proj[half, :]
    a_o[:, :n_q] = qkv[...]
    a_o[:, n_q:] = proj[...]


def prep(qkv, proj):
    n = qkv.shape[1] + proj.shape[1]
    return vmcall(
        prep_kernel, "prep_weights", [], [qkv, proj], [], [((SLICE, n), bf16), ((HALF, n), bf16)], [], cost(0, 2e6),
    )


VEC = 32


def stack_kernel(x, *rest):
    vecs, o = rest[:-1], rest[-1]
    t = o.shape[1]
    rows = o.shape[0] // 4
    for q in range(4):
        o[q * rows : q * rows + SLICE, :] = x[:, q * t : (q + 1) * t]
    if vecs:
        v = jnp.concatenate([a[...].reshape(1, SLICE).astype(f32) for a in vecs[:-1]] + [vecs[-1][...].astype(f32)], axis=0)
        v = jnp.concatenate([v, jnp.zeros((VEC - v.shape[0], SLICE), f32)], axis=0).astype(bf16)
        for q in range(4):
            o[q * rows + SLICE : (q + 1) * rows, :SLICE] = v
            o[q * rows + SLICE : (q + 1) * rows, SLICE:] = jnp.zeros((VEC, t - SLICE), bf16)


def token_stack(x, *vecs):
    rows = SLICE + (VEC if vecs else 0)
    return vmcall(
        stack_kernel, "token_stack", [], [x, *vecs], [], [((4 * rows, x.shape[1] // 4), bf16)], [], cost(0, 3e6)
    )[0]


def join_kernel(p, o):
    t = p.shape[1]
    for q in range(4):
        o[:, q * t : (q + 1) * t] = p[q * SLICE : (q + 1) * SLICE, :]


def token_join(p):
    return vmcall(join_kernel, "token_join", [], [p], [], [((SLICE, 4 * p.shape[1]), bf16)], [], cost(0, 3e6))[0]


def cross_prep_kernel(qkv, proj, up, down, mine_o, give_o):
    c = lax.axis_index("row") & 1
    at = 0
    for w in (qkv, proj, up, down):
        q = w.shape[1] // 2
        a, b = w[:, :q].astype(f32), w[:, q:].astype(f32)
        mine_o[:, at : at + q] = jnp.where(c == 0, a, b).astype(bf16)
        give_o[:, at : at + q] = jnp.where(c == 0, b, a).astype(bf16)
        at += q


def cross_prep(qkv, proj, up, down):
    vm = pl.BlockSpec(memory_space=pltpu.VMEM)
    n = (qkv.shape[1] + proj.shape[1] + up.shape[1] + down.shape[1]) // 2
    return pl.pallas_call(
        cross_prep_kernel,
        in_specs=[vm] * 4,
        out_specs=[vm] * 2,
        out_shape=[jax.ShapeDtypeStruct((SLICE, n), bf16)] * 2,
        compiler_params=params(0),
        name="cross_prep",
        cost_estimate=cost(0, 4e6),
    )(qkv, proj, up, down)


def pick_kernel(mine, got, o):
    c, p = lax.axis_index("row") & 1, lax.axis_index("dp") & 1

    @pl.when(c == p)
    def _():
        o[...] = mine[...]

    @pl.when(c != p)
    def _():
        o[...] = got[...]


def cross_pick(mine, got):
    vm = pl.BlockSpec(memory_space=pltpu.VMEM)
    return pl.pallas_call(
        pick_kernel,
        in_specs=[vm] * 2,
        out_specs=vm,
        out_shape=jax.ShapeDtypeStruct(mine.shape, bf16),
        compiler_params=params(0),
        name="cross_pick",
        cost_estimate=cost(0, 3e6),
    )(mine, got)


def swap_cores(v):
    s = SLICE
    return jnp.concatenate([v[:, s : 2 * s], v[:, :s], v[:, 3 * s :], v[:, 2 * s : 3 * s]], axis=1)


def core_order(v):
    c = lax.axis_index("row") & 1
    return jnp.where(c == 0, v, swap_cores(v))


def vec_kernel(h, x_o, rel_o, abs_o, c0, c1, c2, c3):
    rows = h.shape[0] // 4
    for q in range(4):
        x_o[q * SLICE : (q + 1) * SLICE, :] = h[q * rows : q * rows + SLICE, :]
    r = lax.axis_index("row")
    part = [
        h[pl.ds(pl.multiple_of((r ^ k) * rows + SLICE, 16), VEC), :][:, : 2 * SEG].astype(f32)[:24, :SLICE] for k in range(4)
    ]
    rel = jnp.concatenate(part, axis=1)
    rel_o[...] = rel
    abs_o[...] = core_order(rel)
    cols = rel[:8].T
    for i, o in enumerate((c0, c1, c2, c3)):
        o[...] = cols[:, i : i + 1]


def unstack(h):
    n = 8 + SEGS
    return vmcall(
        vec_kernel, "unstack", [], [h], [],
        [((D, h.shape[1]), bf16)] + [((n, D), f32)] * 2 + [((D, 1), f32)] * 4, [], cost(0, 3e6),
    )


H2, H1, TE, IV = slice(0, D), slice(D, 2 * D), slice(2 * D, 3 * D), slice(3 * D, 3 * D + SEG)
MSG = 3 * D + SEG


def msg_kernel(hat2, inv2, hat1, teach, o):
    n = hat2.shape[0]
    o[:, H2] = core_order(hat2[...])
    o[:, H1] = core_order(hat1[...])
    o[:, IV] = inv2[...]
    rows = []
    parts = rel_rows(teach)
    for b in range(n):
        at = slice(b * SEG, (b + 1) * SEG)
        rows.append(jnp.concatenate([t[:, at].astype(f32).T[0:1, :] for t in parts], axis=1))
    o[:, TE] = core_order(jnp.concatenate(rows, axis=0))


def cls_message(hat2, inv2, hat1, teach):
    vm = pl.BlockSpec(memory_space=pltpu.VMEM)
    return pl.pallas_call(
        msg_kernel,
        in_specs=[vm] * 4,
        out_specs=vm,
        out_shape=jax.ShapeDtypeStruct((hat2.shape[0], MSG), f32),
        compiler_params=params(0),
        name="cls_message",
        cost_estimate=cost(0, 2e6),
    )(hat2, inv2, hat1, teach)


def pair_kernel(a, b, o):
    n = a.shape[0]
    c = lax.axis_index("row") & 1
    o[pl.ds(pl.multiple_of(c * n, 8), n), :] = a[...]
    o[pl.ds(pl.multiple_of((1 - c) * n, 8), n), :] = b[...]


def pair_rows(a, b):
    return vmcall(pair_kernel, "core_pair", [], [a, b], [], [((2 * a.shape[0], a.shape[1]), a.dtype)], [], cost(0, 1e6))[0]


def fold_kernel(a, b, o):
    o[...] = add4((a, b)).astype(o.dtype)


def fold(a, b):
    return vmcall(fold_kernel, "core_fold", [], [a, b], [], [(a.shape, a.dtype)], [], cost(0, 1e5))[0]


def cross_copies(refs, dst, sem, lo, n, base=0):
    c, p = lax.axis_index("row") & 1, lax.axis_index("dp") & 1
    at = [c * SLICE, (1 - c) * SLICE, 2 * SLICE + p * SLICE, 2 * SLICE + (1 - p) * SLICE]
    return [
        pltpu.make_async_copy(
            src.at[:, pl.ds(lo, n)], dst.at[pl.ds(pl.multiple_of(row, 16), SLICE), :], sem.at[base + i]
        )
        for i, (src, row) in enumerate(zip(refs, at))
    ]


def norm_rows(resid):
    center = jnp.sum(resid, axis=1, keepdims=True) * (1.0 / D)
    spread = jnp.sum(resid * resid, axis=1, keepdims=True) * (1.0 / D) - center * center
    inv = lax.rsqrt(spread + EPS)
    return (resid - center) * inv, inv


def total(parts):
    return sum(p[...].astype(f32) for p in parts)


def cls_rows(vec, m):
    pos = vec[8 : 8 + SEGS, :]
    return m[:, H2] * vec[2:3, :] + vec[3:4, :] + jnp.concatenate([pos] * (m.shape[0] // SEGS), axis=0)


def cross_probs(cproj, lens):
    n = cproj.shape[0]
    qi = lax.broadcasted_iota(jnp.int32, (n, n), 0)
    ki = lax.broadcasted_iota(jnp.int32, (n, n), 1)
    limit = jnp.where(ki < SEGS, lens[0], lens[1])
    ok = (qi // SEGS == ki // SEGS) & ((ki % SEGS) * SEG < limit)
    out = []
    for h in range(cproj.shape[1] // (3 * HEAD_DIM)):
        q, k, v = [cproj[:, (3 * h + j) * HEAD_DIM : (3 * h + j + 1) * HEAD_DIM] for j in range(3)]
        s = jnp.where(ok, dot(q, k, NT) * HEAD_DIM**-0.5, NEG)
        e = jnp.exp(s - jnp.max(s, axis=1, keepdims=True))
        out.append((q, k, v, e / jnp.sum(e, axis=1, keepdims=True)))
    return out


def group_lens(lengths, rows):
    r, _, z = axes()
    here = lax.axis_size("col")
    return [lengths[(z * here + j) * 2 + (r >> 1)] for j in range(2)]


def cross1_kernel(lengths, vec, m0, m1, *rest):
    refs = rest[:4]
    m_o, cproj_o, cmix_o, part_o, vlow_o, w, sem = rest[4:]
    _, y, _ = axes()
    n_q = cproj_o.shape[1]
    cps = cross_copies(refs, w, sem, 0, w.shape[1])
    start_all(cps)
    n = m0.shape[0]
    for m, yy in ((m0, y), (m1, 1 - y)):
        m_o[pl.ds(pl.multiple_of(yy * n, 8), n), :] = m[...]
    v_low = cls_rows(vec[...], m_o[...]).astype(bf16)
    vlow_o[...] = v_low
    wait_all(cps)
    cproj = dot(v_low, w[:, :n_q], NN).astype(bf16)
    cproj_o[...] = cproj
    mix = [dot(p.astype(bf16), v, NN) for _, _, v, p in cross_probs(cproj, group_lens(lengths, None))]
    mix = jnp.concatenate(mix, axis=1).astype(bf16)
    cmix_o[...] = mix
    part_o[...] = dot(mix, w[:, n_q:], NT).astype(bf16)


def cross1(lengths, vec, msgs, refs, n_q, n_o):
    n = 2 * msgs[0].shape[0]
    return vmcall(
        cross1_kernel, "cross_attend", [lengths], [vec, *msgs], refs,
        [((n, MSG), f32), ((n, n_q), bf16), ((n, n_o), bf16), ((n, D), bf16), ((n, D), bf16)],
        [pltpu.VMEM((D, n_q + n_o), bf16), pltpu.SemaphoreType.DMA((4,))],
        cost(2e7, 2e6),
    )


def cross2_kernel(vec, m, p0, p1, *rest):
    refs = rest[:4]
    hat_o, inv_o, low_o, act_o, slope_o, part_o, wu, wd, sem = rest[4:]
    n = wu.shape[1]
    lo = refs[0].shape[1] - 2 * n
    cps = cross_copies(refs, wu, sem, lo, n) + cross_copies(refs, wd, sem, lo + n, n, 4)
    start_all(cps)
    hat, inv = norm_rows(cls_rows(vec[...], m[...]) + total((p0, p1)))
    hat_o[...] = hat
    inv_o[...] = jnp.broadcast_to(inv, inv_o.shape)
    low = (hat * vec[4:5, :] + vec[5:6, :]).astype(bf16)
    low_o[...] = low
    wait_all(cps)
    hidden = dot(low, wu[...], NN)
    phi = 0.5 * (1.0 + lax.erf(hidden * ROOT_HALF))
    act = (hidden * phi).astype(bf16)
    act_o[...] = act
    slope_o[...] = phi + hidden * jnp.exp(-0.5 * hidden * hidden) * INV_ROOT_TAU
    part_o[...] = dot(act, wd[...], NT).astype(bf16)


def cross2(vec, m, parts, refs, n_u):
    n = m.shape[0]
    return vmcall(
        cross2_kernel, "cross_ffn", [], [vec, m, *parts], refs,
        [((n, D), f32), ((n, SEG), f32), ((n, D), bf16), ((n, n_u), bf16), ((n, n_u), f32), ((n, D), bf16)],
        [pltpu.VMEM((D, n_u), bf16)] * 2 + [pltpu.SemaphoreType.DMA((8,))],
        cost(2e7, 3e6),
    )


def own_rows(ref, n):
    r, y, _ = axes()
    return ref[pl.ds(pl.multiple_of((y * 2 + (r & 1)) * n, 8), n), :]


def cross3_kernel(lengths, vec, m, hat1, slope, p0, p1, *rest):
    refs = rest[:4]
    cls_o, sq_o, sums_o, d2_o, d2low_o, dhid_o, part_o, wu, wd, keep, sem = rest[4:]
    n = wu.shape[1]
    lo = refs[0].shape[1] - 2 * n
    cps = cross_copies(refs, wu, sem, lo, n) + cross_copies(refs, wd, sem, lo + n, n, 4)
    start_all(cps)
    first = hat1[...] * vec[4:5, :] + vec[5:6, :]
    hat2, inv2 = norm_rows(first + total((p0, p1)))
    out = hat2 * vec[6:7, :] + vec[7:8, :]
    rows = out.shape[0]
    ti = lax.broadcasted_iota(jnp.int32, (rows, 1), 0)
    lens = group_lens(lengths, rows)
    live = (ti % SEGS) * SEG < jnp.where(ti < SEGS, lens[0], lens[1])
    diff = jnp.where(live, out - m[:, TE], 0.0)
    k = cls_o.shape[0]
    keep[...] = out
    cls_o[...] = core_order(own_rows(keep, k))
    keep[...] = diff
    mine = own_rows(keep, k)
    sq_o[...] = jnp.sum(mine * mine, axis=0, keepdims=True)
    yv = diff * scale_of(lengths)
    sums_o[0:1, :] = jnp.sum(yv * hat2, axis=0, keepdims=True)
    sums_o[1:2, :] = jnp.sum(yv, axis=0, keepdims=True)
    d2 = norm_back_rows(yv, hat2, inv2, vec[6:7, :])
    d2_o[...] = d2
    d2_low = d2.astype(bf16)
    d2low_o[...] = d2_low
    wait_all(cps)
    dhid = (dot(d2_low, wd[...], NN) * slope[...]).astype(bf16)
    dhid_o[...] = dhid
    part_o[...] = dot(dhid, wu[...], NT).astype(bf16)


def cross3(lengths, vec, m, hat1, slope, parts, refs):
    n, n_u = slope.shape
    return vmcall(
        cross3_kernel, "cross_ffn_back", [lengths], [vec, m, hat1, slope, *parts], refs,
        [((n // 4, D), f32), ((1, D), f32), ((2, D), f32), ((n, D), f32), ((n, D), bf16), ((n, n_u), bf16), ((n, D), bf16)],
        [pltpu.VMEM((D, n_u), bf16)] * 2 + [pltpu.VMEM((n, D), f32), pltpu.SemaphoreType.DMA((8,))],
        cost(2e7, 3e6),
    )


def cross4_kernel(lengths, vec, d2, hat1, inv1, cproj, p0, p1, *rest):
    refs = rest[:4]
    d1_o, d1low_o, sums_o, dproj_o, part_o, w, sem = rest[4:]
    n_q = dproj_o.shape[1]
    cps = cross_copies(refs, w, sem, 0, w.shape[1])
    start_all(cps)
    s = d2[...] + total((p0, p1))
    h1 = hat1[...]
    sums_o[0:1, :] = jnp.sum(s * h1, axis=0, keepdims=True)
    sums_o[1:2, :] = jnp.sum(s, axis=0, keepdims=True)
    d1 = norm_back_rows(s, h1, inv1[:, 0:1], vec[4:5, :])
    d1_o[...] = d1
    d1_low = d1.astype(bf16)
    d1low_o[...] = d1_low
    wait_all(cps)
    dmix = dot(d1_low, w[:, n_q:], NN).astype(bf16)
    outs = []
    for h, (q, k, v, p) in enumerate(cross_probs(cproj[...], group_lens(lengths, None))):
        dm = dmix[:, h * HEAD_DIM : (h + 1) * HEAD_DIM]
        dv = dot(p.astype(bf16), dm, TN)
        dp = dot(dm, v, NT)
        ds = (p * (dp - jnp.sum(p * dp, axis=1, keepdims=True))).astype(bf16)
        outs += [dot(ds, k, NN) * HEAD_DIM**-0.5, dot(ds, q, TN) * HEAD_DIM**-0.5, dv]
    dproj = jnp.concatenate(outs, axis=1).astype(bf16)
    dproj_o[...] = dproj
    part_o[...] = dot(dproj, w[:, :n_q], NT).astype(bf16)


def cross4(lengths, vec, d2, hat1, inv1, cproj, parts, refs, n_o):
    n, n_q = cproj.shape
    return vmcall(
        cross4_kernel, "cross_attend_back", [lengths], [vec, d2, hat1, inv1, cproj, *parts], refs,
        [((n, D), f32), ((n, D), bf16), ((2, D), f32), ((n, n_q), bf16), ((n, D), bf16)],
        [pltpu.VMEM((D, n_q + n_o), bf16), pltpu.SemaphoreType.DMA((4,))],
        cost(2e7, 2e6),
    )


def quarter_copies(ref, dst, sem, base=0):
    r, y, _ = axes()
    n = dst.shape[1]
    cols = pl.ds(pl.multiple_of((r & 1) * n, 128), n)
    return [
        pltpu.make_async_copy(
            ref.at[(((r >> 1) ^ (s >> 1)) * 2 + (s & 1)) * 2 + y, :, cols],
            dst.at[pl.ds(s * SLICE, SLICE), :],
            sem.at[base + s],
        )
        for s in range(4)
    ]


def cross5_kernel(vec, m, d1, p0, p1, *rest):
    ups, downs, pos_o, sums_o, d2_o, d2low_o, low_o, act_o, dhid_o, part_o, wu, wd, sem = rest
    cps = quarter_copies(ups, wu, sem) + quarter_copies(downs, wd, sem, 4)
    start_all(cps)
    dcls = d1[...] + total((p0, p1))
    pos_o[...] = sum(dcls[i : i + SEGS] for i in range(0, dcls.shape[0], SEGS))
    yv = dcls.astype(bf16).astype(f32)
    h2 = m[:, H2]
    sums_o[0:1, :] = jnp.sum(yv * h2, axis=0, keepdims=True)
    sums_o[1:2, :] = jnp.sum(yv, axis=0, keepdims=True)
    d2 = norm_back_rows(yv, h2, m[:, 3 * D : 3 * D + 1], vec[2:3, :])
    d2_o[...] = d2
    d2_low = d2.astype(bf16)
    d2low_o[...] = d2_low
    low = (m[:, H1] * vec[0:1, :] + vec[1:2, :]).astype(bf16)
    low_o[...] = low
    wait_all(cps)
    hidden = dot(low, wu[...], NN)
    phi = 0.5 * (1.0 + lax.erf(hidden * ROOT_HALF))
    act_o[...] = (hidden * phi).astype(bf16)
    slope = phi + hidden * jnp.exp(-0.5 * hidden * hidden) * INV_ROOT_TAU
    dhid = (dot(d2_low, wd[...], NN) * slope).astype(bf16)
    dhid_o[...] = dhid
    part_o[...] = dot(dhid, wu[...], NT).astype(bf16)


def cross5(vec, m, d1, parts, ups, downs):
    n = m.shape[0]
    n_u = ups.shape[2] // 2
    return vmcall(
        cross5_kernel, "cls_ffn_back", [], [vec, m, d1, *parts], [ups, downs],
        [((SEGS, D), f32), ((2, D), f32), ((n, D), f32), ((n, D), bf16), ((n, D), bf16), ((n, n_u), bf16),
         ((n, n_u), bf16), ((n, D), bf16)],
        [pltpu.VMEM((D, n_u), bf16)] * 2 + [pltpu.SemaphoreType.DMA((12,))],
        cost(3e7, 3e6),
    )


def cross6_kernel(vec, m, d2, inv1, p0, p1, d1_o, sums_o, keep):
    s = d2[...] + total((p0, p1))
    h1 = m[:, H1]
    sums_o[0:1, :] = jnp.sum(s * h1, axis=0, keepdims=True)
    sums_o[1:2, :] = jnp.sum(s, axis=0, keepdims=True)
    n = d1_o.shape[0]
    keep[...] = s
    mine = own_rows(keep, n)
    keep[...] = h1
    d1_o[...] = core_order(norm_back_rows(mine, own_rows(keep, n), inv1[:, 0:1], vec[0:1, :]))


def cross6(vec, m, d2, inv1, parts):
    n = m.shape[0]
    return vmcall(
        cross6_kernel, "cls_norm_back", [], [vec, m, d2, inv1, *parts], [],
        [((n // 4, D), f32), ((2, D), f32)], [pltpu.VMEM((n, D), f32)], cost(0, 1e6),
    )


def pack_kernel(count, *refs):
    wides, narrows, (own_o, far_o) = refs[:count], refs[count:-2], refs[-2:]
    c = lax.axis_index("row") & 1
    at = 0
    for w in wides:
        v = w[...].astype(f32)
        s = [v[:, i * SLICE : (i + 1) * SLICE] for i in range(4)]
        own_o[:, at : at + SLICE] = jnp.where(c == 0, s[0], s[1]).astype(bf16)
        far_o[:, at : at + SLICE] = jnp.where(c == 0, s[2], s[3]).astype(bf16)
        at += SLICE
    for w in narrows:
        v = w[...]
        own_o[:, at : at + v.shape[1]] = v
        far_o[:, at : at + v.shape[1]] = v
        at += v.shape[1]


def pack_acts(wides, narrows):
    n = wides[0].shape[0]
    width = len(wides) * SLICE + sum(a.shape[1] for a in narrows)
    return vmcall(
        functools.partial(pack_kernel, len(wides)), "pack_factors", [], [*wides, *narrows], [],
        [((n, width), bf16)] * 2, [], cost(0, 2e6),
    )


def join_rows_kernel(*refs):
    o, at = refs[-1], 0
    for a in refs[:-1]:
        o[at : at + a.shape[0], :] = a[...]
        at += a.shape[0]


def join_rows(*parts):
    rows = sum(a.shape[0] for a in parts)
    return vmcall(join_rows_kernel, "join_rows", [], parts, [], [((rows, parts[0].shape[1]), bf16)], [], cost(0, 1e6))[0]


def factor_kernel(widths, mine, theirs, *outs):
    c = lax.axis_index("row") & 1
    at = len(widths) * SLICE
    for i, (w, o) in enumerate(zip(widths, outs)):
        wide = mine[:, i * SLICE : (i + 1) * SLICE]
        got = [dot(wide, b[:, at : at + w], TN) for b in (mine, theirs)]
        o[:, :w] = jnp.where(c == 0, got[0], got[1])
        o[:, w:] = jnp.where(c == 0, got[1], got[0])
        at += w


def factor_grads(mine, theirs, widths):
    return vmcall(
        functools.partial(factor_kernel, widths), "factor_grads", [], [mine, theirs], [],
        [((SLICE, 2 * w), f32) for w in widths], [], cost(1e9, 8e6),
    )


def add_kernel(a, b, o):
    o[...] = a[...] + b[...]


def add_rows(a, b):
    return vmcall(add_kernel, "add_sums", [], [a, b], [], [(a.shape, f32)], [], cost(0, 1e5))[0]


def small_kernel(sb, sa, gb, ga, cb, ca, pos, sq, csq, o):
    r, y, _ = axes()
    one = jnp.where((r & 1) + y == 0, 1.0, 0.0)
    rel = jnp.concatenate([sb[...], sa[...]], axis=0)
    total = jnp.sum(sq[...], axis=1, keepdims=True) + jnp.sum(csq[...], axis=1, keepdims=True)
    seg = core_order(rel) + one * jnp.concatenate([gb[...], ga[...]], axis=0)
    rows = jnp.concatenate(
        [seg, one * jnp.concatenate([cb[...], ca[...]], axis=0), jnp.broadcast_to(total, (1, D)), one * pos[...]], axis=0
    )
    h = 2 * SLICE
    o[:25, :] = jnp.where(r >> 1 == 0, rows, jnp.concatenate([rows[:, h:], rows[:, :h]], axis=1))
    o[25:, :] = jnp.zeros((7, D), f32)


def small_sums(*parts):
    return vmcall(small_kernel, "small_sums", [], parts, [], [((32, D), f32)], [], cost(0, 1e5))[0]


def own_kernel(a, o):
    r = lax.axis_index("row")
    v = a[...]
    o[...] = sum(jnp.where(r == q, v[:, q * SLICE : (q + 1) * SLICE], 0.0) for q in range(4))


def own_sums(a):
    return vmcall(own_kernel, "own_sums", [], [a], [], [((32, SLICE), f32)], [], cost(0, 1e5))[0]


def row_swap(k):
    def move(a):
        return lax.ppermute(a, "row", [(i, i ^ k) for i in range(4)])

    return move


to_core = row_swap(1)
to_x = row_swap(2)
ALL = ("dp", "row", "col")


def exchange(a, groups):
    return lax.all_to_all(a, ALL, 0, 0, axis_index_groups=groups, tiled=True)


def spots():
    n = lax.axis_size("dp")
    return lambda z, r, y: (z * 4 + r) * 2 + y, n


def to_rows(a):
    at, n = spots()
    return exchange(a, [[at(z, r, y) for r in range(4)] for z in range(n) for y in range(2)])


def to_plane(a):
    at, n = spots()
    return exchange(a, [[at(z, 2 * x + c, y) for x in range(2) for y in range(2)] for z in range(n) for c in range(2)])


def to_y(a):
    return lax.ppermute(a, "col", [(0, 1), (1, 0)])


def to_z(a, k):
    n = lax.axis_size("dp")
    return lax.ppermute(a, "dp", [(i, i ^ k) for i in range(n)])


def after(a, *first):
    return lax.optimization_barrier((a, *first))[0]


class Order:
    def __init__(self):
        self.last = None

    def __call__(self, fn, *args):
        leaves, tree = jax.tree.flatten(args)
        if self.last is not None:
            leaves = lax.optimization_barrier((*leaves, self.last))[:-1]
        out = fn(*jax.tree.unflatten(tree, leaves))
        self.last = jax.tree.leaves(out)[-1]
        return out


def by_index(i, mine, other, axis):
    return jnp.where(
        i == 0,
        jnp.concatenate([mine, other], axis=axis),
        jnp.concatenate([other, mine], axis=axis),
    )


def group_send(run, a):
    a = run(fold, a, to_core(a))
    return (a, to_y(a))


def gather_all(a):
    return lax.all_gather(a, ("row", "col"), axis=0, tiled=False)


def scatter_all(a):
    return lax.psum_scatter(a.reshape(-1, *a.shape[2:]), ("row", "col"), scatter_dimension=0, tiled=False)


def dp_gather(a):
    n = lax.axis_size("dp")
    if n != 4:
        return (lax.all_gather(a, "dp", axis=0, tiled=True),)
    return (a, to_z(a, 1), to_z(a, 2), to_z(a, 3))


def to_d(a):
    return lax.ppermute(a, ("row", "col"), [(i, i ^ 5) for i in range(8)])


def dp_scatter(run, sums, got, *parts):
    if lax.axis_size("dp") != 4:
        return (lax.psum(sum(p.astype(f32) for p in parts).astype(bf16), "dp"), lax.psum(own_sums(sums + got), "dp"))
    q = run(plane_sum, sums, got, *parts)
    return (q[0], *[to_z(q[k], k) for k in (1, 2, 3)])


def to_depth(a):
    at, n = spots()
    return exchange(a, [[at(z, r, y) for z in range(n)] for r in range(4) for y in range(2)])


def pair_scatter(run, a, fa, b, fb, first):
    if lax.axis_size("dp") != 4:
        return lax.psum(jnp.concatenate([(a + fa).astype(bf16), (b + fb).astype(bf16)]), "dp")
    return to_depth(after(run(lambda *a: pair_call(pair_split_kernel, a, 2 * SLICE, bf16, 1, "pair_split")[0], a, fa, b, fb), first))


def pair_total(run, parts):
    if lax.axis_size("dp") != 4:
        return parts
    return run(lambda a: pair_call(pair_sum_kernel, (a,), 2 * SLICE, bf16, 1, "pair_sum")[0], parts)


def pair_result(run, parts):
    if lax.axis_size("dp") != 4:
        a = parts.astype(f32)
        return a[:SLICE], a[SLICE:]
    return run(lambda a: pair_call(pair_place_kernel, (a,), SLICE, f32, 2, "pair_place"), parts)


def dp_quarters(run, quarters):
    if len(quarters) == 2:
        return quarters[:1], quarters[1]
    q, sums = run(quarter_sum, *quarters)
    return (q, *[to_z(q, k) for k in (1, 2, 3)]), sums


def dp_place(run, quarters, cut):
    if len(quarters) == 1:
        a = quarters[0].astype(f32)
        return [a[:, :cut], a[:, cut:]]
    return run(lambda *a: place_quarters(a, cut), *quarters)


def body(
    hidden_in, teacher, lengths, pos_embed,
    seg_qkv, seg_proj, seg_gain1, seg_bias1, seg_up, seg_down, seg_gain2, seg_bias2,
    cross_qkv, cross_proj, cross_gain1, cross_bias1, cross_up, cross_down, cross_gain2, cross_bias2,
):
    run = Order()
    c = lax.axis_index("row") & 1
    n_q, n_o, n_u = seg_qkv.shape[1], seg_proj.shape[1], seg_up.shape[1]
    q_q, q_o, q_u = n_q // 2, n_o // 2, n_u // 2

    vecs = (seg_gain1, seg_bias1, seg_gain2, seg_bias2, cross_gain1, cross_bias1, cross_gain2, cross_bias2)
    wa, xa = run(prep, seg_qkv, seg_proj)
    ax = to_x(xa)
    ay = to_y(wa)
    h = run(token_stack, hidden_in, *vecs, pos_embed)
    ax_ = after(ax, h)
    h = to_rows(h)
    wu = gather_all(after(seg_up, ax))
    az = to_z(ax_, 1)
    ayx = to_y(ax_)
    ac1 = to_core(run(join_rows, wa, ay, ax))
    ayz = to_z(ayx, 1)
    ac2 = to_core(run(join_rows, az, ayx, ayz))
    pa = (wa, ay, ax, az, ayx, ayz, ac1, ac2)
    h, rel, vab, sg1, sb1, sg2, sb2 = run(unstack, h)
    teach = to_rows(run(token_stack, teacher))
    cw_mine, cw_give = run(cross_prep, cross_qkv, cross_proj, cross_up, cross_down)
    wd = gather_all(after(seg_down, h))
    cw_got = to_core(cw_give)
    proj, mix, hat1, inv1, low, hatc1, invc1 = run(attn_fwd, lengths, h, sg1, sb1, pa)
    cw_x = to_x(run(cross_pick, cw_mine, cw_got))
    act, slope = run(ffn_up, after(low, teach), wu)
    hat2, inv2, hatc2, invc2 = run(ffn_down, act, hat1, sg1, sb1, sg2, sb2, wd)
    cw_z = to_z(after(cw_x, hatc2), 1)
    cw = (cw_mine, cw_got, cw_x, cw_z)

    msg = run(cls_message, hatc2, invc2, hatc1, teach)
    msg = run(pair_rows, msg, to_core(msg))
    msgs = (msg, to_y(msg))
    d2, d2_low, dhid, sums_a, sq = run(ffn_back, lengths, hat2, inv2, teach, slope, sg2, sb2, wd)
    m, cproj, cmix, part, v_low = run(lambda *a: cross1(*a, q_q, q_o), lengths, vab, msgs, cw)
    part = group_send(run, part)
    grad_d = run(weight_grad, d2_low, act)
    sum_d = scatter_all(grad_d)
    chat1, cinv1, clow, cact, cslope, part = run(lambda *a: cross2(*a, q_u), vab, m, part, cw)
    part = group_send(run, part)
    grad_u = run(weight_grad, low, dhid)
    sum_u = scatter_all(grad_u)
    cls_out, csq, csums_a, cd2, cd2_low, cdhid, part = run(cross3, lengths, vab, m, chat1, cslope, part, cw)
    part = group_send(run, part)
    d1, sums_b = run(up_back, d2, dhid, hat1, inv1, sg1, wu)
    cd1, cd1_low, csums_b, cdproj, part = run(
        lambda *a: cross4(*a, q_o), lengths, vab, cd2, chat1, cinv1, cproj, part, cw
    )
    part = group_send(run, part)
    outs = run(emit_output, hat2, sg2, sb2, cls_out)
    c_own, c_far = run(pack_acts, (v_low, cd1_low, clow, cd2_low), (cdproj, cmix, cdhid, cact))
    c_far = to_x(c_far)
    pos_part, ssums_a, sd2, sd2_low, slow, sact, sdhid, part = run(cross5, vab, m, cd1, part, wu, wd)
    part = group_send(run, part)
    s_own, s_far = run(pack_acts, (sd2_low, slow), (sact, sdhid))
    s_far = to_x(s_far)
    acts = dp_gather(run(join_rows, c_own, c_far))
    d1c, ssums_b = run(cross6, vab, m, sd2, invc1, part)
    facts = run(join_rows, s_own, s_far)
    facts_c = to_core(facts)
    sums = run(small_sums, sums_b, sums_a, ssums_b, ssums_a, csums_b, csums_a, pos_part, sq, csq)
    dproj1, d1_low, dxp = run(lambda *a: attn_back(1, *a), lengths, proj, d1, d1c, pa)
    f_d, f_u = run(lambda a, b: factor_grads(a, b, (q_u, q_u)), facts, facts_c)
    keep1, send = run(lambda *a: attn_grad(1, *a), h, d1_low, dproj1, mix)
    got1 = to_core(send)
    acts = run(join_rows, *acts) if len(acts) > 1 else acts[0]
    q_f = pair_scatter(run, sum_d, f_d, sum_u, f_u, keep1)
    a_y, a_d = run(chip_half, keep1, got1)
    a_y, a_d = to_y(a_y), to_d(a_d)
    dproj0, dxs = run(lambda *a: attn_back(0, *a), lengths, proj, dxp, d1_low, pa)
    outs = to_rows(after(outs, dproj0))
    sums = run(add_rows, sums, to_core(sums))
    keep0, send = run(lambda *a: attn_grad(0, *a), h, after(d1_low, a_y, a_d), dproj0, mix)
    got0 = to_core(send)
    q_f = pair_total(run, q_f)
    a_0, a_x = run(chip_half, keep0, got0)
    q_f = q_f if lax.axis_size("dp") != 4 else to_depth(after(q_f, a_0))
    a_x = to_x(a_x)
    acts_c = to_core(after(acts, a_0))
    sums = run(add_rows, sums, to_y(sums))
    q_a = dp_scatter(run, sums, to_x(sums), a_0, a_y, a_x, a_d)
    output = run(token_join, outs)
    g_cqkv, g_cproj, g_cup, g_cdown = run(
        lambda a, b: factor_grads(a, b, (q_q, q_o, q_u, q_u)), acts, acts_c
    )
    g_down, g_up = pair_result(run, q_f)
    q_a, al = dp_quarters(run, q_a)
    dxs = to_rows(after(dxs, g_up, al))
    dx_out = run(token_join, dxs)
    g_qkv, g_proj = dp_place(run, q_a, n_q)
    valid = jnp.sum(lengths).astype(f32)
    loss = al[8, 0] / (2.0 * valid)
    return (
        output, loss, dx_out, al[9:25],
        g_qkv, g_proj, al[0], al[1], g_up, g_down, al[2], al[3],
        g_cqkv, g_cproj, al[4], al[5], g_cup, g_cdown, al[6], al[7],
    )


def solution(mesh):
    wide, cut, one = P("row", ("dp", "col")), P("row", "col"), P("row")
    block = (cut, cut, one, one, cut, cut, one, one)
    in_specs = (wide, wide, P(), P(None, "row")) + block + block
    out_specs = (wide, P(), wide, P(None, "row")) + block + block
    return jax.shard_map(body, mesh=mesh, in_specs=in_specs, out_specs=out_specs, check_vma=False)
```
